32 devices in a mesh: head: 4 (over z), blk: 8 (over y, x, core).
Axes of the slice: x: 2, y: 2, z: 4, core: 2. Of those that a mesh axis runs over, the one named last changes fastest.
Arguments:
- tokens: bfloat16 [8192, 1024], P(('blk', 'head')), may hold values from -6 to 6
- cotangent: bfloat16 [8192, 1024], P(('blk', 'head')), may hold values from -6 to 6
- segment: int32 [8192], replicated, may hold values from 0 to 3, never falling along the last dimension, each value on 1 to 6144 neighbouring positions
- norm_gain: bfloat16 [1024], P(('head', 'blk')), may hold values from 0.5 to 1.5
- norm_shift: bfloat16 [1024], P(('head', 'blk')), may hold values from -1.5 to 1.5
- in_weight: bfloat16 [1024, 3072], P(('head', 'blk')), may hold values from -0.1875 to 0.1875
- query_bias: bfloat16 [1024], P(('head', 'blk')), may hold values from -2.5 to 2.5
- value_bias: bfloat16 [1024], P(('head', 'blk')), may hold values from -1.5 to 1.5
- out_weight: bfloat16 [1024, 1024], P(('head', 'blk')), may hold values from -3 to 3
- out_bias: bfloat16 [1024], P(('head', 'blk')), may hold values from -1.5 to 1.5
- post_gain: bfloat16 [1024], P(('head', 'blk')), may hold values from 0.5 to 1.5
- post_shift: bfloat16 [1024], P(('head', 'blk')), may hold values from -1.5 to 1.5
- up_weight: bfloat16 [1024, 4096], P(('head', 'blk')), may hold values from -0.1875 to 0.1875
- up_bias: bfloat16 [4096], P(('head', 'blk')), may hold values from -1.5 to 1.5
- down_weight: bfloat16 [4096, 1024], P(('head', 'blk')), may hold values from -0.09375 to 0.09375
- down_bias: bfloat16 [1024], P(('head', 'blk')), may hold values from -1.5 to 1.5
Outputs:
- output: bfloat16 [8192, 1024], P(('blk', 'head'))
- tokens_grad: bfloat16 [8192, 1024], P(('blk', 'head'))
- norm_gain_grad: float32 [1024], P(('head', 'blk'))
- norm_shift_grad: float32 [1024], P(('head', 'blk'))
- in_weight_grad: float32 [1024, 3072], P(('head', 'blk'))
- query_bias_grad: float32 [1024], P(('head', 'blk'))
- value_bias_grad: float32 [1024], P(('head', 'blk'))
- out_weight_grad: float32 [1024, 1024], P(('head', 'blk'))
- out_bias_grad: float32 [1024], P(('head', 'blk'))
- post_gain_grad: float32 [1024], P(('head', 'blk'))
- post_shift_grad: float32 [1024], P(('head', 'blk'))
- up_weight_grad: float32 [1024, 4096], P(('head', 'blk'))
- up_bias_grad: float32 [4096], P(('head', 'blk'))
- down_weight_grad: float32 [4096, 1024], P(('head', 'blk'))
- down_bias_grad: float32 [1024], P(('head', 'blk'))
The draws below stay inside these ranges and needn't reach their ends.
Inputs may be any that keep to these rules, and one draw needn't show every extreme that they name: `segment`: document numbers never fall along the sequence; each document holds 1 to 6144 tokens and one holds exactly 6144.
All inputs are finite; a program needn't handle non-finite values.
Results may differ from the reference program's by a relative error of at most 0.019.
Values may be sent and summed in bfloat16 or wider, within the bound.
No kernel may reach another device: no remote copies, remote signals or barrier semaphores. Data moves between devices by JAX's collectives and lax.ppermute only.
A program may use at most 256 MiB of HBM per device.

```python
import math
import jax
import jax.numpy as jnp
import numpy as np
from jax import lax

D = 1024
HEADS = 16
HEAD_DIM = 64
FF = 4096
LEN = 8192
DOCS = 4
DOC_MOST = 6144


def levels(rng, extent, split, least, top_value):
    loudness, own = 1.0, jax.random.fold_in(rng, 6)
    for position, blocks in split:
        heights = jnp.exp(jax.random.uniform(jax.random.fold_in(own, position), (blocks,), jnp.float32, least / len(split), top_value / len(split)))
        loudness = loudness * jnp.repeat(heights, extent[position] // blocks).reshape([-1 if axis == position else 1 for axis in range(len(extent))])
    return loudness


def length_profile(count, total, reach, skew):
    portions = [(1 << 20) // math.isqrt(grade ** skew) + 1 for grade in range(2, count + 1)]
    surplus, given = total - reach - (count - 1), [1] * (count - 1)
    while surplus > 0:
        free = [i for i in range(count - 1) if given[i] < reach]
        pool, left = sum([portions[i] for i in free]), surplus
        for i in free:
            more = min(reach - given[i], max(1, left * portions[i] // pool), surplus)
            given[i] = given[i] + more
            surplus = surplus - more
    return np.array([reach] + given)


def ragged(key, count, total, reach, skew):
    if count == 2:
        one = jax.random.randint(key, (), max(1, total - reach), min(reach, total - 1) + 1)
        return jnp.stack([one, total - one])
    sizes = jnp.asarray(length_profile(count, total, reach, skew), jnp.int32)
    twos = (count - 1) // 2
    donor, receiver = sizes[1:1 + 2 * twos:2], sizes[2:2 + 2 * twos:2]
    margin = jnp.minimum(donor - 1, reach - receiver)
    moved = jax.random.randint(jax.random.fold_in(key, 1), (twos,), 0, 1 << 20) % (margin + 1)
    sizes = sizes.at[1:1 + 2 * twos:2].set(donor - moved).at[2:2 + 2 * twos:2].set(receiver + moved)
    return sizes[jax.random.permutation(jax.random.fold_in(key, 2), count)]


def gaussian(rng, extent, scale, limit, shards=(), held_as=jnp.bfloat16):
    values = jax.random.normal(rng, extent, jnp.float32) * scale
    if len(shards) > 0:
        values = levels(rng, extent, shards, -0.22, 0.18) * values
    return jnp.clip(values, min=-limit, max=limit).astype(held_as)


def setup_inputs(seed: int = 0) -> dict:
    arg_keys = jax.random.split(jax.random.key(seed), 17)
    tokens = gaussian(arg_keys[0], (LEN, D), 1.0, 6.0, ((0, 32),))
    cotangent = gaussian(arg_keys[1], (LEN, D), 1.0, 6.0, ((0, 32),))
    segment = jnp.searchsorted(jnp.cumsum(ragged(arg_keys[2], DOCS, LEN, DOC_MOST, 0)), jnp.arange(LEN), side="right").astype(jnp.int32)
    norm_gain = jnp.clip(1.0 + 0.1 * jax.random.normal(arg_keys[3], (D,), jnp.float32), 0.5, 1.5).astype(jnp.bfloat16)
    norm_shift = gaussian(arg_keys[4], (D,), 0.3, 1.5, ((0, 32),))
    in_weight = gaussian(arg_keys[5], (D, 3 * D), D ** -0.5, 0.1875, ((0, 32),))
    query_bias = gaussian(arg_keys[6], (D,), 0.5, 2.5, ((0, 32),))
    value_bias = gaussian(arg_keys[7], (D,), 0.3, 1.5, ((0, 32),))
    out_weight = gaussian(arg_keys[8], (D, D), (max(1, D // 256)) ** -0.5, 3.0, ((0, 32),))
    out_bias = gaussian(arg_keys[9], (D,), 0.3, 1.5, ((0, 32),))
    post_gain = jnp.clip(1.0 + 0.1 * jax.random.normal(arg_keys[10], (D,), jnp.float32), 0.5, 1.5).astype(jnp.bfloat16)
    post_shift = gaussian(arg_keys[11], (D,), 0.3, 1.5, ((0, 32),))
    up_weight = gaussian(arg_keys[12], (D, FF), D ** -0.5, 0.1875, ((0, 32),))
    up_bias = gaussian(arg_keys[13], (FF,), 0.3, 1.5, ((0, 32),))
    down_weight = gaussian(arg_keys[14], (FF, D), FF ** -0.5, 0.09375, ((0, 32),))
    down_bias = gaussian(arg_keys[15], (D,), 0.3, 1.5, ((0, 32),))
    return dict(tokens=tokens, cotangent=cotangent, segment=segment, norm_gain=norm_gain, norm_shift=norm_shift, in_weight=in_weight, query_bias=query_bias, value_bias=value_bias, out_weight=out_weight, out_bias=out_bias, post_gain=post_gain, post_shift=post_shift, up_weight=up_weight, up_bias=up_bias, down_weight=down_weight, down_bias=down_bias)


@jax.custom_vjp
def low(v):
    return lax.optimization_barrier(v.astype(jnp.bfloat16)).astype(jnp.float32)

@jax.custom_vjp
def low_back(v):
    return v

def low_keep(v):
    return (low(v), None)

def low_pass(kept, grad):
    return (grad,)

def back_keep(v):
    return (v, None)

def back_low(kept, grad):
    return (low(grad),)
low.defvjp(low_keep, low_pass)
low_back.defvjp(back_keep, back_low)
EPS = 1e-05
NEGATIVE = -1e+30
GELU_C = 0.7978845608028654

def matmul(left, right):
    return jnp.dot(left, right, precision=lax.Precision.HIGHEST, preferred_element_type=jnp.float32)

def layer_norm(rows, gain, shift):
    center = rows - lax.optimization_barrier(jnp.mean(rows, axis=-1, keepdims=True))
    var = lax.optimization_barrier(jnp.mean(center * center, axis=-1, keepdims=True))
    return center * lax.rsqrt(var + EPS) * gain + shift

def gelu(pre):
    return 0.5 * pre * (1.0 + jnp.tanh(GELU_C * (pre + 0.044715 * pre * pre * pre)))

def attention(queries, keys, values, segment):
    length = queries.shape[0]
    rows_block = 512 if length % 512 == 0 else length
    count = length // rows_block
    scale = HEAD_DIM ** (-0.5)
    q_heads = queries.reshape(length, HEADS, HEAD_DIM).transpose(1, 0, 2)
    k_heads = keys.reshape(length, HEADS, HEAD_DIM).transpose(1, 0, 2)
    v_heads = values.reshape(length, HEADS, HEAD_DIM).transpose(1, 0, 2)
    positions = jnp.arange(length, dtype=jnp.int32)

    def one_block(item):
        q_block, start = item
        q_pos = start + jnp.arange(rows_block, dtype=jnp.int32)
        seg_rows = lax.dynamic_slice_in_dim(segment, start, rows_block)
        scores = jnp.einsum('hqd,hkd->hqk', q_block, k_heads, precision=lax.Precision.HIGHEST) * scale
        scores = low_back(scores)
        allowed = (positions[None, :] <= q_pos[:, None]) & (segment[None, :] == seg_rows[:, None])
        scores = jnp.where(allowed[None], scores, NEGATIVE)
        top = lax.optimization_barrier(jnp.max(scores, axis=-1, keepdims=True))
        expo = jnp.exp(scores - top)
        probs = low(expo / lax.optimization_barrier(jnp.sum(expo, axis=-1, keepdims=True)))
        return jnp.einsum('hqk,hkd->hqd', probs, v_heads, precision=lax.Precision.HIGHEST)
    blocks = q_heads.reshape(HEADS, count, rows_block, HEAD_DIM).transpose(1, 0, 2, 3)
    starts = jnp.arange(count, dtype=jnp.int32) * rows_block
    mixed = lax.map(jax.checkpoint(one_block), (blocks, starts))
    return mixed.transpose(0, 2, 1, 3).reshape(length, HEADS * HEAD_DIM)

def forward(rows, norm_gain, norm_shift, in_weight, query_bias, value_bias, out_weight, out_bias, post_gain, post_shift, up_weight, up_bias, down_weight, down_bias, segment):
    normed = low(layer_norm(rows, norm_gain, norm_shift))
    proj = matmul(normed, in_weight)
    queries = low_back(low(proj[:, :D] + query_bias))
    keys = low_back(low(proj[:, D:2 * D]))
    values = low_back(low(proj[:, 2 * D:] + value_bias))
    attended = low_back(low(attention(queries, keys, values, segment)))
    branch = low_back(matmul(attended, out_weight) + out_bias)
    middle = rows + branch
    hidden_in = low(layer_norm(middle, post_gain, post_shift))
    pre = low_back(matmul(hidden_in, up_weight) + up_bias)
    act = low(gelu(pre))
    down = low_back(matmul(act, down_weight) + down_bias)
    return middle + down

def reference(tokens, cotangent, segment, norm_gain, norm_shift, in_weight, query_bias, value_bias, out_weight, out_bias, post_gain, post_shift, up_weight, up_bias, down_weight, down_bias):
    inputs = (tokens, norm_gain, norm_shift, in_weight, query_bias, value_bias, out_weight, out_bias, post_gain, post_shift, up_weight, up_bias, down_weight, down_bias)
    floats = tuple((item.astype(jnp.float32) for item in inputs))

    def wrapped(*params):
        return forward(*params, segment)
    result, pullback = jax.vjp(wrapped, *floats)
    grads = pullback(cotangent.astype(jnp.float32))
    return (result.astype(jnp.bfloat16), grads[0].astype(jnp.bfloat16), grads[1], grads[2], grads[3], grads[4], grads[5], grads[6], grads[7], grads[8], grads[9], grads[10], grads[11], grads[12], grads[13])
```

```python
import functools

import jax
import jax.numpy as jnp
from jax import lax
from jax.experimental import pallas as pl
from jax.experimental.pallas import tpu as pltpu
from jax.sharding import Mesh
from jax.sharding import PartitionSpec as P

HEADS = 16
HEAD_DIM = 64
DOCS = 4
BLOCK_Q = 512
BLOCK_K = 512
VMEM_BYTES = 56 * 1024 * 1024

EPS = 1e-05
NEGATIVE = -1e30
GELU_C = 0.7978845608028654
SCALE = HEAD_DIM ** (-0.5)
ALL = ("head", "u", "v", "rest")
f32 = jnp.float32
bf16 = jnp.bfloat16


def norm_forward(rows, gain, shift):
    center = rows - jnp.mean(rows, axis=-1, keepdims=True)
    var = jnp.mean(center * center, axis=-1, keepdims=True)
    inverse = lax.rsqrt(var + EPS)
    unit = center * inverse
    return (unit * gain + shift, unit, inverse)


def norm_inner(grad, unit, inverse, gain):
    scaled = grad * gain
    inner = (
        scaled
        - jnp.mean(scaled, axis=-1, keepdims=True)
        - unit * jnp.mean(scaled * unit, axis=-1, keepdims=True)
    )
    return inverse * inner


def gelu_parts(pre):
    cubic = pre * pre * pre
    tangent = jnp.tanh(GELU_C * (pre + 0.044715 * cubic))
    value = 0.5 * pre * (1.0 + tangent)
    slope = 0.5 * (1.0 + tangent) + 0.5 * pre * (1.0 - tangent * tangent) * GELU_C * (
        1.0 + 3.0 * 0.044715 * pre * pre
    )
    return (value, slope)


def shifted(x, axis, k):
    n = lax.axis_size(axis)
    return lax.ppermute(x, axis, [(i, (i + k) % n) for i in range(n)])


def put(buffer, x, index):
    return lax.dynamic_update_index_in_dim(buffer, x, index, 0)


def gather_axis(x, axis):
    n = lax.axis_size(axis)
    if n == 1:
        return x[None]
    me = lax.axis_index(axis)
    out = put(jnp.zeros((n,) + x.shape, x.dtype), x, me)
    for k in range(1, n):
        out = put(out, shifted(x, axis, k), (me - k) % n)
    return out


def gather_line(x, axis):
    n = lax.axis_size(axis)
    if n != 4:
        return gather_axis(x, axis)
    me = lax.axis_index(axis)
    up = [(i, i + 1) for i in range(n - 1)]
    down = [(i + 1, i) for i in range(n - 1)]
    left, right = [x], [x]
    for _ in range(n - 1):
        left.append(lax.ppermute(left[-1], axis, up))
        right.append(lax.ppermute(right[-1], axis, down))
    low = me < 2
    first = jnp.where(low, right[1], left[1])
    second = jnp.where(low, right[2], left[2])
    inner = jnp.where(me == 1, left[1], right[1])
    third = jnp.where(me == 0, right[3], jnp.where(me == 3, left[3], inner))
    out = put(jnp.zeros((n,) + x.shape, x.dtype), x, me)
    out = put(out, first, jnp.where(low, me + 1, me - 1))
    out = put(out, second, jnp.where(low, me + 2, me - 2))
    return put(out, third, jnp.where(me == 0, 3, jnp.where(me == 3, 0, jnp.where(me == 1, 0, 3))))


def reduce_axis(x, axis):
    n = lax.axis_size(axis)
    if n == 1:
        return x[0].astype(f32)
    me = lax.axis_index(axis)
    total = lax.dynamic_index_in_dim(x, me, 0, keepdims=False).astype(f32)
    for k in range(1, n):
        piece = lax.dynamic_index_in_dim(x, (me + k) % n, 0, keepdims=False)
        total = total + shifted(piece, axis, k).astype(f32)
    return total


def exchange_axis(x, axis):
    n = lax.axis_size(axis)
    if n == 1:
        return x
    me = lax.axis_index(axis)
    mine = lax.dynamic_index_in_dim(x, me, 0, keepdims=False)
    out = put(jnp.zeros_like(x), mine, me)
    for k in range(1, n):
        piece = lax.dynamic_index_in_dim(x, (me + k) % n, 0, keepdims=False)
        out = put(out, shifted(piece, axis, k), (me - k) % n)
    return out


def allowed_keys(kb, starts, pos):
    t = kb * BLOCK_K + lax.broadcasted_iota(jnp.int32, (BLOCK_K, BLOCK_Q), 0)
    return (t >= starts) & (t <= pos)


def lay_rows(kv_ref, rows_ref):
    def lay(i, _):
        rows_ref[pl.ds(pl.multiple_of(i * BLOCK_K, BLOCK_K), BLOCK_K), :] = kv_ref[i].T
        return 0

    lax.fori_loop(0, kv_ref.shape[0], lay, 0)


def forward_kernel(lo_ref, mid_ref, q0_ref, q_ref, kv_ref, start_ref, o_ref, wide_ref, lse_ref, rows_ref):
    step = pl.program_id(0)

    @pl.when(step == 0)
    def _():
        lay_rows(kv_ref, rows_ref)

    first = q0_ref[step]
    q = q_ref[0] * jnp.asarray(SCALE, bf16)
    q_pad = jnp.concatenate([q, jnp.zeros_like(q)], axis=0)
    starts = start_ref[0]
    pos = first + lax.broadcasted_iota(jnp.int32, (1, BLOCK_Q), 1)

    def body(masked, kb, carry):
        top, total, acc = carry
        rows = rows_ref[pl.ds(pl.multiple_of(kb * BLOCK_K, BLOCK_K), BLOCK_K), :]
        s = jnp.dot(rows, q_pad, preferred_element_type=f32)
        if masked:
            s = jnp.where(allowed_keys(kb, starts, pos), s, NEGATIVE)
        new_top = jnp.maximum(top, jnp.max(s, axis=0, keepdims=True))
        p = jnp.exp(s - new_top)
        factor = jnp.exp(top - new_top)
        values = kv_ref[kb, HEAD_DIM:, :]
        acc = acc * factor + jnp.dot(values, p.astype(bf16), preferred_element_type=f32)
        return (new_top, total * factor + jnp.sum(p, axis=0, keepdims=True), acc)

    diagonal = first // BLOCK_K
    mid = jnp.minimum(mid_ref[step], diagonal)
    carry = (
        jnp.full((1, BLOCK_Q), NEGATIVE, f32),
        jnp.zeros((1, BLOCK_Q), f32),
        jnp.zeros((HEAD_DIM, BLOCK_Q), f32),
    )
    carry = lax.fori_loop(lo_ref[step], mid, functools.partial(body, True), carry)
    carry = lax.fori_loop(mid, diagonal, functools.partial(body, False), carry)
    last = (first + BLOCK_Q + BLOCK_K - 1) // BLOCK_K
    top, total, acc = lax.fori_loop(diagonal, last, functools.partial(body, True), carry)
    out = acc / total
    wide_ref[0] = out
    lse_ref[0] = top + jnp.log(total)
    low = out.astype(bf16)
    piece = o_ref.shape[3]
    for i in range(o_ref.shape[0]):
        o_ref[i, 0] = low[:, i * piece : (i + 1) * piece]


def backward_kernel(
    n_steps, lo_ref, mid_ref, q0_ref, q_ref, kv_ref, start_ref, do_ref, wide_ref, lse_ref, dq_ref, dkv_ref, rows_ref, acc_ref
):
    step = pl.program_id(0)

    @pl.when(step == 0)
    def _():
        lay_rows(kv_ref, rows_ref)
        acc_ref[...] = jnp.zeros_like(acc_ref)

    @pl.when(step < n_steps)
    def _():
        first = q0_ref[step]
        q = q_ref[0] * jnp.asarray(SCALE, bf16)
        do = jnp.concatenate([do_ref[i, 0] for i in range(do_ref.shape[0])], axis=1)
        zero = jnp.zeros_like(q)
        q_pad = jnp.concatenate([q, zero], axis=0)
        do_pad = jnp.concatenate([zero, do], axis=0)
        q_rows = q_pad.T
        do_rows = do_pad.T
        starts = start_ref[0]
        lse = lse_ref[0]
        delta = jnp.sum(do.astype(f32) * wide_ref[0], axis=0, keepdims=True)
        pos = first + lax.broadcasted_iota(jnp.int32, (1, BLOCK_Q), 1)

        def body(masked, kb, dq):
            at = pl.ds(pl.multiple_of(kb * BLOCK_K, BLOCK_K), BLOCK_K)
            rows = rows_ref[at, :]
            s = jnp.dot(rows, q_pad, preferred_element_type=f32)
            p = jnp.exp(s - lse)
            if masked:
                p = jnp.where(allowed_keys(kb, starts, pos), p, 0.0)
            dp = jnp.dot(rows, do_pad, preferred_element_type=f32)
            ds = (p * (dp - delta)).astype(bf16)
            acc_ref[at, :] += jnp.dot(p.astype(bf16), do_rows, preferred_element_type=f32) + jnp.dot(
                ds, q_rows, preferred_element_type=f32
            )
            return dq + jnp.dot(kv_ref[kb, :HEAD_DIM, :], ds, preferred_element_type=f32)

        diagonal = first // BLOCK_K
        mid = jnp.minimum(mid_ref[step], diagonal)
        dq = jnp.zeros((HEAD_DIM, BLOCK_Q), f32)
        dq = lax.fori_loop(lo_ref[step], mid, functools.partial(body, True), dq)
        dq = lax.fori_loop(mid, diagonal, functools.partial(body, False), dq)
        last = (first + BLOCK_Q + BLOCK_K - 1) // BLOCK_K
        dq = lax.fori_loop(diagonal, last, functools.partial(body, True), dq)
        dq_ref[0] = (dq * SCALE).astype(bf16)

    @pl.when(step >= n_steps)
    def _():
        kb = jnp.maximum(step - n_steps, 0)
        at = pl.ds(pl.multiple_of(kb * BLOCK_K, BLOCK_K), BLOCK_K)
        dkv_ref[0] = acc_ref[at, :].astype(bf16).T


def attention_specs(block_rows, tok_rows, keys):
    subs = block_rows // BLOCK_Q
    pieces = BLOCK_Q // tok_rows
    n_kb = keys // BLOCK_K

    def wrap(index):
        return lambda i, *_: index(i)

    q_spec = lambda cap: pl.BlockSpec((1, HEAD_DIM, BLOCK_Q), wrap(lambda i: (cap(i) // subs, 0, cap(i) % subs)))
    row_spec = lambda cap: pl.BlockSpec((1, 1, BLOCK_Q), wrap(lambda i: (cap(i) // subs, 0, cap(i) % subs)))
    piece_spec = lambda cap: pl.BlockSpec(
        (pieces, 1, HEAD_DIM, tok_rows), wrap(lambda i: (cap(i) % subs, cap(i) // subs, 0, 0))
    )
    kv_spec = pl.BlockSpec(
        (n_kb, 2 * HEAD_DIM, BLOCK_K), wrap(lambda i: (0, 0, 0)), pipeline_mode=pl.Buffered(1)
    )
    return q_spec, row_spec, piece_spec, kv_spec


def attention_forward(bounds, qkv, kv, starts, n_head, tok_rows):
    hb, _, block_rows = qkv.shape
    keys = kv.shape[0] * BLOCK_K
    n_steps = hb * block_rows // BLOCK_Q
    q_spec, row_spec, piece_spec, kv_spec = attention_specs(block_rows, tok_rows, keys)
    same = lambda i: i
    return pl.pallas_call(
        forward_kernel,
        grid_spec=pltpu.PrefetchScalarGridSpec(
            num_scalar_prefetch=3,
            grid=(n_steps,),
            in_specs=[q_spec(same), kv_spec, row_spec(same)],
            out_specs=[piece_spec(same), q_spec(same), row_spec(same)],
            scratch_shapes=[pltpu.VMEM((keys, 2 * HEAD_DIM), bf16)],
        ),
        out_shape=[
            jax.ShapeDtypeStruct((n_head, hb, HEAD_DIM, tok_rows), bf16),
            jax.ShapeDtypeStruct((hb, HEAD_DIM, block_rows), f32),
            jax.ShapeDtypeStruct((hb, 1, block_rows), f32),
        ],
        compiler_params=pltpu.CompilerParams(vmem_limit_bytes=VMEM_BYTES),
        name="attention_forward",
    )(*bounds, qkv, kv, starts)


def attention_backward(bounds, qkv, kv, starts, do, wide, lse):
    hb, _, block_rows = qkv.shape
    n_kb = kv.shape[0]
    keys = n_kb * BLOCK_K
    n_steps = hb * block_rows // BLOCK_Q
    q_spec, row_spec, piece_spec, kv_spec = attention_specs(block_rows, do.shape[3], keys)
    cap = lambda i: jnp.minimum(i, n_steps - 1)
    return pl.pallas_call(
        functools.partial(backward_kernel, n_steps),
        grid_spec=pltpu.PrefetchScalarGridSpec(
            num_scalar_prefetch=3,
            grid=(n_steps + n_kb,),
            in_specs=[q_spec(cap), kv_spec, row_spec(cap), piece_spec(cap), q_spec(cap), row_spec(cap)],
            out_specs=[
                q_spec(cap),
                pl.BlockSpec((1, 2 * HEAD_DIM, BLOCK_K), lambda i, *_: (jnp.maximum(i - n_steps, 0), 0, 0)),
            ],
            scratch_shapes=[pltpu.VMEM((keys, 2 * HEAD_DIM), bf16), pltpu.VMEM((keys, 2 * HEAD_DIM), f32)],
        ),
        out_shape=[
            jax.ShapeDtypeStruct((hb, HEAD_DIM, block_rows), bf16),
            jax.ShapeDtypeStruct((n_kb, 2 * HEAD_DIM, BLOCK_K), bf16),
        ],
        compiler_params=pltpu.CompilerParams(vmem_limit_bytes=VMEM_BYTES),
        name="attention_backward",
    )(*bounds, qkv, kv, starts, do, wide, lse)


def on_device(
    tokens,
    cotangent,
    segment,
    norm_gain,
    norm_shift,
    in_weight,
    query_bias,
    value_bias,
    out_weight,
    out_bias,
    post_gain,
    post_shift,
    up_weight,
    up_bias,
    down_weight,
    down_bias,
):
    n_head, n_u, n_v, n_rest = (lax.axis_size(a) for a in ALL)
    hb = n_u * n_v
    n_blk = hb * n_rest
    n_all = n_head * n_blk
    me_head, me_u, me_v, me_rest = (lax.axis_index(a) for a in ALL)
    me_blk = (me_u * n_v + me_v) * n_rest + me_rest
    tok_rows, width = tokens.shape
    block_rows = tok_rows * n_head
    length = segment.shape[0]
    w_rows = in_weight.shape[0]
    group = 3 * hb * HEAD_DIM

    w_up = lax.all_gather(up_weight, ALL, axis=0, tiled=True)
    w_down = lax.all_gather(down_weight, ALL, axis=0, tiled=True)
    w_out = lax.all_gather(out_weight, ALL, axis=0, tiled=True)

    parts = [norm_gain, norm_shift, query_bias, value_bias, out_bias, post_gain, post_shift, down_bias, up_bias]
    packed = jnp.concatenate(parts).reshape(1, -1)
    for axis in ("rest", "v", "u", "head"):
        packed = gather_axis(packed, axis)
    packed = packed.reshape(n_all, -1)
    vectors, at = [], 0
    for part in parts:
        size = part.shape[0]
        vectors.append(packed[:, at : at + size].reshape(-1).astype(f32))
        at += size
    gain_a, shift_a, bias_q, bias_v, bias_out, gain_b, shift_b, bias_down, bias_up = vectors

    cols = in_weight.reshape(w_rows, 3, n_head, hb, HEAD_DIM).transpose(2, 0, 3, 1, 4).reshape(n_head, w_rows, group)
    w_in = exchange_axis(cols, "head")
    for axis in ("v", "u", "rest"):
        w_in = gather_axis(w_in, axis)
    w_in = w_in.transpose(3, 1, 2, 0, 4, 5).reshape(width, group)

    rows_all = gather_line(tokens, "head").reshape(block_rows, width).astype(f32)
    normed, unit_all, inverse_all = norm_forward(rows_all, gain_a, shift_a)
    normed_low = normed.astype(bf16)
    group_bias = jnp.stack([bias_q, jnp.zeros_like(bias_q), bias_v]).reshape(3, n_head, hb, HEAD_DIM)
    group_bias = lax.dynamic_index_in_dim(group_bias, me_head, 1, keepdims=False).transpose(1, 0, 2).reshape(group, 1)
    projected = lax.dot_general(w_in, normed_low, (((0,), (1,)), ((), ())), preferred_element_type=f32)
    projected = (projected + group_bias).astype(bf16)
    qkv = lax.all_to_all(
        projected.reshape(hb, 3 * HEAD_DIM, block_rows), ("u", "v"), split_axis=0, concat_axis=0, tiled=True
    )
    subs_k = block_rows // BLOCK_K
    kv = gather_axis(qkv[:, HEAD_DIM:], "rest")
    kv = kv.reshape(n_rest, hb, 2 * HEAD_DIM, subs_k, BLOCK_K).transpose(1, 0, 3, 2, 4)
    kv = kv.reshape(n_blk * subs_k, 2 * HEAD_DIM, BLOCK_K)

    doc_start = jnp.zeros_like(segment)
    for doc in range(1, DOCS):
        first = jnp.sum((segment < doc).astype(jnp.int32))
        doc_start = jnp.where(segment == doc, first, doc_start)
    starts = lax.dynamic_index_in_dim(doc_start.reshape(hb, n_rest, block_rows), me_rest, 1, keepdims=False)
    starts_q = starts.reshape(-1, BLOCK_Q)
    lo = starts_q[:, 0] // BLOCK_K
    mid = (starts_q[:, -1] + BLOCK_K - 1) // BLOCK_K
    q_first = (jnp.arange(hb, dtype=jnp.int32)[:, None] * n_rest + me_rest) * block_rows
    q_first = (q_first + jnp.arange(block_rows // BLOCK_Q, dtype=jnp.int32)[None] * BLOCK_Q).reshape(-1)
    bounds = (lo, mid, q_first)
    starts = starts.reshape(hb, 1, block_rows)

    attended, wide, lse = attention_forward(bounds, qkv, kv, starts, n_head, tok_rows)
    back = lax.all_to_all(
        attended.reshape(HEADS, HEAD_DIM, tok_rows), ("head", "u", "v"), split_axis=0, concat_axis=0, tiled=True
    ).reshape(width, tok_rows)

    rows = tokens.astype(f32)
    branch = lax.dot_general(back, w_out, (((0,), (0,)), ((), ())), preferred_element_type=f32) + bias_out
    middle = rows + branch
    hidden_in, unit_mid, inverse_mid = norm_forward(middle, gain_b, shift_b)
    hidden_low = hidden_in.astype(bf16)
    pre = jnp.dot(hidden_low, w_up, preferred_element_type=f32) + bias_up
    act, slope = gelu_parts(pre)
    act_low = act.astype(bf16)
    result = middle + jnp.dot(act_low, w_down, preferred_element_type=f32) + bias_down
    output = result.astype(bf16)
    grad_out = cotangent.astype(f32)
    grad_act = jnp.einsum("td,fd->tf", cotangent, w_down, preferred_element_type=f32)
    grad_pre = (grad_act * slope).astype(bf16)
    grad_hidden = jnp.einsum("tf,df->td", grad_pre, w_up, preferred_element_type=f32)
    grad_middle = grad_out + norm_inner(grad_hidden, unit_mid, inverse_mid, gain_b)
    grad_branch = grad_middle.astype(bf16)
    grad_back = lax.dot_general(w_out, grad_branch, (((1,), (1,)), ((), ())), preferred_element_type=f32).astype(bf16)
    grad_heads = lax.all_to_all(
        grad_back.reshape(HEADS, HEAD_DIM, tok_rows), ("head", "u", "v"), split_axis=0, concat_axis=0, tiled=True
    ).reshape(n_head, hb, HEAD_DIM, tok_rows)

    down_grad = jnp.einsum("tf,td->fd", act_low, cotangent, preferred_element_type=f32).astype(bf16)
    up_grad = jnp.einsum("td,tf->df", hidden_low, grad_pre, preferred_element_type=f32).astype(bf16)
    out_grad = jnp.einsum("dt,te->de", back, grad_branch, preferred_element_type=f32).astype(bf16)
    down_weight_grad = lax.psum_scatter(down_grad, ALL, scatter_dimension=0, tiled=True).astype(f32)
    up_weight_grad = lax.psum_scatter(up_grad, ALL, scatter_dimension=0, tiled=True).astype(f32)
    out_weight_grad = lax.psum_scatter(out_grad, ALL, scatter_dimension=0, tiled=True).astype(f32)
    sums = [
        jnp.sum(grad_branch.astype(f32), axis=0),
        jnp.sum(grad_hidden * unit_mid, axis=0),
        jnp.sum(grad_hidden, axis=0),
        jnp.sum(grad_out, axis=0),
        jnp.sum(grad_pre.astype(f32), axis=0),
    ]
    small = jnp.concatenate([s.reshape(n_all, -1) for s in sums], axis=1)
    small = small.reshape(n_head, n_u, n_v, n_rest, 1, -1)
    small = reduce_axis(small, "head")
    for axis in ("u", "v", "rest"):
        small = reduce_axis(small, axis)
    small = small.reshape(-1)
    size = width // n_all
    out_bias_grad, post_gain_grad, post_shift_grad, down_bias_grad = (
        small[i * size : (i + 1) * size] for i in range(4)
    )
    up_bias_grad = small[4 * size :]

    dq, dkv = attention_backward(bounds, qkv, kv, starts, grad_heads, wide, lse)
    dkv = dkv.reshape(hb, n_rest, subs_k, 2 * HEAD_DIM, BLOCK_K).transpose(1, 0, 3, 2, 4)
    dkv = reduce_axis(dkv.reshape(n_rest, hb, 2 * HEAD_DIM, block_rows), "rest").astype(bf16)
    grad_proj = lax.all_to_all(
        jnp.concatenate([dq, dkv], axis=1), ("u", "v"), split_axis=0, concat_axis=0, tiled=True
    ).reshape(group, block_rows)

    grad_normed = lax.dot_general(grad_proj, w_in, (((0,), (1,)), ((), ())), preferred_element_type=f32)
    grad_tokens = reduce_axis(grad_normed.astype(bf16).reshape(n_head, tok_rows, width), "head")
    unit_in = lax.dynamic_index_in_dim(unit_all.reshape(n_head, tok_rows, width), me_head, 0, keepdims=False)
    inverse_in = lax.dynamic_index_in_dim(inverse_all.reshape(n_head, tok_rows, 1), me_head, 0, keepdims=False)
    tokens_grad = (grad_middle + norm_inner(grad_tokens, unit_in, inverse_in, gain_a)).astype(bf16)

    in_grad = lax.dot_general(normed_low, grad_proj, (((0,), (1,)), ((), ())), preferred_element_type=f32)
    gain_grad = jnp.sum(grad_normed * unit_all, axis=0).reshape(n_head, n_blk, w_rows)
    shift_grad = jnp.sum(grad_normed, axis=0).reshape(n_head, n_blk, w_rows)
    col_sum = jnp.sum(grad_proj.astype(f32), axis=1).reshape(hb, 3, HEAD_DIM)
    mine = (jnp.arange(n_head) == me_head)[:, None, None]
    query_sum = jnp.where(mine, col_sum[:, 0].reshape(1, n_blk, w_rows), 0.0)
    value_sum = jnp.where(mine, col_sum[:, 2].reshape(1, n_blk, w_rows), 0.0)
    extra = jnp.stack([gain_grad, shift_grad, query_sum, value_sum], axis=-1)
    extra = jnp.pad(extra, ((0, 0), (0, 0), (0, 0), (0, 124)))
    joined = jnp.concatenate([in_grad.reshape(n_head, n_blk, w_rows, group), extra], axis=-1).astype(bf16)
    joined = joined.transpose(1, 0, 2, 3).reshape(hb, n_rest, n_head, w_rows, group + 128).transpose(1, 0, 2, 3, 4)
    joined = reduce_axis(joined, "rest").astype(bf16).reshape(n_u, n_v, n_head, w_rows, group + 128)
    joined = reduce_axis(joined, "u").astype(bf16)
    joined = reduce_axis(joined, "v").astype(bf16)
    joined = exchange_axis(joined, "head").astype(f32)
    in_weight_grad = joined[:, :, :group].reshape(n_head, w_rows, hb, 3, HEAD_DIM).transpose(1, 3, 0, 2, 4)
    in_weight_grad = in_weight_grad.reshape(w_rows, 3 * width)
    extra = jnp.sum(joined[:, :, group : group + 4], axis=0)
    return (
        output,
        tokens_grad,
        extra[:, 0],
        extra[:, 1],
        in_weight_grad,
        extra[:, 2],
        extra[:, 3],
        out_weight_grad,
        out_bias_grad,
        post_gain_grad,
        post_shift_grad,
        up_weight_grad,
        up_bias_grad,
        down_weight_grad,
        down_bias_grad,
    )


def solution(mesh):
    n_head, n_blk = mesh.shape["head"], mesh.shape["blk"]
    hb = HEADS // n_head
    n_u = 2 if hb % 2 == 0 else 1
    fine = Mesh(mesh.devices.reshape(n_head, n_u, hb // n_u, n_blk // hb), ALL)
    tok = P(("u", "v", "rest", "head"), None)
    vec = P(ALL)
    mat = P(ALL, None)
    return jax.shard_map(
        on_device,
        mesh=fine,
        in_specs=(tok, tok, P(), vec, vec, mat, vec, vec, mat, vec, vec, vec, mat, vec, mat, vec),
        out_specs=(tok, tok, vec, vec, mat, vec, vec, mat, vec, vec, vec, mat, vec, mat, vec),
        check_vma=False,
    )
```

```python
import functools

import jax
import jax.numpy as jnp
from jax import lax
from jax.experimental import pallas as pl
from jax.experimental.pallas import tpu as pltpu
from jax.sharding import Mesh
from jax.sharding import PartitionSpec as P

HEADS = 16
HEAD_DIM = 64
DOCS = 4
BLOCK_Q = 512
BLOCK_K = 512
VMEM_BYTES = 56 * 1024 * 1024

EPS = 1e-05
NEGATIVE = -1e30
GELU_C = 0.7978845608028654
SCALE = HEAD_DIM ** (-0.5)
ALL = ("head", "u", "v", "rest")
f32 = jnp.float32
bf16 = jnp.bfloat16


def norm_forward(rows, gain, shift):
    center = rows - jnp.mean(rows, axis=-1, keepdims=True)
    var = jnp.mean(center * center, axis=-1, keepdims=True)
    inverse = lax.rsqrt(var + EPS)
    unit = center * inverse
    return (unit * gain + shift, unit, inverse)


def norm_inner(grad, unit, inverse, gain):
    scaled = grad * gain
    inner = (
        scaled
        - jnp.mean(scaled, axis=-1, keepdims=True)
        - unit * jnp.mean(scaled * unit, axis=-1, keepdims=True)
    )
    return inverse * inner


def gelu_parts(pre):
    cubic = pre * pre * pre
    tangent = jnp.tanh(GELU_C * (pre + 0.044715 * cubic))
    value = 0.5 * pre * (1.0 + tangent)
    slope = 0.5 * (1.0 + tangent) + 0.5 * pre * (1.0 - tangent * tangent) * GELU_C * (
        1.0 + 3.0 * 0.044715 * pre * pre
    )
    return (value, slope)


def shifted(x, axis, k):
    n = lax.axis_size(axis)
    return lax.ppermute(x, axis, [(i, (i + k) % n) for i in range(n)])


def put(buffer, x, index):
    return lax.dynamic_update_index_in_dim(buffer, x, index, 0)


def gather_axis(x, axis):
    n = lax.axis_size(axis)
    if n == 1:
        return x[None]
    me = lax.axis_index(axis)
    out = put(jnp.zeros((n,) + x.shape, x.dtype), x, me)
    for k in range(1, n):
        out = put(out, shifted(x, axis, k), (me - k) % n)
    return out


def gather_line(x, axis, beside):
    n = lax.axis_size(axis)
    if n != 4:
        for make in beside:
            if make is not None:
                make()
        return gather_axis(x, axis)
    me = lax.axis_index(axis)
    up = [(i, i + 1) for i in range(n - 1)]
    down = [(i + 1, i) for i in range(n - 1)]
    left, right = [x], [x]
    for i in range(n - 1):
        left.append(lax.ppermute(left[-1], axis, up))
        right.append(lax.ppermute(right[-1], axis, down))
        if beside[i] is not None:
            made = beside[i]()
            left[-1], right[-1], _ = lax.optimization_barrier((left[-1], right[-1], made))
    low = me < 2
    first = jnp.where(low, right[1], left[1])
    second = jnp.where(low, right[2], left[2])
    inner = jnp.where(me == 1, left[1], right[1])
    third = jnp.where(me == 0, right[3], jnp.where(me == 3, left[3], inner))
    out = put(jnp.zeros((n,) + x.shape, x.dtype), x, me)
    out = put(out, first, jnp.where(low, me + 1, me - 1))
    out = put(out, second, jnp.where(low, me + 2, me - 2))
    return put(out, third, jnp.where(me == 0, 3, jnp.where(me == 3, 0, jnp.where(me == 1, 0, 3))))


def reduce_axis(x, axis):
    n = lax.axis_size(axis)
    if n == 1:
        return x[0].astype(f32)
    me = lax.axis_index(axis)
    total = lax.dynamic_index_in_dim(x, me, 0, keepdims=False).astype(f32)
    for k in range(1, n):
        piece = lax.dynamic_index_in_dim(x, (me + k) % n, 0, keepdims=False)
        total = total + shifted(piece, axis, k).astype(f32)
    return total


def exchange_axis(x, axis):
    n = lax.axis_size(axis)
    if n == 1:
        return x
    me = lax.axis_index(axis)
    mine = lax.dynamic_index_in_dim(x, me, 0, keepdims=False)
    out = put(jnp.zeros_like(x), mine, me)
    for k in range(1, n):
        piece = lax.dynamic_index_in_dim(x, (me + k) % n, 0, keepdims=False)
        out = put(out, shifted(piece, axis, k), (me - k) % n)
    return out


def allowed_keys(kb, starts, pos):
    t = kb * BLOCK_K + lax.broadcasted_iota(jnp.int32, (BLOCK_K, BLOCK_Q), 0)
    return (t >= starts) & (t <= pos)


def lay_rows(kv_ref, rows_ref):
    def lay(i, _):
        rows_ref[pl.ds(pl.multiple_of(i * BLOCK_K, BLOCK_K), BLOCK_K), :] = kv_ref[i].T
        return 0

    lax.fori_loop(0, kv_ref.shape[0], lay, 0)


def forward_kernel(lo_ref, mid_ref, q0_ref, q_ref, kv_ref, start_ref, o_ref, wide_ref, lse_ref, rows_ref):
    step = pl.program_id(0)

    @pl.when(step == 0)
    def _():
        lay_rows(kv_ref, rows_ref)

    first = q0_ref[step]
    q = q_ref[0] * jnp.asarray(SCALE, bf16)
    q_pad = jnp.concatenate([q, jnp.zeros_like(q)], axis=0)
    starts = start_ref[0]
    pos = first + lax.broadcasted_iota(jnp.int32, (1, BLOCK_Q), 1)

    def body(masked, kb, carry):
        top, total, acc = carry
        rows = rows_ref[pl.ds(pl.multiple_of(kb * BLOCK_K, BLOCK_K), BLOCK_K), :]
        s = jnp.dot(rows, q_pad, preferred_element_type=f32)
        if masked:
            s = jnp.where(allowed_keys(kb, starts, pos), s, NEGATIVE)
        new_top = jnp.maximum(top, jnp.max(s, axis=0, keepdims=True))
        p = jnp.exp(s - new_top)
        factor = jnp.exp(top - new_top)
        values = kv_ref[kb, HEAD_DIM:, :]
        acc = acc * factor + jnp.dot(values, p.astype(bf16), preferred_element_type=f32)
        return (new_top, total * factor + jnp.sum(p, axis=0, keepdims=True), acc)

    diagonal = first // BLOCK_K
    mid = jnp.minimum(mid_ref[step], diagonal)
    carry = (
        jnp.full((1, BLOCK_Q), NEGATIVE, f32),
        jnp.zeros((1, BLOCK_Q), f32),
        jnp.zeros((HEAD_DIM, BLOCK_Q), f32),
    )
    carry = lax.fori_loop(lo_ref[step], mid, functools.partial(body, True), carry)
    carry = lax.fori_loop(mid, diagonal, functools.partial(body, False), carry)
    last = (first + BLOCK_Q + BLOCK_K - 1) // BLOCK_K
    top, total, acc = lax.fori_loop(diagonal, last, functools.partial(body, True), carry)
    out = acc / total
    wide_ref[0] = out
    lse_ref[0] = top + jnp.log(total)
    low = out.astype(bf16)
    piece = o_ref.shape[3]
    for i in range(o_ref.shape[0]):
        o_ref[i, 0] = low[:, i * piece : (i + 1) * piece]


def backward_kernel(
    n_steps, lo_ref, mid_ref, q0_ref, q_ref, kv_ref, start_ref, do_ref, wide_ref, lse_ref, dq_ref, dkv_ref, rows_ref, acc_ref
):
    step = pl.program_id(0)

    @pl.when(step == 0)
    def _():
        lay_rows(kv_ref, rows_ref)
        acc_ref[...] = jnp.zeros_like(acc_ref)

    @pl.when(step < n_steps)
    def _():
        first = q0_ref[step]
        q = q_ref[0] * jnp.asarray(SCALE, bf16)
        do = jnp.concatenate([do_ref[i, 0] for i in range(do_ref.shape[0])], axis=1)
        zero = jnp.zeros_like(q)
        q_pad = jnp.concatenate([q, zero], axis=0)
        do_pad = jnp.concatenate([zero, do], axis=0)
        q_rows = q_pad.T
        do_rows = do_pad.T
        starts = start_ref[0]
        lse = lse_ref[0]
        delta = jnp.sum(do.astype(f32) * wide_ref[0], axis=0, keepdims=True)
        pos = first + lax.broadcasted_iota(jnp.int32, (1, BLOCK_Q), 1)

        def body(masked, kb, dq):
            at = pl.ds(pl.multiple_of(kb * BLOCK_K, BLOCK_K), BLOCK_K)
            rows = rows_ref[at, :]
            s = jnp.dot(rows, q_pad, preferred_element_type=f32)
            p = jnp.exp(s - lse)
            if masked:
                p = jnp.where(allowed_keys(kb, starts, pos), p, 0.0)
            dp = jnp.dot(rows, do_pad, preferred_element_type=f32)
            ds = (p * (dp - delta)).astype(bf16)
            acc_ref[at, :] += jnp.dot(p.astype(bf16), do_rows, preferred_element_type=f32) + jnp.dot(
                ds, q_rows, preferred_element_type=f32
            )
            return dq + jnp.dot(kv_ref[kb, :HEAD_DIM, :], ds, preferred_element_type=f32)

        diagonal = first // BLOCK_K
        mid = jnp.minimum(mid_ref[step], diagonal)
        dq = jnp.zeros((HEAD_DIM, BLOCK_Q), f32)
        dq = lax.fori_loop(lo_ref[step], mid, functools.partial(body, True), dq)
        dq = lax.fori_loop(mid, diagonal, functools.partial(body, False), dq)
        last = (first + BLOCK_Q + BLOCK_K - 1) // BLOCK_K
        dq = lax.fori_loop(diagonal, last, functools.partial(body, True), dq)
        dq_ref[0] = (dq * SCALE).astype(bf16)

    @pl.when(step >= n_steps)
    def _():
        kb = jnp.maximum(step - n_steps, 0)
        at = pl.ds(pl.multiple_of(kb * BLOCK_K, BLOCK_K), BLOCK_K)
        dkv_ref[0] = acc_ref[at, :].astype(bf16).T


def attention_specs(block_rows, tok_rows, keys):
    subs = block_rows // BLOCK_Q
    pieces = BLOCK_Q // tok_rows
    n_kb = keys // BLOCK_K

    def wrap(index):
        return lambda i, *_: index(i)

    q_spec = lambda cap: pl.BlockSpec((1, HEAD_DIM, BLOCK_Q), wrap(lambda i: (cap(i) // subs, 0, cap(i) % subs)))
    row_spec = lambda cap: pl.BlockSpec((1, 1, BLOCK_Q), wrap(lambda i: (cap(i) // subs, 0, cap(i) % subs)))
    piece_spec = lambda cap: pl.BlockSpec(
        (pieces, 1, HEAD_DIM, tok_rows), wrap(lambda i: (cap(i) % subs, cap(i) // subs, 0, 0))
    )
    kv_spec = pl.BlockSpec(
        (n_kb, 2 * HEAD_DIM, BLOCK_K), wrap(lambda i: (0, 0, 0)), pipeline_mode=pl.Buffered(1)
    )
    return q_spec, row_spec, piece_spec, kv_spec


def attention_forward(bounds, qkv, kv, starts, n_head, tok_rows):
    hb, _, block_rows = qkv.shape
    keys = kv.shape[0] * BLOCK_K
    n_steps = hb * block_rows // BLOCK_Q
    q_spec, row_spec, piece_spec, kv_spec = attention_specs(block_rows, tok_rows, keys)
    same = lambda i: i
    return pl.pallas_call(
        forward_kernel,
        grid_spec=pltpu.PrefetchScalarGridSpec(
            num_scalar_prefetch=3,
            grid=(n_steps,),
            in_specs=[q_spec(same), kv_spec, row_spec(same)],
            out_specs=[piece_spec(same), q_spec(same), row_spec(same)],
            scratch_shapes=[pltpu.VMEM((keys, 2 * HEAD_DIM), bf16)],
        ),
        out_shape=[
            jax.ShapeDtypeStruct((n_head, hb, HEAD_DIM, tok_rows), bf16),
            jax.ShapeDtypeStruct((hb, HEAD_DIM, block_rows), f32),
            jax.ShapeDtypeStruct((hb, 1, block_rows), f32),
        ],
        compiler_params=pltpu.CompilerParams(vmem_limit_bytes=VMEM_BYTES),
        name="attention_forward",
    )(*bounds, qkv, kv, starts)


def attention_backward(bounds, qkv, kv, starts, do, wide, lse):
    hb, _, block_rows = qkv.shape
    n_kb = kv.shape[0]
    keys = n_kb * BLOCK_K
    n_steps = hb * block_rows // BLOCK_Q
    q_spec, row_spec, piece_spec, kv_spec = attention_specs(block_rows, do.shape[3], keys)
    cap = lambda i: jnp.minimum(i, n_steps - 1)
    return pl.pallas_call(
        functools.partial(backward_kernel, n_steps),
        grid_spec=pltpu.PrefetchScalarGridSpec(
            num_scalar_prefetch=3,
            grid=(n_steps + n_kb,),
            in_specs=[q_spec(cap), kv_spec, row_spec(cap), piece_spec(cap), q_spec(cap), row_spec(cap)],
            out_specs=[
                q_spec(cap),
                pl.BlockSpec((1, 2 * HEAD_DIM, BLOCK_K), lambda i, *_: (jnp.maximum(i - n_steps, 0), 0, 0)),
            ],
            scratch_shapes=[pltpu.VMEM((keys, 2 * HEAD_DIM), bf16), pltpu.VMEM((keys, 2 * HEAD_DIM), f32)],
        ),
        out_shape=[
            jax.ShapeDtypeStruct((hb, HEAD_DIM, block_rows), bf16),
            jax.ShapeDtypeStruct((n_kb, 2 * HEAD_DIM, BLOCK_K), bf16),
        ],
        compiler_params=pltpu.CompilerParams(vmem_limit_bytes=VMEM_BYTES),
        name="attention_backward",
    )(*bounds, qkv, kv, starts, do, wide, lse)


def on_device(
    tokens,
    cotangent,
    segment,
    norm_gain,
    norm_shift,
    in_weight,
    query_bias,
    value_bias,
    out_weight,
    out_bias,
    post_gain,
    post_shift,
    up_weight,
    up_bias,
    down_weight,
    down_bias,
):
    n_head, n_u, n_v, n_rest = (lax.axis_size(a) for a in ALL)
    hb = n_u * n_v
    n_blk = hb * n_rest
    n_all = n_head * n_blk
    me_head, me_u, me_v, me_rest = (lax.axis_index(a) for a in ALL)
    me_blk = (me_u * n_v + me_v) * n_rest + me_rest
    tok_rows, width = tokens.shape
    block_rows = tok_rows * n_head
    length = segment.shape[0]
    w_rows = in_weight.shape[0]
    group = 3 * hb * HEAD_DIM

    chips = n_head * hb
    f_rows = down_weight.shape[0] // 2

    up_cols = up_weight.reshape(w_rows, chips, n_rest, 2, f_rows).transpose(2, 0, 3, 1, 4)
    up_cols = exchange_axis(up_cols.reshape(n_rest, w_rows, 2 * chips * f_rows), "rest").reshape(n_rest * w_rows, -1)
    out_rows = gather_axis(out_weight, "rest").reshape(n_rest * w_rows, width)
    down_rows = down_weight.reshape(2, f_rows, width)
    f_half = chips * f_rows
    if f_rows == n_rest * w_rows:
        joint = jnp.concatenate([up_cols, down_rows[0], down_rows[1], out_rows], axis=1)
        joint = lax.all_gather(joint, ("head", "u", "v"), axis=0, tiled=True)
        w_up = joint[:, : 2 * f_half]
        w_down = joint[:, 2 * f_half : 2 * f_half + width], joint[:, 2 * f_half + width : 2 * f_half + 2 * width]
        w_out = joint[:, 2 * f_half + 2 * width :]
    else:
        w_up, w_down_a, w_down_b, w_out = (
            lax.all_gather(w, ("head", "u", "v"), axis=0, tiled=True)
            for w in (up_cols, down_rows[0], down_rows[1], out_rows)
        )
        w_down = w_down_a, w_down_b

    parts = [norm_gain, norm_shift, query_bias, value_bias, out_bias, post_gain, post_shift, down_bias, up_bias]
    packed = [jnp.concatenate(parts).reshape(1, -1)]

    cols = in_weight.reshape(w_rows, 3, n_head, hb, HEAD_DIM).transpose(2, 0, 3, 1, 4).reshape(n_head, w_rows, group)
    w_in = [cols]

    def chain_one():
        for axis in ("rest", "v"):
            packed[0] = gather_axis(packed[0], axis)
        w_in[0] = exchange_axis(w_in[0], "head")
        return (packed[0], w_in[0])

    def chain_two():
        for axis in ("u", "head"):
            packed[0] = gather_axis(packed[0], axis)
        w_in[0] = gather_axis(w_in[0], "v")
        return (packed[0], w_in[0])

    rows_all = gather_line(tokens, "head", [chain_one, chain_two, None]).reshape(block_rows, width).astype(f32)
    packed = packed[0].reshape(n_all, -1)
    vectors, at = [], 0
    for part in parts:
        size = part.shape[0]
        vectors.append(packed[:, at : at + size].reshape(-1).astype(f32))
        at += size
    gain_a, shift_a, bias_q, bias_v, bias_out, gain_b, shift_b, bias_down, bias_up = vectors
    w_in = gather_axis(gather_axis(w_in[0], "u"), "rest")
    w_in = w_in.transpose(3, 1, 2, 0, 4, 5).reshape(width, group)

    normed, unit_all, inverse_all = norm_forward(rows_all, gain_a, shift_a)
    normed_low = normed.astype(bf16)
    group_bias = jnp.stack([bias_q, jnp.zeros_like(bias_q), bias_v]).reshape(3, n_head, hb, HEAD_DIM)
    group_bias = lax.dynamic_index_in_dim(group_bias, me_head, 1, keepdims=False).transpose(1, 0, 2).reshape(group, 1)
    projected = lax.dot_general(w_in, normed_low, (((0,), (1,)), ((), ())), preferred_element_type=f32)
    projected = (projected + group_bias).astype(bf16)
    qkv = lax.all_to_all(
        projected.reshape(hb, 3 * HEAD_DIM, block_rows), ("u", "v"), split_axis=0, concat_axis=0, tiled=True
    )
    subs_k = block_rows // BLOCK_K
    kv = gather_axis(qkv[:, HEAD_DIM:], "rest")
    kv = kv.reshape(n_rest, hb, 2 * HEAD_DIM, subs_k, BLOCK_K).transpose(1, 0, 3, 2, 4)
    kv = kv.reshape(n_blk * subs_k, 2 * HEAD_DIM, BLOCK_K)

    doc_start = jnp.zeros_like(segment)
    for doc in range(1, DOCS):
        first = jnp.sum((segment < doc).astype(jnp.int32))
        doc_start = jnp.where(segment == doc, first, doc_start)
    starts = lax.dynamic_index_in_dim(doc_start.reshape(hb, n_rest, block_rows), me_rest, 1, keepdims=False)
    starts_q = starts.reshape(-1, BLOCK_Q)
    lo = starts_q[:, 0] // BLOCK_K
    mid = (starts_q[:, -1] + BLOCK_K - 1) // BLOCK_K
    q_first = (jnp.arange(hb, dtype=jnp.int32)[:, None] * n_rest + me_rest) * block_rows
    q_first = (q_first + jnp.arange(block_rows // BLOCK_Q, dtype=jnp.int32)[None] * BLOCK_Q).reshape(-1)
    bounds = (lo, mid, q_first)
    starts = starts.reshape(hb, 1, block_rows)

    attended, wide, lse = attention_forward(bounds, qkv, kv, starts, n_head, tok_rows)
    back = lax.all_to_all(
        attended.reshape(HEADS, HEAD_DIM, tok_rows), ("head", "u", "v"), split_axis=0, concat_axis=0, tiled=True
    ).reshape(width, tok_rows)

    rows = tokens.astype(f32)
    branch = lax.dot_general(back, w_out, (((0,), (0,)), ((), ())), preferred_element_type=f32) + bias_out
    middle = rows + branch
    hidden_in, unit_mid, inverse_mid = norm_forward(middle, gain_b, shift_b)
    hidden_low = hidden_in.astype(bf16)
    hidden_all = gather_axis(hidden_low, "rest").reshape(n_rest * tok_rows, width)
    cot_all = gather_axis(cotangent, "rest").reshape(n_rest * tok_rows, width)
    bias_units = lax.dynamic_index_in_dim(bias_up.reshape(chips, n_rest, 2, f_rows), me_rest, 1, keepdims=False)
    bias_units = bias_units.transpose(1, 0, 2).reshape(-1)
    pre = jnp.dot(hidden_all, w_up, preferred_element_type=f32) + bias_units
    act, slope = gelu_parts(pre)
    act_low = act.astype(bf16)
    acts = act_low[:, :f_half], act_low[:, f_half:]
    down = jnp.dot(acts[0], w_down[0], preferred_element_type=f32)
    down = down + jnp.dot(acts[1], w_down[1], preferred_element_type=f32)
    down = reduce_axis(down.reshape(n_rest, tok_rows, width), "rest")
    output = (middle + down + bias_down).astype(bf16)
    grad_out = cotangent.astype(f32)
    grad_act = jnp.concatenate(
        [jnp.einsum("td,fd->tf", cot_all, w, preferred_element_type=f32) for w in w_down], axis=1
    )
    grad_pre = (grad_act * slope).astype(bf16)
    grad_hidden = jnp.einsum("tf,df->td", grad_pre, w_up, preferred_element_type=f32)
    grad_hidden = reduce_axis(grad_hidden.reshape(n_rest, tok_rows, width), "rest")
    grad_middle = grad_out + norm_inner(grad_hidden, unit_mid, inverse_mid, gain_b)
    grad_branch = grad_middle.astype(bf16)
    grad_back = lax.dot_general(w_out, grad_branch, (((1,), (1,)), ((), ())), preferred_element_type=f32).astype(bf16)
    grad_heads = lax.all_to_all(
        grad_back.reshape(HEADS, HEAD_DIM, tok_rows), ("head", "u", "v"), split_axis=0, concat_axis=0, tiled=True
    ).reshape(n_head, hb, HEAD_DIM, tok_rows)

    down_grads = [jnp.einsum("tf,td->fd", a, cot_all, preferred_element_type=f32).astype(bf16) for a in acts]
    up_grad = jnp.einsum("td,tf->df", hidden_all, grad_pre, preferred_element_type=f32).astype(bf16)
    out_grad = jnp.einsum("dt,te->de", back, grad_branch, preferred_element_type=f32).astype(bf16)
    out_grad = out_grad.reshape(chips, n_rest, w_rows, width).transpose(1, 0, 2, 3)
    out_grad = reduce_axis(out_grad, "rest").astype(bf16)
    plane = lambda x: x.reshape(n_head, n_u, n_v, -1, x.shape[-1])
    by_u = [plane(up_grad).transpose(1, 2, 0, 3, 4)]
    by_v = [plane(x).transpose(2, 1, 0, 3, 4) for x in (*down_grads, out_grad)]
    sums = [
        jnp.sum(grad_branch.astype(f32), axis=0),
        jnp.sum(grad_hidden * unit_mid, axis=0),
        jnp.sum(grad_hidden, axis=0),
        jnp.sum(grad_out, axis=0),
    ]
    small = jnp.stack([s.reshape(chips, n_rest, -1) for s in sums], axis=2).reshape(chips, n_rest, -1)
    small = reduce_axis(small.transpose(1, 0, 2), "rest")
    unit_sum = jnp.sum(grad_pre.astype(f32), axis=0).reshape(2, chips, f_rows).transpose(1, 0, 2).reshape(chips, -1)
    small = jnp.concatenate([small, unit_sum], axis=1).reshape(n_head, n_u, n_v, -1)

    grad_heads, by_u, by_v, small = lax.optimization_barrier((grad_heads, by_u, by_v, small))
    by_u = [reduce_axis(x, "u").astype(bf16) for x in by_u]
    by_v = [reduce_axis(x, "v").astype(bf16) for x in by_v]

    dq, dkv = attention_backward(bounds, qkv, kv, starts, grad_heads, wide, lse)
    dkv = dkv.reshape(hb, n_rest, subs_k, 2 * HEAD_DIM, BLOCK_K).transpose(1, 0, 3, 2, 4)
    dkv = reduce_axis(dkv.reshape(n_rest, hb, 2 * HEAD_DIM, block_rows), "rest").astype(bf16)
    grad_proj = lax.all_to_all(
        jnp.concatenate([dq, dkv], axis=1), ("u", "v"), split_axis=0, concat_axis=0, tiled=True
    ).reshape(group, block_rows)

    grad_proj, by_u, by_v, small = lax.optimization_barrier((grad_proj, by_u, by_v, small))
    by_u = [reduce_axis(x, "v").astype(bf16) for x in by_u]
    by_v = [reduce_axis(x, "u").astype(bf16) for x in by_v]
    small = reduce_axis(reduce_axis(small, "head"), "u")
    small = reduce_axis(small, "v")

    grad_normed = lax.dot_general(grad_proj, w_in, (((0,), (1,)), ((), ())), preferred_element_type=f32)
    grad_tokens = reduce_axis(grad_normed.astype(bf16).reshape(n_head, tok_rows, width), "head")
    grad_tokens, by_u, by_v = lax.optimization_barrier((grad_tokens, by_u, by_v))
    up_weight_grad = reduce_axis(by_u[0], "head").astype(bf16).reshape(n_rest, w_rows, -1)
    up_weight_grad = exchange_axis(up_weight_grad, "rest").astype(f32)
    up_weight_grad = up_weight_grad.reshape(n_rest, w_rows, 2, chips, f_rows).transpose(1, 3, 0, 2, 4)
    up_weight_grad = up_weight_grad.reshape(w_rows, -1)
    down_a, down_b, out_weight_grad = (reduce_axis(x, "head") for x in by_v)
    down_weight_grad = jnp.concatenate([down_a, down_b], axis=0)
    size = width // n_all
    out_bias_grad, post_gain_grad, post_shift_grad, down_bias_grad = (
        small[i * size : (i + 1) * size] for i in range(4)
    )
    up_bias_grad = small[4 * size :]
    unit_in = lax.dynamic_index_in_dim(unit_all.reshape(n_head, tok_rows, width), me_head, 0, keepdims=False)
    inverse_in = lax.dynamic_index_in_dim(inverse_all.reshape(n_head, tok_rows, 1), me_head, 0, keepdims=False)
    tokens_grad = (grad_middle + norm_inner(grad_tokens, unit_in, inverse_in, gain_a)).astype(bf16)

    in_grad = lax.dot_general(normed_low, grad_proj, (((0,), (1,)), ((), ())), preferred_element_type=f32)
    gain_grad = jnp.sum(grad_normed * unit_all, axis=0).reshape(n_head, n_blk, w_rows)
    shift_grad = jnp.sum(grad_normed, axis=0).reshape(n_head, n_blk, w_rows)
    col_sum = jnp.sum(grad_proj.astype(f32), axis=1).reshape(hb, 3, HEAD_DIM)
    mine = (jnp.arange(n_head) == me_head)[:, None, None]
    query_sum = jnp.where(mine, col_sum[:, 0].reshape(1, n_blk, w_rows), 0.0)
    value_sum = jnp.where(mine, col_sum[:, 2].reshape(1, n_blk, w_rows), 0.0)
    extra = jnp.stack([gain_grad, shift_grad, query_sum, value_sum], axis=-1)
    extra = jnp.pad(extra, ((0, 0), (0, 0), (0, 0), (0, 124)))
    joined = jnp.concatenate([in_grad.reshape(n_head, n_blk, w_rows, group), extra], axis=-1).astype(bf16)
    joined = joined.transpose(1, 0, 2, 3).reshape(hb, n_rest, n_head, w_rows, group + 128).transpose(1, 0, 2, 3, 4)
    joined = reduce_axis(joined, "rest").astype(bf16).reshape(n_u, n_v, n_head, w_rows, group + 128)
    joined = reduce_axis(joined, "u").astype(bf16)
    joined = reduce_axis(joined, "v").astype(bf16)
    joined = exchange_axis(joined, "head").astype(f32)
    in_weight_grad = joined[:, :, :group].reshape(n_head, w_rows, hb, 3, HEAD_DIM).transpose(1, 3, 0, 2, 4)
    in_weight_grad = in_weight_grad.reshape(w_rows, 3 * width)
    extra = jnp.sum(joined[:, :, group : group + 4], axis=0)
    return (
        output,
        tokens_grad,
        extra[:, 0],
        extra[:, 1],
        in_weight_grad,
        extra[:, 2],
        extra[:, 3],
        out_weight_grad,
        out_bias_grad,
        post_gain_grad,
        post_shift_grad,
        up_weight_grad,
        up_bias_grad,
        down_weight_grad,
        down_bias_grad,
    )


def solution(mesh):
    n_head, n_blk = mesh.shape["head"], mesh.shape["blk"]
    hb = HEADS // n_head
    n_u = 2 if hb % 2 == 0 else 1
    fine = Mesh(mesh.devices.reshape(n_head, n_u, hb // n_u, n_blk // hb), ALL)
    tok = P(("u", "v", "rest", "head"), None)
    vec = P(ALL)
    mat = P(ALL, None)
    return jax.shard_map(
        on_device,
        mesh=fine,
        in_specs=(tok, tok, P(), vec, vec, mat, vec, vec, mat, vec, vec, vec, mat, vec, mat, vec),
        out_specs=(tok, tok, vec, vec, mat, vec, vec, mat, vec, vec, vec, mat, vec, mat, vec),
        check_vma=False,
    )
```

```python
import functools

import jax
import jax.numpy as jnp
from jax import lax
from jax.experimental import pallas as pl
from jax.experimental.pallas import tpu as pltpu
from jax.sharding import Mesh
from jax.sharding import PartitionSpec as P

HEADS = 16
HEAD_DIM = 64
DOCS = 4
BLOCK_Q = 512
BLOCK_K = 512
VMEM_BYTES = 56 * 1024 * 1024

EPS = 1e-05
NEGATIVE = -1e30
GELU_C = 0.7978845608028654
SCALE = HEAD_DIM ** (-0.5)
ALL = ("head", "u", "v", "rest")
f32 = jnp.float32
bf16 = jnp.bfloat16


def norm_forward(rows, gain, shift):
    center = rows - jnp.mean(rows, axis=-1, keepdims=True)
    var = jnp.mean(center * center, axis=-1, keepdims=True)
    inverse = lax.rsqrt(var + EPS)
    unit = center * inverse
    return (unit * gain + shift, unit, inverse)


def norm_inner(grad, unit, inverse, gain):
    scaled = grad * gain
    inner = (
        scaled
        - jnp.mean(scaled, axis=-1, keepdims=True)
        - unit * jnp.mean(scaled * unit, axis=-1, keepdims=True)
    )
    return inverse * inner


def gelu_parts(pre):
    cubic = pre * pre * pre
    tangent = jnp.tanh(GELU_C * (pre + 0.044715 * cubic))
    value = 0.5 * pre * (1.0 + tangent)
    slope = 0.5 * (1.0 + tangent) + 0.5 * pre * (1.0 - tangent * tangent) * GELU_C * (
        1.0 + 3.0 * 0.044715 * pre * pre
    )
    return (value, slope)


def shifted(x, axis, k):
    n = lax.axis_size(axis)
    return lax.ppermute(x, axis, [(i, (i + k) % n) for i in range(n)])


def put(buffer, x, index):
    return lax.dynamic_update_index_in_dim(buffer, x, index, 0)


def gather_axis(x, axis):
    n = lax.axis_size(axis)
    if n == 1:
        return x[None]
    me = lax.axis_index(axis)
    out = put(jnp.zeros((n,) + x.shape, x.dtype), x, me)
    for k in range(1, n):
        out = put(out, shifted(x, axis, k), (me - k) % n)
    return out


def gather_line(x, axis, beside):
    n = lax.axis_size(axis)
    if n != 4:
        for make in beside:
            if make is not None:
                make()
        return gather_axis(x, axis)
    me = lax.axis_index(axis)
    up = [(i, i + 1) for i in range(n - 1)]
    down = [(i + 1, i) for i in range(n - 1)]
    left, right = [x], [x]
    for i in range(n - 1):
        left.append(lax.ppermute(left[-1], axis, up))
        right.append(lax.ppermute(right[-1], axis, down))
        if beside[i] is not None:
            made = beside[i]()
            left[-1], right[-1], _ = lax.optimization_barrier((left[-1], right[-1], made))
    low = me < 2
    first = jnp.where(low, right[1], left[1])
    second = jnp.where(low, right[2], left[2])
    inner = jnp.where(me == 1, left[1], right[1])
    third = jnp.where(me == 0, right[3], jnp.where(me == 3, left[3], inner))
    out = put(jnp.zeros((n,) + x.shape, x.dtype), x, me)
    out = put(out, first, jnp.where(low, me + 1, me - 1))
    out = put(out, second, jnp.where(low, me + 2, me - 2))
    return put(out, third, jnp.where(me == 0, 3, jnp.where(me == 3, 0, jnp.where(me == 1, 0, 3))))


def reduce_begin(x, axis):
    n = lax.axis_size(axis)
    if n == 1:
        return [x[0]]
    me = lax.axis_index(axis)
    pieces = [lax.dynamic_index_in_dim(x, (me + k) % n, 0, keepdims=False) for k in range(n)]
    return pieces[:1] + [shifted(pieces[k], axis, k) for k in range(1, n)]


def reduce_end(pieces):
    total = pieces[0].astype(f32)
    for piece in pieces[1:]:
        total = total + piece.astype(f32)
    return total


def reduce_axis(x, axis):
    return reduce_end(reduce_begin(x, axis))


def exchange_axis(x, axis):
    n = lax.axis_size(axis)
    if n == 1:
        return x
    me = lax.axis_index(axis)
    mine = lax.dynamic_index_in_dim(x, me, 0, keepdims=False)
    out = put(jnp.zeros_like(x), mine, me)
    for k in range(1, n):
        piece = lax.dynamic_index_in_dim(x, (me + k) % n, 0, keepdims=False)
        out = put(out, shifted(piece, axis, k), (me - k) % n)
    return out


def allowed_keys(kb, starts, pos):
    t = kb * BLOCK_K + lax.broadcasted_iota(jnp.int32, (BLOCK_K, BLOCK_Q), 0)
    return (t >= starts) & (t <= pos)


def lay_rows(me, own_ref, far_ref, rows_ref, cols_ref, first):
    hb, _, block_rows = own_ref.shape
    n_rest = far_ref.shape[0] + 1
    subs = block_rows // BLOCK_K

    def lay(read, b, rest):
        for sub in range(subs):
            kb = (b * n_rest + rest) * subs + sub
            block = read(b)[:, sub * BLOCK_K : (sub + 1) * BLOCK_K]
            rows_ref[pl.ds(pl.multiple_of(kb * BLOCK_K, BLOCK_K), BLOCK_K), :] = block[HEAD_DIM:].T
            cols_ref[kb] = block[first : first + HEAD_DIM]

    def each(b, _):
        lay(lambda b: own_ref[b], b, me)
        for k in range(1, n_rest):
            lay(lambda b: far_ref[k - 1, b], b, (me - k) % n_rest)
        return 0

    lax.fori_loop(0, hb, each, 0)


def forward_kernel(
    lo_ref, mid_ref, q0_ref, me_ref, q_ref, own_ref, far_ref, start_ref, o_ref, wide_ref, lse_ref, rows_ref, cols_ref
):
    step = pl.program_id(0)

    @pl.when(step == 0)
    def _():
        lay_rows(me_ref[0], own_ref, far_ref, rows_ref, cols_ref, 2 * HEAD_DIM)

    first = q0_ref[step]
    q = q_ref[0] * jnp.asarray(SCALE, bf16)
    q_pad = jnp.concatenate([q, jnp.zeros_like(q)], axis=0)
    starts = start_ref[0]
    pos = first + lax.broadcasted_iota(jnp.int32, (1, BLOCK_Q), 1)

    def body(masked, kb, carry):
        top, total, acc = carry
        rows = rows_ref[pl.ds(pl.multiple_of(kb * BLOCK_K, BLOCK_K), BLOCK_K), :]
        s = jnp.dot(rows, q_pad, preferred_element_type=f32)
        if masked:
            s = jnp.where(allowed_keys(kb, starts, pos), s, NEGATIVE)
        new_top = jnp.maximum(top, jnp.max(s, axis=0, keepdims=True))
        p = jnp.exp(s - new_top)
        factor = jnp.exp(top - new_top)
        values = cols_ref[kb]
        acc = acc * factor + jnp.dot(values, p.astype(bf16), preferred_element_type=f32)
        return (new_top, total * factor + jnp.sum(p, axis=0, keepdims=True), acc)

    diagonal = first // BLOCK_K
    mid = jnp.minimum(mid_ref[step], diagonal)
    carry = (
        jnp.full((1, BLOCK_Q), NEGATIVE, f32),
        jnp.zeros((1, BLOCK_Q), f32),
        jnp.zeros((HEAD_DIM, BLOCK_Q), f32),
    )
    carry = lax.fori_loop(lo_ref[step], mid, functools.partial(body, True), carry)
    carry = lax.fori_loop(mid, diagonal, functools.partial(body, False), carry)
    last = (first + BLOCK_Q + BLOCK_K - 1) // BLOCK_K
    top, total, acc = lax.fori_loop(diagonal, last, functools.partial(body, True), carry)
    out = acc / total
    wide_ref[0] = out
    lse_ref[0] = top + jnp.log(total)
    low = out.astype(bf16)
    piece = o_ref.shape[3]
    for i in range(o_ref.shape[0]):
        o_ref[i, 0] = low[:, i * piece : (i + 1) * piece]


def backward_kernel(
    n_steps,
    lo_ref,
    mid_ref,
    q0_ref,
    me_ref,
    q_ref,
    own_ref,
    far_ref,
    start_ref,
    do_ref,
    wide_ref,
    lse_ref,
    dq_ref,
    dkv_ref,
    rows_ref,
    cols_ref,
    acc_ref,
):
    step = pl.program_id(0)

    @pl.when(step == 0)
    def _():
        lay_rows(me_ref[0], own_ref, far_ref, rows_ref, cols_ref, HEAD_DIM)
        acc_ref[...] = jnp.zeros_like(acc_ref)

    @pl.when(step < n_steps)
    def _():
        first = q0_ref[step]
        q = q_ref[0] * jnp.asarray(SCALE, bf16)
        do = jnp.concatenate([do_ref[i, 0] for i in range(do_ref.shape[0])], axis=1)
        zero = jnp.zeros_like(q)
        q_pad = jnp.concatenate([q, zero], axis=0)
        do_pad = jnp.concatenate([zero, do], axis=0)
        q_rows = q_pad.T
        do_rows = do_pad.T
        starts = start_ref[0]
        lse = lse_ref[0]
        delta = jnp.sum(do.astype(f32) * wide_ref[0], axis=0, keepdims=True)
        pos = first + lax.broadcasted_iota(jnp.int32, (1, BLOCK_Q), 1)

        def body(masked, kb, dq):
            at = pl.ds(pl.multiple_of(kb * BLOCK_K, BLOCK_K), BLOCK_K)
            rows = rows_ref[at, :]
            s = jnp.dot(rows, q_pad, preferred_element_type=f32)
            p = jnp.exp(s - lse)
            if masked:
                p = jnp.where(allowed_keys(kb, starts, pos), p, 0.0)
            dp = jnp.dot(rows, do_pad, preferred_element_type=f32)
            ds = (p * (dp - delta)).astype(bf16)
            acc_ref[at, :] += jnp.dot(p.astype(bf16), do_rows, preferred_element_type=f32) + jnp.dot(
                ds, q_rows, preferred_element_type=f32
            )
            return dq + jnp.dot(cols_ref[kb], ds, preferred_element_type=f32)

        diagonal = first // BLOCK_K
        mid = jnp.minimum(mid_ref[step], diagonal)
        dq = jnp.zeros((HEAD_DIM, BLOCK_Q), f32)
        dq = lax.fori_loop(lo_ref[step], mid, functools.partial(body, True), dq)
        dq = lax.fori_loop(mid, diagonal, functools.partial(body, False), dq)
        last = (first + BLOCK_Q + BLOCK_K - 1) // BLOCK_K
        dq = lax.fori_loop(diagonal, last, functools.partial(body, True), dq)
        dq_ref[0] = (dq * SCALE).astype(bf16)

    @pl.when(step >= n_steps)
    def _():
        kb = jnp.maximum(step - n_steps, 0)
        at = pl.ds(pl.multiple_of(kb * BLOCK_K, BLOCK_K), BLOCK_K)
        dkv_ref[0, 0] = acc_ref[at, :].astype(bf16).T


def attention_specs(qkv, far, tok_rows):
    hb, depth, block_rows = qkv.shape
    subs = block_rows // BLOCK_Q
    pieces = BLOCK_Q // tok_rows

    def wrap(index):
        return lambda i, *_: index(i)

    q_spec = lambda cap: pl.BlockSpec((1, HEAD_DIM, BLOCK_Q), wrap(lambda i: (cap(i) // subs, 0, cap(i) % subs)))
    row_spec = lambda cap: pl.BlockSpec((1, 1, BLOCK_Q), wrap(lambda i: (cap(i) // subs, 0, cap(i) % subs)))
    piece_spec = lambda cap: pl.BlockSpec(
        (pieces, 1, HEAD_DIM, tok_rows), wrap(lambda i: (cap(i) % subs, cap(i) // subs, 0, 0))
    )
    own_spec = pl.BlockSpec((hb, depth, block_rows), wrap(lambda i: (0, 0, 0)), pipeline_mode=pl.Buffered(1))
    far_spec = pl.BlockSpec(far.shape, wrap(lambda i: (0, 0, 0, 0)), pipeline_mode=pl.Buffered(1))
    return q_spec, row_spec, piece_spec, own_spec, far_spec


def padded_cost(products, queries, keys):
    pairs = queries * keys // 2
    return pl.CostEstimate(flops=products * 2 * 256 * pairs, transcendentals=pairs, bytes_accessed=8 * keys * HEAD_DIM)


def attention_forward(bounds, qkv, far, starts, n_head, tok_rows):
    hb, _, block_rows = qkv.shape
    queries = hb * block_rows
    keys = queries * (far.shape[0] + 1)
    q_spec, row_spec, piece_spec, own_spec, far_spec = attention_specs(qkv, far, tok_rows)
    same = lambda i: i
    return pl.pallas_call(
        forward_kernel,
        grid_spec=pltpu.PrefetchScalarGridSpec(
            num_scalar_prefetch=4,
            grid=(queries // BLOCK_Q,),
            in_specs=[q_spec(same), own_spec, far_spec, row_spec(same)],
            out_specs=[piece_spec(same), q_spec(same), row_spec(same)],
            scratch_shapes=[
                pltpu.VMEM((keys, 2 * HEAD_DIM), bf16),
                pltpu.VMEM((keys // BLOCK_K, HEAD_DIM, BLOCK_K), bf16),
            ],
        ),
        out_shape=[
            jax.ShapeDtypeStruct((n_head, hb, HEAD_DIM, tok_rows), bf16),
            jax.ShapeDtypeStruct((hb, HEAD_DIM, block_rows), f32),
            jax.ShapeDtypeStruct((hb, 1, block_rows), f32),
        ],
        compiler_params=pltpu.CompilerParams(vmem_limit_bytes=VMEM_BYTES),
        cost_estimate=padded_cost(2, queries, keys),
        name="attention_forward",
    )(*bounds, qkv, qkv, far, starts)


def attention_backward(bounds, qkv, far, starts, do, wide, lse):
    hb, _, block_rows = qkv.shape
    n_rest = far.shape[0] + 1
    queries = hb * block_rows
    keys = queries * n_rest
    n_kb = keys // BLOCK_K
    subs = block_rows // BLOCK_K
    n_steps = queries // BLOCK_Q
    q_spec, row_spec, piece_spec, own_spec, far_spec = attention_specs(qkv, far, do.shape[3])
    cap = lambda i: jnp.minimum(i, n_steps - 1)

    def place(i, *_):
        kb = jnp.maximum(i - n_steps, 0)
        return (kb // subs % n_rest, kb // subs // n_rest, 0, kb % subs)

    return pl.pallas_call(
        functools.partial(backward_kernel, n_steps),
        grid_spec=pltpu.PrefetchScalarGridSpec(
            num_scalar_prefetch=4,
            grid=(n_steps + n_kb,),
            in_specs=[q_spec(cap), own_spec, far_spec, row_spec(cap), piece_spec(cap), q_spec(cap), row_spec(cap)],
            out_specs=[q_spec(cap), pl.BlockSpec((1, 1, 2 * HEAD_DIM, BLOCK_K), place)],
            scratch_shapes=[
                pltpu.VMEM((keys, 2 * HEAD_DIM), bf16),
                pltpu.VMEM((n_kb, HEAD_DIM, BLOCK_K), bf16),
                pltpu.VMEM((keys, 2 * HEAD_DIM), f32),
            ],
        ),
        out_shape=[
            jax.ShapeDtypeStruct((hb, HEAD_DIM, block_rows), bf16),
            jax.ShapeDtypeStruct((n_rest, hb, 2 * HEAD_DIM, block_rows), bf16),
        ],
        compiler_params=pltpu.CompilerParams(vmem_limit_bytes=VMEM_BYTES),
        cost_estimate=padded_cost(5, queries, keys),
        name="attention_backward",
    )(*bounds, qkv, qkv, far, starts, do, wide, lse)


def on_device(
    tokens,
    cotangent,
    segment,
    norm_gain,
    norm_shift,
    in_weight,
    query_bias,
    value_bias,
    out_weight,
    out_bias,
    post_gain,
    post_shift,
    up_weight,
    up_bias,
    down_weight,
    down_bias,
):
    n_head, n_u, n_v, n_rest = (lax.axis_size(a) for a in ALL)
    hb = n_u * n_v
    n_blk = hb * n_rest
    n_all = n_head * n_blk
    me_head, me_u, me_v, me_rest = (lax.axis_index(a) for a in ALL)
    me_blk = (me_u * n_v + me_v) * n_rest + me_rest
    tok_rows, width = tokens.shape
    block_rows = tok_rows * n_head
    length = segment.shape[0]
    w_rows = in_weight.shape[0]
    group = 3 * hb * HEAD_DIM

    chips = n_head * hb
    f_rows = down_weight.shape[0] // 2

    up_cols = up_weight.reshape(w_rows, chips, n_rest, 2, f_rows).transpose(2, 0, 3, 1, 4)
    up_cols = exchange_axis(up_cols.reshape(n_rest, w_rows, 2 * chips * f_rows), "rest").reshape(n_rest * w_rows, -1)
    out_rows = gather_axis(out_weight, "rest").reshape(n_rest * w_rows, width)
    down_rows = down_weight.reshape(2, f_rows, width)
    f_half = chips * f_rows

    parts = [norm_gain, norm_shift, query_bias, value_bias, out_bias, post_gain, post_shift, down_bias, up_bias]
    packed = [jnp.concatenate(parts).reshape(1, -1)]

    cols = in_weight.reshape(w_rows, 3, n_head, hb, HEAD_DIM).transpose(2, 0, 3, 1, 4).reshape(n_head, w_rows, group)
    w_in = [cols]

    def chain_one():
        for axis in ("rest", "v"):
            packed[0] = gather_axis(packed[0], axis)
        w_in[0] = exchange_axis(w_in[0], "head")
        return (packed[0], w_in[0])

    def chain_two():
        for axis in ("u", "head"):
            packed[0] = gather_axis(packed[0], axis)
        w_in[0] = gather_axis(w_in[0], "v")
        return (packed[0], w_in[0])

    rows_all = gather_line(tokens, "head", [chain_one, chain_two, None]).reshape(block_rows, width).astype(f32)
    rows_all, up_cols, down_rows, out_rows = lax.optimization_barrier((rows_all, up_cols, down_rows, out_rows))
    if f_rows == n_rest * w_rows:
        joint = jnp.concatenate([up_cols, down_rows[0], down_rows[1], out_rows], axis=1)
        joint = lax.all_gather(joint, ("head", "u", "v"), axis=0, tiled=True)
        w_up = joint[:, : 2 * f_half]
        w_down = joint[:, 2 * f_half : 2 * f_half + width], joint[:, 2 * f_half + width : 2 * f_half + 2 * width]
        w_out = joint[:, 2 * f_half + 2 * width :]
    else:
        w_up, w_down_a, w_down_b, w_out = (
            lax.all_gather(w, ("head", "u", "v"), axis=0, tiled=True)
            for w in (up_cols, down_rows[0], down_rows[1], out_rows)
        )
        w_down = w_down_a, w_down_b

    packed = packed[0].reshape(n_all, -1)
    vectors, at = [], 0
    for part in parts:
        size = part.shape[0]
        vectors.append(packed[:, at : at + size].reshape(-1).astype(f32))
        at += size
    gain_a, shift_a, bias_q, bias_v, bias_out, gain_b, shift_b, bias_down, bias_up = vectors
    w_in = gather_axis(gather_axis(w_in[0], "u"), "rest")
    w_in = w_in.transpose(3, 1, 2, 0, 4, 5).reshape(width, group)

    normed, unit_all, inverse_all = norm_forward(rows_all, gain_a, shift_a)
    normed_low = normed.astype(bf16)
    group_bias = jnp.stack([bias_q, jnp.zeros_like(bias_q), bias_v]).reshape(3, n_head, hb, HEAD_DIM)
    group_bias = lax.dynamic_index_in_dim(group_bias, me_head, 1, keepdims=False).transpose(1, 0, 2).reshape(group, 1)
    projected = lax.dot_general(w_in, normed_low, (((0,), (1,)), ((), ())), preferred_element_type=f32)
    projected = (projected + group_bias).astype(bf16)
    qkv = lax.all_to_all(
        projected.reshape(hb, 3 * HEAD_DIM, block_rows), ("u", "v"), split_axis=0, concat_axis=0, tiled=True
    )
    far = [shifted(qkv, "rest", k) for k in range(1, n_rest)]
    far = jnp.stack(far) if n_rest > 2 else far[0][None]

    doc_start = jnp.zeros_like(segment)
    for doc in range(1, DOCS):
        first = jnp.sum((segment < doc).astype(jnp.int32))
        doc_start = jnp.where(segment == doc, first, doc_start)
    starts = lax.dynamic_index_in_dim(doc_start.reshape(hb, n_rest, block_rows), me_rest, 1, keepdims=False)
    starts_q = starts.reshape(-1, BLOCK_Q)
    lo = starts_q[:, 0] // BLOCK_K
    mid = (starts_q[:, -1] + BLOCK_K - 1) // BLOCK_K
    q_first = (jnp.arange(hb, dtype=jnp.int32)[:, None] * n_rest + me_rest) * block_rows
    q_first = (q_first + jnp.arange(block_rows // BLOCK_Q, dtype=jnp.int32)[None] * BLOCK_Q).reshape(-1)
    bounds = (lo, mid, q_first, me_rest.astype(jnp.int32).reshape(1))
    starts = starts.reshape(hb, 1, block_rows)

    attended, wide, lse = attention_forward(bounds, qkv, far, starts, n_head, tok_rows)
    back = lax.all_to_all(
        attended.reshape(HEADS, HEAD_DIM, tok_rows), ("head", "u", "v"), split_axis=0, concat_axis=0, tiled=True
    ).reshape(width, tok_rows)

    rows = tokens.astype(f32)
    branch = lax.dot_general(back, w_out, (((0,), (0,)), ((), ())), preferred_element_type=f32) + bias_out
    middle = rows + branch
    hidden_in, unit_mid, inverse_mid = norm_forward(middle, gain_b, shift_b)
    hidden_low = hidden_in.astype(bf16)
    hidden_all = gather_axis(hidden_low, "rest").reshape(n_rest * tok_rows, width)
    cot_all = gather_axis(cotangent, "rest").reshape(n_rest * tok_rows, width)
    bias_units = lax.dynamic_index_in_dim(bias_up.reshape(chips, n_rest, 2, f_rows), me_rest, 1, keepdims=False)
    bias_units = bias_units.transpose(1, 0, 2).reshape(-1)
    pre = jnp.dot(hidden_all, w_up, preferred_element_type=f32) + bias_units
    act, slope = gelu_parts(pre)
    act_low = act.astype(bf16)
    acts = act_low[:, :f_half], act_low[:, f_half:]
    down = jnp.dot(acts[0], w_down[0], preferred_element_type=f32)
    down = down + jnp.dot(acts[1], w_down[1], preferred_element_type=f32)
    down = reduce_axis(down.reshape(n_rest, tok_rows, width), "rest")
    output = (middle + down + bias_down).astype(bf16)
    grad_out = cotangent.astype(f32)
    grad_act = jnp.concatenate(
        [jnp.einsum("td,fd->tf", cot_all, w, preferred_element_type=f32) for w in w_down], axis=1
    )
    grad_pre = (grad_act * slope).astype(bf16)
    grad_hidden = jnp.einsum("tf,df->td", grad_pre, w_up, preferred_element_type=f32)
    grad_hidden = reduce_axis(grad_hidden.reshape(n_rest, tok_rows, width), "rest")
    grad_middle = grad_out + norm_inner(grad_hidden, unit_mid, inverse_mid, gain_b)
    grad_branch = grad_middle.astype(bf16)
    grad_back = lax.dot_general(w_out, grad_branch, (((1,), (1,)), ((), ())), preferred_element_type=f32).astype(bf16)
    grad_heads = lax.all_to_all(
        grad_back.reshape(HEADS, HEAD_DIM, tok_rows), ("head", "u", "v"), split_axis=0, concat_axis=0, tiled=True
    ).reshape(n_head, hb, HEAD_DIM, tok_rows)

    down_grads = [jnp.einsum("tf,td->fd", a, cot_all, preferred_element_type=f32).astype(bf16) for a in acts]
    up_grad = jnp.einsum("td,tf->df", hidden_all, grad_pre, preferred_element_type=f32).astype(bf16)
    out_grad = jnp.einsum("dt,te->de", back, grad_branch, preferred_element_type=f32).astype(bf16)
    out_grad = out_grad.reshape(chips, n_rest, w_rows, width).transpose(1, 0, 2, 3)
    out_grad = reduce_axis(out_grad, "rest").astype(bf16)
    plane = lambda x: x.reshape(n_head, n_u, n_v, -1, x.shape[-1])
    up_grad = plane(up_grad).transpose(1, 2, 0, 3, 4)
    down_a, out_grad = (plane(x).transpose(2, 1, 0, 3, 4) for x in (down_grads[0], out_grad))
    down_b = plane(down_grads[1])
    sums = [
        jnp.sum(grad_branch.astype(f32), axis=0),
        jnp.sum(grad_hidden * unit_mid, axis=0),
        jnp.sum(grad_hidden, axis=0),
        jnp.sum(grad_out, axis=0),
    ]
    small = jnp.stack([s.reshape(chips, n_rest, -1) for s in sums], axis=2).reshape(chips, n_rest, -1)
    small = reduce_axis(small.transpose(1, 0, 2), "rest")
    unit_sum = jnp.sum(grad_pre.astype(f32), axis=0).reshape(2, chips, f_rows).transpose(1, 0, 2).reshape(chips, -1)
    small = jnp.concatenate([small, unit_sum], axis=1).reshape(n_head, n_u, n_v, -1)

    grad_heads, up_grad, down_a, out_grad, down_b, small = lax.optimization_barrier(
        (grad_heads, up_grad, down_a, out_grad, down_b, small)
    )
    begun = [reduce_begin(up_grad, "u"), reduce_begin(down_a, "v"), reduce_begin(out_grad, "v")]
    begun.append(reduce_begin(down_b, "head"))

    dq, dkv = attention_backward(bounds, qkv, far, starts, grad_heads, wide, lse)
    dq, dkv, begun = lax.optimization_barrier((dq, dkv, begun))
    up_grad, down_a, out_grad, down_b = (reduce_end(x).astype(bf16) for x in begun)
    dkv = reduce_axis(dkv, "rest").astype(bf16)
    grad_proj = lax.all_to_all(
        jnp.concatenate([dq, dkv], axis=1), ("u", "v"), split_axis=0, concat_axis=0, tiled=True
    ).reshape(group, block_rows)

    grad_proj, up_grad, down_a, out_grad, down_b, small = lax.optimization_barrier(
        (grad_proj, up_grad, down_a, out_grad, down_b, small)
    )
    up_grad = reduce_axis(up_grad, "v").astype(bf16)
    down_a, out_grad, down_b = (reduce_axis(x, "u").astype(bf16) for x in (down_a, out_grad, down_b))
    small = reduce_axis(reduce_axis(small, "head"), "u")
    small = reduce_axis(small, "v")

    grad_normed = lax.dot_general(grad_proj, w_in, (((0,), (1,)), ((), ())), preferred_element_type=f32)
    grad_tokens = reduce_axis(grad_normed.astype(bf16).reshape(n_head, tok_rows, width), "head")
    grad_tokens, up_grad, down_a, out_grad, down_b = lax.optimization_barrier(
        (grad_tokens, up_grad, down_a, out_grad, down_b)
    )
    up_weight_grad = reduce_axis(up_grad, "head").astype(bf16).reshape(n_rest, w_rows, -1)
    up_weight_grad = exchange_axis(up_weight_grad, "rest").astype(f32)
    up_weight_grad = up_weight_grad.reshape(n_rest, w_rows, 2, chips, f_rows).transpose(1, 3, 0, 2, 4)
    up_weight_grad = up_weight_grad.reshape(w_rows, -1)
    down_a, out_weight_grad = (reduce_axis(x, "head") for x in (down_a, out_grad))
    down_b = reduce_axis(down_b, "v")
    down_weight_grad = jnp.concatenate([down_a, down_b], axis=0)
    size = width // n_all
    out_bias_grad, post_gain_grad, post_shift_grad, down_bias_grad = (
        small[i * size : (i + 1) * size] for i in range(4)
    )
    up_bias_grad = small[4 * size :]
    unit_in = lax.dynamic_index_in_dim(unit_all.reshape(n_head, tok_rows, width), me_head, 0, keepdims=False)
    inverse_in = lax.dynamic_index_in_dim(inverse_all.reshape(n_head, tok_rows, 1), me_head, 0, keepdims=False)
    tokens_grad = (grad_middle + norm_inner(grad_tokens, unit_in, inverse_in, gain_a)).astype(bf16)

    in_grad = lax.dot_general(normed_low, grad_proj, (((0,), (1,)), ((), ())), preferred_element_type=f32)
    gain_grad = jnp.sum(grad_normed * unit_all, axis=0).reshape(n_head, n_blk, w_rows)
    shift_grad = jnp.sum(grad_normed, axis=0).reshape(n_head, n_blk, w_rows)
    col_sum = jnp.sum(grad_proj.astype(f32), axis=1).reshape(hb, 3, HEAD_DIM)
    mine = (jnp.arange(n_head) == me_head)[:, None, None]
    query_sum = jnp.where(mine, col_sum[:, 0].reshape(1, n_blk, w_rows), 0.0)
    value_sum = jnp.where(mine, col_sum[:, 2].reshape(1, n_blk, w_rows), 0.0)
    extra = jnp.stack([gain_grad, shift_grad, query_sum, value_sum], axis=-1)
    extra = jnp.pad(extra, ((0, 0), (0, 0), (0, 0), (0, 124)))
    joined = jnp.concatenate([in_grad.reshape(n_head, n_blk, w_rows, group), extra], axis=-1).astype(bf16)
    joined = joined.transpose(1, 0, 2, 3).reshape(hb, n_rest, n_head, w_rows, group + 128).transpose(1, 0, 2, 3, 4)
    joined = reduce_axis(joined, "rest").astype(bf16).reshape(n_u, n_v, n_head, w_rows, group + 128)
    joined = reduce_axis(joined, "u").astype(bf16)
    joined = reduce_axis(joined, "v").astype(bf16)
    joined = exchange_axis(joined, "head").astype(f32)
    in_weight_grad = joined[:, :, :group].reshape(n_head, w_rows, hb, 3, HEAD_DIM).transpose(1, 3, 0, 2, 4)
    in_weight_grad = in_weight_grad.reshape(w_rows, 3 * width)
    extra = jnp.sum(joined[:, :, group : group + 4], axis=0)
    return (
        output,
        tokens_grad,
        extra[:, 0],
        extra[:, 1],
        in_weight_grad,
        extra[:, 2],
        extra[:, 3],
        out_weight_grad,
        out_bias_grad,
        post_gain_grad,
        post_shift_grad,
        up_weight_grad,
        up_bias_grad,
        down_weight_grad,
        down_bias_grad,
    )


def solution(mesh):
    n_head, n_blk = mesh.shape["head"], mesh.shape["blk"]
    hb = HEADS // n_head
    n_u = 2 if hb % 2 == 0 else 1
    fine = Mesh(mesh.devices.reshape(n_head, n_u, hb // n_u, n_blk // hb), ALL)
    tok = P(("u", "v", "rest", "head"), None)
    vec = P(ALL)
    mat = P(ALL, None)
    return jax.shard_map(
        on_device,
        mesh=fine,
        in_specs=(tok, tok, P(), vec, vec, mat, vec, vec, mat, vec, vec, vec, mat, vec, mat, vec),
        out_specs=(tok, tok, vec, vec, mat, vec, vec, mat, vec, vec, vec, mat, vec, mat, vec),
        check_vma=False,
    )
```

```python
import functools

import jax
import jax.numpy as jnp
from jax import lax
from jax.experimental import pallas as pl
from jax.experimental.pallas import tpu as pltpu
from jax.sharding import Mesh
from jax.sharding import PartitionSpec as P

HEADS = 16
HEAD_DIM = 64
DOCS = 4
BLOCK_Q = 512
BLOCK_K = 512
VMEM_BYTES = 56 * 1024 * 1024

EPS = 1e-05
NEGATIVE = -1e30
GELU_C = 0.7978845608028654
SCALE = HEAD_DIM ** (-0.5)
ALL = ("head", "u", "v", "rest")
f32 = jnp.float32
bf16 = jnp.bfloat16


def norm_forward(rows, gain, shift):
    center = rows - jnp.mean(rows, axis=-1, keepdims=True)
    var = jnp.mean(center * center, axis=-1, keepdims=True)
    inverse = lax.rsqrt(var + EPS)
    unit = center * inverse
    return (unit * gain + shift, unit, inverse)


def norm_inner(grad, unit, inverse, gain):
    scaled = grad * gain
    inner = (
        scaled
        - jnp.mean(scaled, axis=-1, keepdims=True)
        - unit * jnp.mean(scaled * unit, axis=-1, keepdims=True)
    )
    return inverse * inner


def gelu_parts(pre):
    cubic = pre * pre * pre
    tangent = jnp.tanh(GELU_C * (pre + 0.044715 * cubic))
    value = 0.5 * pre * (1.0 + tangent)
    slope = 0.5 * (1.0 + tangent) + 0.5 * pre * (1.0 - tangent * tangent) * GELU_C * (
        1.0 + 3.0 * 0.044715 * pre * pre
    )
    return (value, slope)


def shifted(x, axis, k):
    n = lax.axis_size(axis)
    return lax.ppermute(x, axis, [(i, (i + k) % n) for i in range(n)])


def put(buffer, x, index):
    return lax.dynamic_update_index_in_dim(buffer, x, index, 0)


def gather_axis(x, axis):
    n = lax.axis_size(axis)
    if n == 1:
        return x[None]
    me = lax.axis_index(axis)
    out = put(jnp.zeros((n,) + x.shape, x.dtype), x, me)
    for k in range(1, n):
        out = put(out, shifted(x, axis, k), (me - k) % n)
    return out


def reduce_begin(x, axis, dim=0):
    n = lax.axis_size(axis)
    if n == 1:
        return [lax.index_in_dim(x, 0, dim, keepdims=False)]
    me = lax.axis_index(axis)
    pieces = [lax.dynamic_index_in_dim(x, (me + k) % n, dim, keepdims=False) for k in range(n)]
    return pieces[:1] + [shifted(pieces[k], axis, k) for k in range(1, n)]


def reduce_end(pieces):
    total = pieces[0].astype(f32)
    for piece in pieces[1:]:
        total = total + piece.astype(f32)
    return total


def reduce_axis(x, axis, dim=0):
    return reduce_end(reduce_begin(x, axis, dim))


def exchange_axis(x, axis):
    n = lax.axis_size(axis)
    if n == 1:
        return x
    me = lax.axis_index(axis)
    mine = lax.dynamic_index_in_dim(x, me, 0, keepdims=False)
    out = put(jnp.zeros_like(x), mine, me)
    for k in range(1, n):
        piece = lax.dynamic_index_in_dim(x, (me + k) % n, 0, keepdims=False)
        out = put(out, shifted(piece, axis, k), (me - k) % n)
    return out


def allowed_keys(kb, starts, pos):
    t = kb * BLOCK_K + lax.broadcasted_iota(jnp.int32, (BLOCK_K, BLOCK_Q), 0)
    return (t >= starts) & (t <= pos)


def lay_rows(me, own_ref, far_ref, rows_ref, cols_ref, first):
    hb, _, block_rows = own_ref.shape
    n_rest = far_ref.shape[0] + 1
    subs = block_rows // BLOCK_K

    def lay(read, b, rest):
        for sub in range(subs):
            kb = (b * n_rest + rest) * subs + sub
            block = read(b)[:, sub * BLOCK_K : (sub + 1) * BLOCK_K]
            rows_ref[pl.ds(pl.multiple_of(kb * BLOCK_K, BLOCK_K), BLOCK_K), :] = block[HEAD_DIM:].T
            cols_ref[kb] = block[first : first + HEAD_DIM]

    def each(b, _):
        lay(lambda b: own_ref[b], b, me)
        for k in range(1, n_rest):
            lay(lambda b: far_ref[k - 1, b], b, (me - k) % n_rest)
        return 0

    lax.fori_loop(0, hb, each, 0)


def forward_kernel(
    lo_ref, mid_ref, q0_ref, me_ref, q_ref, own_ref, far_ref, start_ref, o_ref, wide_ref, lse_ref, rows_ref, cols_ref
):
    step = pl.program_id(0)

    @pl.when(step == 0)
    def _():
        lay_rows(me_ref[0], own_ref, far_ref, rows_ref, cols_ref, 2 * HEAD_DIM)

    first = q0_ref[step]
    q = q_ref[0] * jnp.asarray(SCALE, bf16)
    q_pad = jnp.concatenate([q, jnp.zeros_like(q)], axis=0)
    starts = start_ref[0]
    pos = first + lax.broadcasted_iota(jnp.int32, (1, BLOCK_Q), 1)

    def body(masked, kb, carry):
        top, total, acc = carry
        rows = rows_ref[pl.ds(pl.multiple_of(kb * BLOCK_K, BLOCK_K), BLOCK_K), :]
        s = jnp.dot(rows, q_pad, preferred_element_type=f32)
        if masked:
            s = jnp.where(allowed_keys(kb, starts, pos), s, NEGATIVE)
        new_top = jnp.maximum(top, jnp.max(s, axis=0, keepdims=True))
        p = jnp.exp(s - new_top)
        factor = jnp.exp(top - new_top)
        values = cols_ref[kb]
        acc = acc * factor + jnp.dot(values, p.astype(bf16), preferred_element_type=f32)
        return (new_top, total * factor + jnp.sum(p, axis=0, keepdims=True), acc)

    diagonal = first // BLOCK_K
    mid = jnp.minimum(mid_ref[step], diagonal)
    carry = (
        jnp.full((1, BLOCK_Q), NEGATIVE, f32),
        jnp.zeros((1, BLOCK_Q), f32),
        jnp.zeros((HEAD_DIM, BLOCK_Q), f32),
    )
    carry = lax.fori_loop(lo_ref[step], mid, functools.partial(body, True), carry)
    carry = lax.fori_loop(mid, diagonal, functools.partial(body, False), carry)
    last = (first + BLOCK_Q + BLOCK_K - 1) // BLOCK_K
    top, total, acc = lax.fori_loop(diagonal, last, functools.partial(body, True), carry)
    out = acc / total
    wide_ref[0] = out
    lse_ref[0] = top + jnp.log(total)
    low = out.astype(bf16)
    piece = o_ref.shape[3]
    for i in range(o_ref.shape[0]):
        o_ref[i, 0] = low[:, i * piece : (i + 1) * piece]


def backward_kernel(
    n_steps,
    lo_ref,
    mid_ref,
    q0_ref,
    me_ref,
    q_ref,
    own_ref,
    far_ref,
    start_ref,
    do_ref,
    wide_ref,
    lse_ref,
    dq_ref,
    dkv_ref,
    rows_ref,
    cols_ref,
    acc_ref,
):
    step = pl.program_id(0)

    @pl.when(step == 0)
    def _():
        lay_rows(me_ref[0], own_ref, far_ref, rows_ref, cols_ref, HEAD_DIM)
        acc_ref[...] = jnp.zeros_like(acc_ref)

    @pl.when(step < n_steps)
    def _():
        first = q0_ref[step]
        q = q_ref[0] * jnp.asarray(SCALE, bf16)
        do = jnp.concatenate([do_ref[i, 0] for i in range(do_ref.shape[0])], axis=1)
        zero = jnp.zeros_like(q)
        q_pad = jnp.concatenate([q, zero], axis=0)
        do_pad = jnp.concatenate([zero, do], axis=0)
        q_rows = q_pad.T
        do_rows = do_pad.T
        starts = start_ref[0]
        lse = lse_ref[0]
        delta = jnp.sum(do.astype(f32) * wide_ref[0], axis=0, keepdims=True)
        pos = first + lax.broadcasted_iota(jnp.int32, (1, BLOCK_Q), 1)

        def body(masked, kb, dq):
            at = pl.ds(pl.multiple_of(kb * BLOCK_K, BLOCK_K), BLOCK_K)
            rows = rows_ref[at, :]
            s = jnp.dot(rows, q_pad, preferred_element_type=f32)
            p = jnp.exp(s - lse)
            if masked:
                p = jnp.where(allowed_keys(kb, starts, pos), p, 0.0)
            dp = jnp.dot(rows, do_pad, preferred_element_type=f32)
            ds = (p * (dp - delta)).astype(bf16)
            acc_ref[at, :] += jnp.dot(p.astype(bf16), do_rows, preferred_element_type=f32) + jnp.dot(
                ds, q_rows, preferred_element_type=f32
            )
            return dq + jnp.dot(cols_ref[kb], ds, preferred_element_type=f32)

        diagonal = first // BLOCK_K
        mid = jnp.minimum(mid_ref[step], diagonal)
        dq = jnp.zeros((HEAD_DIM, BLOCK_Q), f32)
        dq = lax.fori_loop(lo_ref[step], mid, functools.partial(body, True), dq)
        dq = lax.fori_loop(mid, diagonal, functools.partial(body, False), dq)
        last = (first + BLOCK_Q + BLOCK_K - 1) // BLOCK_K
        dq = lax.fori_loop(diagonal, last, functools.partial(body, True), dq)
        dq_ref[0] = (dq * SCALE).astype(bf16)

    @pl.when(step >= n_steps)
    def _():
        kb = jnp.maximum(step - n_steps, 0)
        at = pl.ds(pl.multiple_of(kb * BLOCK_K, BLOCK_K), BLOCK_K)
        dkv_ref[0, 0] = acc_ref[at, :].astype(bf16).T


def attention_specs(qkv, far, tok_rows):
    hb, depth, block_rows = qkv.shape
    subs = block_rows // BLOCK_Q
    pieces = BLOCK_Q // tok_rows

    def wrap(index):
        return lambda i, *_: index(i)

    q_spec = lambda cap: pl.BlockSpec((1, HEAD_DIM, BLOCK_Q), wrap(lambda i: (cap(i) // subs, 0, cap(i) % subs)))
    row_spec = lambda cap: pl.BlockSpec((1, 1, BLOCK_Q), wrap(lambda i: (cap(i) // subs, 0, cap(i) % subs)))
    piece_spec = lambda cap: pl.BlockSpec(
        (pieces, 1, HEAD_DIM, tok_rows), wrap(lambda i: (cap(i) % subs, cap(i) // subs, 0, 0))
    )
    own_spec = pl.BlockSpec((hb, depth, block_rows), wrap(lambda i: (0, 0, 0)), pipeline_mode=pl.Buffered(1))
    far_spec = pl.BlockSpec(far.shape, wrap(lambda i: (0, 0, 0, 0)), pipeline_mode=pl.Buffered(1))
    return q_spec, row_spec, piece_spec, own_spec, far_spec


def padded_cost(products, queries, keys):
    pairs = queries * keys // 2
    return pl.CostEstimate(flops=products * 2 * 256 * pairs, transcendentals=pairs, bytes_accessed=8 * keys * HEAD_DIM)


def attention_forward(bounds, qkv, far, starts, n_head, tok_rows):
    hb, _, block_rows = qkv.shape
    queries = hb * block_rows
    keys = queries * (far.shape[0] + 1)
    q_spec, row_spec, piece_spec, own_spec, far_spec = attention_specs(qkv, far, tok_rows)
    same = lambda i: i
    return pl.pallas_call(
        forward_kernel,
        grid_spec=pltpu.PrefetchScalarGridSpec(
            num_scalar_prefetch=4,
            grid=(queries // BLOCK_Q,),
            in_specs=[q_spec(same), own_spec, far_spec, row_spec(same)],
            out_specs=[piece_spec(same), q_spec(same), row_spec(same)],
            scratch_shapes=[
                pltpu.VMEM((keys, 2 * HEAD_DIM), bf16),
                pltpu.VMEM((keys // BLOCK_K, HEAD_DIM, BLOCK_K), bf16),
            ],
        ),
        out_shape=[
            jax.ShapeDtypeStruct((n_head, hb, HEAD_DIM, tok_rows), bf16),
            jax.ShapeDtypeStruct((hb, HEAD_DIM, block_rows), f32),
            jax.ShapeDtypeStruct((hb, 1, block_rows), f32),
        ],
        compiler_params=pltpu.CompilerParams(vmem_limit_bytes=VMEM_BYTES),
        cost_estimate=padded_cost(2, queries, keys),
        name="attention_forward",
    )(*bounds, qkv, qkv, far, starts)


def attention_backward(bounds, qkv, far, starts, do, wide, lse):
    hb, _, block_rows = qkv.shape
    n_rest = far.shape[0] + 1
    queries = hb * block_rows
    keys = queries * n_rest
    n_kb = keys // BLOCK_K
    subs = block_rows // BLOCK_K
    n_steps = queries // BLOCK_Q
    q_spec, row_spec, piece_spec, own_spec, far_spec = attention_specs(qkv, far, do.shape[3])
    cap = lambda i: jnp.minimum(i, n_steps - 1)

    def place(i, *_):
        kb = jnp.maximum(i - n_steps, 0)
        return (kb // subs % n_rest, kb // subs // n_rest, 0, kb % subs)

    return pl.pallas_call(
        functools.partial(backward_kernel, n_steps),
        grid_spec=pltpu.PrefetchScalarGridSpec(
            num_scalar_prefetch=4,
            grid=(n_steps + n_kb,),
            in_specs=[q_spec(cap), own_spec, far_spec, row_spec(cap), piece_spec(cap), q_spec(cap), row_spec(cap)],
            out_specs=[q_spec(cap), pl.BlockSpec((1, 1, 2 * HEAD_DIM, BLOCK_K), place)],
            scratch_shapes=[
                pltpu.VMEM((keys, 2 * HEAD_DIM), bf16),
                pltpu.VMEM((n_kb, HEAD_DIM, BLOCK_K), bf16),
                pltpu.VMEM((keys, 2 * HEAD_DIM), f32),
            ],
        ),
        out_shape=[
            jax.ShapeDtypeStruct((hb, HEAD_DIM, block_rows), bf16),
            jax.ShapeDtypeStruct((n_rest, hb, 2 * HEAD_DIM, block_rows), bf16),
        ],
        compiler_params=pltpu.CompilerParams(vmem_limit_bytes=VMEM_BYTES),
        cost_estimate=padded_cost(5, queries, keys),
        name="attention_backward",
    )(*bounds, qkv, qkv, far, starts, do, wide, lse)


def on_device(
    tokens,
    cotangent,
    segment,
    norm_gain,
    norm_shift,
    in_weight,
    query_bias,
    value_bias,
    out_weight,
    out_bias,
    post_gain,
    post_shift,
    up_weight,
    up_bias,
    down_weight,
    down_bias,
):
    n_head, n_u, n_v, n_rest = (lax.axis_size(a) for a in ALL)
    hb = n_u * n_v
    n_blk = hb * n_rest
    n_all = n_head * n_blk
    me_head, me_u, me_v, me_rest = (lax.axis_index(a) for a in ALL)
    me_blk = (me_u * n_v + me_v) * n_rest + me_rest
    tok_rows, width = tokens.shape
    block_rows = tok_rows * n_head
    length = segment.shape[0]
    w_rows = in_weight.shape[0]
    group = 3 * hb * HEAD_DIM

    chips = n_head * hb
    f_rows = down_weight.shape[0] // 2

    units = up_weight.reshape(w_rows, n_head, n_u, n_v, n_rest, 2, f_rows)
    up_cols = jnp.concatenate(
        [
            units[..., 0, :].transpose(4, 0, 3, 2, 1, 5).reshape(n_rest, w_rows, -1),
            units[..., 1, :].transpose(4, 0, 2, 3, 1, 5).reshape(n_rest, w_rows, -1),
        ],
        axis=2,
    )
    f_half = chips * f_rows
    up_cols = exchange_axis(up_cols, "rest").reshape(n_rest * w_rows, 2 * f_half)
    out_rows = gather_axis(out_weight, "rest").reshape(n_rest * w_rows, width)
    joint = jnp.concatenate([up_cols, out_rows], axis=1)
    joint = lax.all_gather(joint, ("head", "u", "v"), axis=0, tiled=True)
    w_up = joint[:, : 2 * f_half]
    w_out = joint[:, 2 * f_half :]

    n_up = up_bias.shape[0] // w_rows
    vectors = [norm_gain, norm_shift, query_bias, value_bias, out_bias, post_gain, post_shift, down_bias]
    vectors = jnp.concatenate([jnp.stack(vectors), up_bias.reshape(n_up, w_rows)]).T
    vectors = jnp.pad(vectors, ((0, 0), (0, 128 - vectors.shape[1])))
    cols = in_weight.reshape(w_rows, 3, n_head, hb, HEAD_DIM).transpose(2, 0, 3, 1, 4).reshape(n_head, w_rows, group)
    cols = jnp.concatenate([cols, jnp.broadcast_to(vectors, (n_head, w_rows, 128))], axis=2)
    cols = exchange_axis(cols, "head")
    for axis in ("v", "u", "rest"):
        cols = gather_axis(cols, axis)
    cols = cols.transpose(3, 1, 2, 0, 4, 5).reshape(width, group + 128)
    w_in = cols[:, :group]
    vectors = cols[:, group : group + 8 + n_up].T.astype(f32)
    gain_a, shift_a, bias_q, bias_v, bias_out, gain_b, shift_b, bias_down = (vectors[i] for i in range(8))
    bias_up = vectors[8:].reshape(n_up, n_all, w_rows).transpose(1, 0, 2)

    rows_all = gather_axis(tokens, "head").reshape(block_rows, width)

    rows_all, down_weight = lax.optimization_barrier((rows_all, down_weight))
    rows_all = rows_all.astype(f32)
    down_rows = down_weight.reshape(2, f_rows, width)
    w_down = [gather_axis(down_rows[i], "head") for i in range(2)]
    w_down = [gather_axis(w_down[0], "u"), gather_axis(w_down[1], "v")]
    w_down = [gather_axis(w_down[0], "v"), gather_axis(w_down[1], "u")]
    w_down = [w.reshape(f_half, width) for w in w_down]

    normed, unit_all, inverse_all = norm_forward(rows_all, gain_a, shift_a)
    normed_low = normed.astype(bf16)
    group_bias = jnp.stack([bias_q, jnp.zeros_like(bias_q), bias_v]).reshape(3, n_head, hb, HEAD_DIM)
    group_bias = lax.dynamic_index_in_dim(group_bias, me_head, 1, keepdims=False).transpose(1, 0, 2).reshape(group, 1)
    projected = lax.dot_general(w_in, normed_low, (((0,), (1,)), ((), ())), preferred_element_type=f32)
    projected = (projected + group_bias).astype(bf16)
    qkv = lax.all_to_all(
        projected.reshape(hb, 3 * HEAD_DIM, block_rows), ("u", "v"), split_axis=0, concat_axis=0, tiled=True
    )
    far = [shifted(qkv, "rest", k) for k in range(1, n_rest)]
    far = jnp.stack(far) if n_rest > 2 else far[0][None]

    doc_start = jnp.zeros_like(segment)
    for doc in range(1, DOCS):
        first = jnp.sum((segment < doc).astype(jnp.int32))
        doc_start = jnp.where(segment == doc, first, doc_start)
    starts = lax.dynamic_index_in_dim(doc_start.reshape(hb, n_rest, block_rows), me_rest, 1, keepdims=False)
    starts_q = starts.reshape(-1, BLOCK_Q)
    lo = starts_q[:, 0] // BLOCK_K
    mid = (starts_q[:, -1] + BLOCK_K - 1) // BLOCK_K
    q_first = (jnp.arange(hb, dtype=jnp.int32)[:, None] * n_rest + me_rest) * block_rows
    q_first = (q_first + jnp.arange(block_rows // BLOCK_Q, dtype=jnp.int32)[None] * BLOCK_Q).reshape(-1)
    bounds = (lo, mid, q_first, me_rest.astype(jnp.int32).reshape(1))
    starts = starts.reshape(hb, 1, block_rows)

    attended, wide, lse = attention_forward(bounds, qkv, far, starts, n_head, tok_rows)
    back = lax.all_to_all(
        attended.reshape(HEADS, HEAD_DIM, tok_rows), ("head", "u", "v"), split_axis=0, concat_axis=0, tiled=True
    ).reshape(width, tok_rows)

    rows = tokens.astype(f32)
    branch = lax.dot_general(back, w_out, (((0,), (0,)), ((), ())), preferred_element_type=f32) + bias_out
    middle = rows + branch
    hidden_in, unit_mid, inverse_mid = norm_forward(middle, gain_b, shift_b)
    hidden_low = hidden_in.astype(bf16)
    hidden_all = gather_axis(hidden_low, "rest").reshape(n_rest * tok_rows, width)
    cot_all = gather_axis(cotangent, "rest").reshape(n_rest * tok_rows, width)
    bias_units = bias_up.reshape(n_head, n_u, n_v, n_rest, 2, f_rows)
    bias_units = lax.dynamic_index_in_dim(bias_units, me_rest, 3, keepdims=False)
    bias_units = jnp.concatenate(
        [bias_units[..., 0, :].transpose(2, 1, 0, 3).reshape(-1), bias_units[..., 1, :].transpose(1, 2, 0, 3).reshape(-1)]
    )
    pre = jnp.dot(hidden_all, w_up, preferred_element_type=f32) + bias_units
    act, slope = gelu_parts(pre)
    act_low = act.astype(bf16)
    acts = act_low[:, :f_half], act_low[:, f_half:]
    down = jnp.dot(acts[0], w_down[0], preferred_element_type=f32)
    down = down + jnp.dot(acts[1], w_down[1], preferred_element_type=f32)
    down = reduce_axis(down.reshape(n_rest, tok_rows, width), "rest")
    output = (middle + down + bias_down).astype(bf16)
    grad_out = cotangent.astype(f32)
    grad_act = jnp.concatenate(
        [jnp.einsum("td,fd->tf", cot_all, w, preferred_element_type=f32) for w in w_down], axis=1
    )
    grad_pre = (grad_act * slope).astype(bf16)
    grad_hidden = jnp.einsum("tf,df->td", grad_pre, w_up, preferred_element_type=f32)
    grad_hidden = reduce_axis(grad_hidden.reshape(n_rest, tok_rows, width), "rest")
    grad_middle = grad_out + norm_inner(grad_hidden, unit_mid, inverse_mid, gain_b)
    grad_branch = grad_middle.astype(bf16)
    grad_back = lax.dot_general(w_out, grad_branch, (((1,), (1,)), ((), ())), preferred_element_type=f32).astype(bf16)
    grad_heads = lax.all_to_all(
        grad_back.reshape(HEADS, HEAD_DIM, tok_rows), ("head", "u", "v"), split_axis=0, concat_axis=0, tiled=True
    ).reshape(n_head, hb, HEAD_DIM, tok_rows)

    down_grads = [jnp.einsum("tf,td->fd", a, cot_all, preferred_element_type=f32).astype(bf16) for a in acts]
    up_grad = jnp.einsum("td,tf->df", hidden_all, grad_pre, preferred_element_type=f32).astype(bf16)
    out_grad = jnp.einsum("dt,te->de", back, grad_branch, preferred_element_type=f32).astype(bf16)
    out_grad = out_grad.reshape(chips, n_rest, w_rows, width).transpose(1, 0, 2, 3)
    out_grad = reduce_axis(out_grad, "rest").astype(bf16)
    up_grad = up_grad.reshape(n_head, n_u, n_v, -1, 2 * f_half)
    out_grad = out_grad.reshape(n_head, n_u, n_v, -1, width)
    down_a = down_grads[0].reshape(n_v, n_u, n_head, f_rows, width)
    down_b = down_grads[1].reshape(n_u, n_v, n_head, f_rows, width)
    sums = [
        jnp.sum(grad_branch.astype(f32), axis=0),
        jnp.sum(grad_hidden * unit_mid, axis=0),
        jnp.sum(grad_hidden, axis=0),
        jnp.sum(grad_out, axis=0),
    ]
    unit_sum = jnp.sum(grad_pre.astype(f32), axis=0)
    unit_sum = jnp.stack(
        [
            unit_sum[:f_half].reshape(n_v, n_u, n_head, f_rows).transpose(2, 1, 0, 3),
            unit_sum[f_half:].reshape(n_u, n_v, n_head, f_rows).transpose(2, 0, 1, 3),
        ],
        axis=3,
    ).reshape(chips, 1, 2 * f_rows)
    unit_sum = jnp.where((jnp.arange(n_rest) == me_rest)[:, None], unit_sum, 0.0).reshape(n_head, n_blk, n_up, w_rows)

    grad_heads, up_grad, down_a, out_grad, down_b = lax.optimization_barrier(
        (grad_heads, up_grad, down_a, out_grad, down_b)
    )
    begun = [reduce_begin(up_grad, "u", 1), reduce_begin(down_a, "v"), reduce_begin(out_grad, "v", 2)]
    begun.append(reduce_begin(down_b, "head", 2))

    dq, dkv = attention_backward(bounds, qkv, far, starts, grad_heads, wide, lse)
    dq, dkv, begun = lax.optimization_barrier((dq, dkv, begun))
    up_grad, down_a, out_grad, down_b = (reduce_end(x).astype(bf16) for x in begun)
    dkv = reduce_axis(dkv, "rest").astype(bf16)
    grad_proj = lax.all_to_all(
        jnp.concatenate([dq, dkv], axis=1), ("u", "v"), split_axis=0, concat_axis=0, tiled=True
    ).reshape(group, block_rows)

    grad_normed = lax.dot_general(grad_proj, w_in, (((0,), (1,)), ((), ())), preferred_element_type=f32)
    tokens_low = grad_normed.astype(bf16).reshape(n_head, tok_rows, width)
    tokens_low, grad_proj, up_grad, down_a, out_grad, down_b = lax.optimization_barrier(
        (tokens_low, grad_proj, up_grad, down_a, out_grad, down_b)
    )
    begun = reduce_begin(tokens_low, "head")

    in_grad = lax.dot_general(normed_low, grad_proj, (((0,), (1,)), ((), ())), preferred_element_type=f32)
    rowed = lambda x: x.reshape(n_head, n_blk, w_rows)
    gain_grad = rowed(jnp.sum(grad_normed * unit_all, axis=0))
    shift_grad = rowed(jnp.sum(grad_normed, axis=0))
    col_sum = jnp.sum(grad_proj.astype(f32), axis=1).reshape(hb, 3, HEAD_DIM)
    mine = (jnp.arange(n_head) == me_head)[:, None, None]
    query_sum = jnp.where(mine, col_sum[:, 0].reshape(1, n_blk, w_rows), 0.0)
    value_sum = jnp.where(mine, col_sum[:, 2].reshape(1, n_blk, w_rows), 0.0)
    extra = jnp.stack([gain_grad, shift_grad, query_sum, value_sum, *(rowed(x) for x in sums)], axis=2)
    extra = jnp.concatenate([extra, unit_sum], axis=2)
    n_extra = extra.shape[2]
    extra = jnp.pad(extra.transpose(0, 1, 3, 2), ((0, 0), (0, 0), (0, 0), (0, 128 - n_extra)))
    joined = jnp.concatenate([in_grad.reshape(n_head, n_blk, w_rows, group), extra], axis=-1).astype(bf16)
    joined = joined.reshape(n_head, n_u, n_v, n_rest, w_rows, group + 128)
    joined = reduce_axis(joined, "rest", 3).astype(bf16)
    joined = reduce_axis(joined, "u", 1).astype(bf16)
    joined = reduce_axis(joined, "v", 1).astype(bf16)

    up_grad = reduce_axis(up_grad, "v", 1).astype(bf16)
    down_a = reduce_axis(down_a, "u").astype(bf16)
    out_grad = reduce_axis(out_grad, "u", 1).astype(bf16)
    down_b = reduce_axis(down_b, "u").astype(bf16)

    begun, joined, up_grad, down_a, out_grad, down_b = lax.optimization_barrier(
        (begun, joined, up_grad, down_a, out_grad, down_b)
    )
    up_grad = reduce_axis(up_grad, "head").astype(bf16).reshape(n_rest, w_rows, 2 * f_half)
    down_a, out_weight_grad = (reduce_axis(x, "head") for x in (down_a, out_grad))
    down_b = reduce_axis(down_b, "v")
    down_weight_grad = jnp.concatenate([down_a, down_b], axis=0)
    up_grad = exchange_axis(up_grad, "rest").astype(f32)
    up_weight_grad = jnp.stack(
        [
            up_grad[..., :f_half].reshape(n_rest, w_rows, n_v, n_u, n_head, f_rows).transpose(1, 4, 3, 2, 0, 5),
            up_grad[..., f_half:].reshape(n_rest, w_rows, n_u, n_v, n_head, f_rows).transpose(1, 4, 2, 3, 0, 5),
        ],
        axis=5,
    ).reshape(w_rows, -1)
    joined = exchange_axis(joined, "head").astype(f32)
    in_weight_grad = joined[:, :, :group].reshape(n_head, w_rows, hb, 3, HEAD_DIM).transpose(1, 3, 0, 2, 4)
    in_weight_grad = in_weight_grad.reshape(w_rows, 3 * width)
    extra = jnp.sum(joined[:, :, group : group + n_extra], axis=0).T
    norm_gain_grad, norm_shift_grad, query_bias_grad, value_bias_grad = (extra[i] for i in range(4))
    out_bias_grad, post_gain_grad, post_shift_grad, down_bias_grad = (extra[i] for i in range(4, 8))
    up_bias_grad = extra[8:].reshape(-1)

    grad_tokens = reduce_end(begun)
    unit_in = lax.dynamic_index_in_dim(unit_all.reshape(n_head, tok_rows, width), me_head, 0, keepdims=False)
    inverse_in = lax.dynamic_index_in_dim(inverse_all.reshape(n_head, tok_rows, 1), me_head, 0, keepdims=False)
    tokens_grad = (grad_middle + norm_inner(grad_tokens, unit_in, inverse_in, gain_a)).astype(bf16)
    return (
        output,
        tokens_grad,
        norm_gain_grad,
        norm_shift_grad,
        in_weight_grad,
        query_bias_grad,
        value_bias_grad,
        out_weight_grad,
        out_bias_grad,
        post_gain_grad,
        post_shift_grad,
        up_weight_grad,
        up_bias_grad,
        down_weight_grad,
        down_bias_grad,
    )


def solution(mesh):
    n_head, n_blk = mesh.shape["head"], mesh.shape["blk"]
    hb = HEADS // n_head
    n_u = 2 if hb % 2 == 0 else 1
    fine = Mesh(mesh.devices.reshape(n_head, n_u, hb // n_u, n_blk // hb), ALL)
    tok = P(("u", "v", "rest", "head"), None)
    vec = P(ALL)
    mat = P(ALL, None)
    return jax.shard_map(
        on_device,
        mesh=fine,
        in_specs=(tok, tok, P(), vec, vec, mat, vec, vec, mat, vec, vec, vec, mat, vec, mat, vec),
        out_specs=(tok, tok, vec, vec, mat, vec, vec, mat, vec, vec, vec, mat, vec, mat, vec),
        check_vma=False,
    )
```

```python
import functools

import jax
import jax.numpy as jnp
from jax import lax
from jax.experimental import pallas as pl
from jax.experimental.pallas import tpu as pltpu
from jax.sharding import Mesh
from jax.sharding import PartitionSpec as P

HEADS = 16
HEAD_DIM = 64
DOCS = 4
BLOCK_Q = 512
BLOCK_K = 512
VMEM_BYTES = 56 * 1024 * 1024

EPS = 1e-05
NEGATIVE = -1e30
GELU_C = 0.7978845608028654
SCALE = HEAD_DIM ** (-0.5)
ALL = ("head", "u", "v", "rest")
f32 = jnp.float32
bf16 = jnp.bfloat16


def norm_forward(rows, gain, shift):
    center = rows - jnp.mean(rows, axis=-1, keepdims=True)
    var = jnp.mean(center * center, axis=-1, keepdims=True)
    inverse = lax.rsqrt(var + EPS)
    unit = center * inverse
    return (unit * gain + shift, unit, inverse)


def norm_inner(grad, unit, inverse, gain):
    scaled = grad * gain
    inner = (
        scaled
        - jnp.mean(scaled, axis=-1, keepdims=True)
        - unit * jnp.mean(scaled * unit, axis=-1, keepdims=True)
    )
    return inverse * inner


def gelu_parts(pre):
    cubic = pre * pre * pre
    tangent = jnp.tanh(GELU_C * (pre + 0.044715 * cubic))
    value = 0.5 * pre * (1.0 + tangent)
    slope = 0.5 * (1.0 + tangent) + 0.5 * pre * (1.0 - tangent * tangent) * GELU_C * (
        1.0 + 3.0 * 0.044715 * pre * pre
    )
    return (value, slope)


def shifted(x, axis, k):
    n = lax.axis_size(axis)
    return lax.ppermute(x, axis, [(i, (i + k) % n) for i in range(n)])


def put(buffer, x, index):
    return lax.dynamic_update_index_in_dim(buffer, x, index, 0)


def gather_axis(x, axis):
    n = lax.axis_size(axis)
    if n == 1:
        return x[None]
    me = lax.axis_index(axis)
    out = put(jnp.zeros((n,) + x.shape, x.dtype), x, me)
    for k in range(1, n):
        out = put(out, shifted(x, axis, k), (me - k) % n)
    return out


def reduce_begin(x, axis, dim=0):
    n = lax.axis_size(axis)
    if n == 1:
        return [lax.index_in_dim(x, 0, dim, keepdims=False)]
    me = lax.axis_index(axis)
    pieces = [lax.dynamic_index_in_dim(x, (me + k) % n, dim, keepdims=False) for k in range(n)]
    return pieces[:1] + [shifted(pieces[k], axis, k) for k in range(1, n)]


def reduce_end(pieces):
    total = pieces[0].astype(f32)
    for piece in pieces[1:]:
        total = total + piece.astype(f32)
    return total


def reduce_axis(x, axis, dim=0):
    return reduce_end(reduce_begin(x, axis, dim))


def exchange_axis(x, axis):
    n = lax.axis_size(axis)
    if n == 1:
        return x
    me = lax.axis_index(axis)
    mine = lax.dynamic_index_in_dim(x, me, 0, keepdims=False)
    out = put(jnp.zeros_like(x), mine, me)
    for k in range(1, n):
        piece = lax.dynamic_index_in_dim(x, (me + k) % n, 0, keepdims=False)
        out = put(out, shifted(piece, axis, k), (me - k) % n)
    return out


def allowed_keys(kb, starts, pos):
    t = kb * BLOCK_K + lax.broadcasted_iota(jnp.int32, (BLOCK_K, BLOCK_Q), 0)
    return (t >= starts) & (t <= pos)


def lay_rows(me, own_ref, far_ref, rows_ref, cols_ref, first):
    hb, _, block_rows = own_ref.shape
    n_rest = far_ref.shape[0] + 1
    subs = block_rows // BLOCK_K

    def lay(read, b, rest):
        for sub in range(subs):
            kb = (b * n_rest + rest) * subs + sub
            block = read(b)[:, sub * BLOCK_K : (sub + 1) * BLOCK_K]
            rows_ref[pl.ds(pl.multiple_of(kb * BLOCK_K, BLOCK_K), BLOCK_K), :] = block[HEAD_DIM:].T
            cols_ref[kb] = block[first : first + HEAD_DIM]

    def each(b, _):
        lay(lambda b: own_ref[b], b, me)
        for k in range(1, n_rest):
            lay(lambda b: far_ref[k - 1, b], b, (me - k) % n_rest)
        return 0

    lax.fori_loop(0, hb, each, 0)


def forward_kernel(
    lo_ref, mid_ref, q0_ref, me_ref, q_ref, own_ref, far_ref, start_ref, o_ref, wide_ref, lse_ref, rows_ref, cols_ref
):
    step = pl.program_id(0)

    @pl.when(step == 0)
    def _():
        lay_rows(me_ref[0], own_ref, far_ref, rows_ref, cols_ref, 2 * HEAD_DIM)

    first = q0_ref[step]
    q = q_ref[0] * jnp.asarray(SCALE, bf16)
    q_pad = jnp.concatenate([q, jnp.zeros_like(q)], axis=0)
    starts = start_ref[0]
    pos = first + lax.broadcasted_iota(jnp.int32, (1, BLOCK_Q), 1)

    def body(masked, kb, carry):
        top, total, acc = carry
        rows = rows_ref[pl.ds(pl.multiple_of(kb * BLOCK_K, BLOCK_K), BLOCK_K), :]
        s = jnp.dot(rows, q_pad, preferred_element_type=f32)
        if masked:
            s = jnp.where(allowed_keys(kb, starts, pos), s, NEGATIVE)
        new_top = jnp.maximum(top, jnp.max(s, axis=0, keepdims=True))
        p = jnp.exp(s - new_top)
        factor = jnp.exp(top - new_top)
        values = cols_ref[kb]
        acc = acc * factor + jnp.dot(values, p.astype(bf16), preferred_element_type=f32)
        return (new_top, total * factor + jnp.sum(p, axis=0, keepdims=True), acc)

    diagonal = first // BLOCK_K
    mid = jnp.minimum(mid_ref[step], diagonal)
    carry = (
        jnp.full((1, BLOCK_Q), NEGATIVE, f32),
        jnp.zeros((1, BLOCK_Q), f32),
        jnp.zeros((HEAD_DIM, BLOCK_Q), f32),
    )
    carry = lax.fori_loop(lo_ref[step], mid, functools.partial(body, True), carry)
    carry = lax.fori_loop(mid, diagonal, functools.partial(body, False), carry)
    last = (first + BLOCK_Q + BLOCK_K - 1) // BLOCK_K
    top, total, acc = lax.fori_loop(diagonal, last, functools.partial(body, True), carry)
    out = acc / total
    wide_ref[0] = out
    lse_ref[0] = top + jnp.log(total)
    low = out.astype(bf16)
    piece = o_ref.shape[3]
    for i in range(o_ref.shape[0]):
        o_ref[i, 0] = low[:, i * piece : (i + 1) * piece]


def backward_kernel(
    n_steps,
    lo_ref,
    mid_ref,
    q0_ref,
    me_ref,
    q_ref,
    own_ref,
    far_ref,
    start_ref,
    do_ref,
    wide_ref,
    lse_ref,
    dq_ref,
    dkv_ref,
    rows_ref,
    cols_ref,
    acc_ref,
):
    step = pl.program_id(0)

    @pl.when(step == 0)
    def _():
        lay_rows(me_ref[0], own_ref, far_ref, rows_ref, cols_ref, HEAD_DIM)
        acc_ref[...] = jnp.zeros_like(acc_ref)

    @pl.when(step < n_steps)
    def _():
        first = q0_ref[step]
        q = q_ref[0] * jnp.asarray(SCALE, bf16)
        do = jnp.concatenate([do_ref[i, 0] for i in range(do_ref.shape[0])], axis=1)
        zero = jnp.zeros_like(q)
        q_pad = jnp.concatenate([q, zero], axis=0)
        do_pad = jnp.concatenate([zero, do], axis=0)
        q_rows = q_pad.T
        do_rows = do_pad.T
        starts = start_ref[0]
        lse = lse_ref[0]
        delta = jnp.sum(do.astype(f32) * wide_ref[0], axis=0, keepdims=True)
        pos = first + lax.broadcasted_iota(jnp.int32, (1, BLOCK_Q), 1)

        def body(masked, kb, dq):
            at = pl.ds(pl.multiple_of(kb * BLOCK_K, BLOCK_K), BLOCK_K)
            rows = rows_ref[at, :]
            s = jnp.dot(rows, q_pad, preferred_element_type=f32)
            p = jnp.exp(s - lse)
            if masked:
                p = jnp.where(allowed_keys(kb, starts, pos), p, 0.0)
            dp = jnp.dot(rows, do_pad, preferred_element_type=f32)
            ds = (p * (dp - delta)).astype(bf16)
            acc_ref[at, :] += jnp.dot(p.astype(bf16), do_rows, preferred_element_type=f32) + jnp.dot(
                ds, q_rows, preferred_element_type=f32
            )
            return dq + jnp.dot(cols_ref[kb], ds, preferred_element_type=f32)

        diagonal = first // BLOCK_K
        mid = jnp.minimum(mid_ref[step], diagonal)
        dq = jnp.zeros((HEAD_DIM, BLOCK_Q), f32)
        dq = lax.fori_loop(lo_ref[step], mid, functools.partial(body, True), dq)
        dq = lax.fori_loop(mid, diagonal, functools.partial(body, False), dq)
        last = (first + BLOCK_Q + BLOCK_K - 1) // BLOCK_K
        dq = lax.fori_loop(diagonal, last, functools.partial(body, True), dq)
        dq_ref[0] = (dq * SCALE).astype(bf16)

    @pl.when(step >= n_steps)
    def _():
        kb = jnp.maximum(step - n_steps, 0)
        at = pl.ds(pl.multiple_of(kb * BLOCK_K, BLOCK_K), BLOCK_K)
        dkv_ref[0, 0] = acc_ref[at, :].astype(bf16).T


def attention_specs(qkv, far, tok_rows):
    hb, depth, block_rows = qkv.shape
    subs = block_rows // BLOCK_Q
    pieces = BLOCK_Q // tok_rows

    def wrap(index):
        return lambda i, *_: index(i)

    q_spec = lambda cap: pl.BlockSpec((1, HEAD_DIM, BLOCK_Q), wrap(lambda i: (cap(i) // subs, 0, cap(i) % subs)))
    row_spec = lambda cap: pl.BlockSpec((1, 1, BLOCK_Q), wrap(lambda i: (cap(i) // subs, 0, cap(i) % subs)))
    piece_spec = lambda cap: pl.BlockSpec(
        (pieces, 1, HEAD_DIM, tok_rows), wrap(lambda i: (cap(i) % subs, cap(i) // subs, 0, 0))
    )
    own_spec = pl.BlockSpec((hb, depth, block_rows), wrap(lambda i: (0, 0, 0)), pipeline_mode=pl.Buffered(1))
    far_spec = pl.BlockSpec(far.shape, wrap(lambda i: (0, 0, 0, 0)), pipeline_mode=pl.Buffered(1))
    return q_spec, row_spec, piece_spec, own_spec, far_spec


def padded_cost(products, queries, keys):
    pairs = queries * keys // 2
    return pl.CostEstimate(flops=products * 2 * 256 * pairs, transcendentals=pairs, bytes_accessed=8 * keys * HEAD_DIM)


def attention_forward(bounds, qkv, far, starts, n_head, tok_rows):
    hb, _, block_rows = qkv.shape
    queries = hb * block_rows
    keys = queries * (far.shape[0] + 1)
    q_spec, row_spec, piece_spec, own_spec, far_spec = attention_specs(qkv, far, tok_rows)
    same = lambda i: i
    return pl.pallas_call(
        forward_kernel,
        grid_spec=pltpu.PrefetchScalarGridSpec(
            num_scalar_prefetch=4,
            grid=(queries // BLOCK_Q,),
            in_specs=[q_spec(same), own_spec, far_spec, row_spec(same)],
            out_specs=[piece_spec(same), q_spec(same), row_spec(same)],
            scratch_shapes=[
                pltpu.VMEM((keys, 2 * HEAD_DIM), bf16),
                pltpu.VMEM((keys // BLOCK_K, HEAD_DIM, BLOCK_K), bf16),
            ],
        ),
        out_shape=[
            jax.ShapeDtypeStruct((n_head, hb, HEAD_DIM, tok_rows), bf16),
            jax.ShapeDtypeStruct((hb, HEAD_DIM, block_rows), f32),
            jax.ShapeDtypeStruct((hb, 1, block_rows), f32),
        ],
        compiler_params=pltpu.CompilerParams(vmem_limit_bytes=VMEM_BYTES),
        cost_estimate=padded_cost(2, queries, keys),
        name="attention_forward",
    )(*bounds, qkv, qkv, far, starts)


def attention_backward(bounds, qkv, far, starts, do, wide, lse):
    hb, _, block_rows = qkv.shape
    n_rest = far.shape[0] + 1
    queries = hb * block_rows
    keys = queries * n_rest
    n_kb = keys // BLOCK_K
    subs = block_rows // BLOCK_K
    n_steps = queries // BLOCK_Q
    q_spec, row_spec, piece_spec, own_spec, far_spec = attention_specs(qkv, far, do.shape[3])
    cap = lambda i: jnp.minimum(i, n_steps - 1)

    def place(i, *_):
        kb = jnp.maximum(i - n_steps, 0)
        return (kb // subs % n_rest, kb // subs // n_rest, 0, kb % subs)

    return pl.pallas_call(
        functools.partial(backward_kernel, n_steps),
        grid_spec=pltpu.PrefetchScalarGridSpec(
            num_scalar_prefetch=4,
            grid=(n_steps + n_kb,),
            in_specs=[q_spec(cap), own_spec, far_spec, row_spec(cap), piece_spec(cap), q_spec(cap), row_spec(cap)],
            out_specs=[q_spec(cap), pl.BlockSpec((1, 1, 2 * HEAD_DIM, BLOCK_K), place)],
            scratch_shapes=[
                pltpu.VMEM((keys, 2 * HEAD_DIM), bf16),
                pltpu.VMEM((n_kb, HEAD_DIM, BLOCK_K), bf16),
                pltpu.VMEM((keys, 2 * HEAD_DIM), f32),
            ],
        ),
        out_shape=[
            jax.ShapeDtypeStruct((hb, HEAD_DIM, block_rows), bf16),
            jax.ShapeDtypeStruct((n_rest, hb, 2 * HEAD_DIM, block_rows), bf16),
        ],
        compiler_params=pltpu.CompilerParams(vmem_limit_bytes=VMEM_BYTES),
        cost_estimate=padded_cost(5, queries, keys),
        name="attention_backward",
    )(*bounds, qkv, qkv, far, starts, do, wide, lse)


def on_device(
    tokens,
    cotangent,
    segment,
    norm_gain,
    norm_shift,
    in_weight,
    query_bias,
    value_bias,
    out_weight,
    out_bias,
    post_gain,
    post_shift,
    up_weight,
    up_bias,
    down_weight,
    down_bias,
):
    n_head, n_u, n_v, n_rest = (lax.axis_size(a) for a in ALL)
    hb = n_u * n_v
    n_blk = hb * n_rest
    n_all = n_head * n_blk
    me_head, me_u, me_v, me_rest = (lax.axis_index(a) for a in ALL)
    me_blk = (me_u * n_v + me_v) * n_rest + me_rest
    tok_rows, width = tokens.shape
    block_rows = tok_rows * n_head
    length = segment.shape[0]
    w_rows = in_weight.shape[0]
    group = 3 * hb * HEAD_DIM

    chips = n_head * hb
    f_rows = down_weight.shape[0] // 2

    units = up_weight.reshape(w_rows, n_head, n_u, n_v, n_rest, 2, f_rows)
    up_cols = jnp.concatenate(
        [
            units[..., 0, :].transpose(4, 0, 3, 2, 1, 5).reshape(n_rest, w_rows, -1),
            units[..., 1, :].transpose(4, 0, 2, 3, 1, 5).reshape(n_rest, w_rows, -1),
        ],
        axis=2,
    )
    f_half = chips * f_rows
    up_cols = exchange_axis(up_cols, "rest").reshape(n_rest * w_rows, 2 * f_half)
    out_rows = gather_axis(out_weight, "rest").reshape(n_rest * w_rows, width)
    n_up = up_bias.shape[0] // w_rows
    vectors = [norm_gain, norm_shift, query_bias, value_bias, out_bias, post_gain, post_shift, down_bias]
    vectors = jnp.concatenate([jnp.stack(vectors), up_bias.reshape(n_up, w_rows)]).T
    vectors = jnp.pad(vectors, ((0, 0), (0, 128 - vectors.shape[1])))
    cols = in_weight.reshape(w_rows, 3, n_head, hb, HEAD_DIM).transpose(2, 0, 3, 1, 4).reshape(n_head, w_rows, group)
    cols = jnp.concatenate([cols, jnp.broadcast_to(vectors, (n_head, w_rows, 128))], axis=2)
    cols = exchange_axis(cols, "head")
    cols = gather_axis(gather_axis(cols, "v"), "u")
    sent = [tokens] + [shifted(tokens, "head", k) for k in range(1, n_head)]
    sent, cols = lax.optimization_barrier((sent, cols))
    cols = gather_axis(cols, "rest")
    cols = cols.transpose(3, 1, 2, 0, 4, 5).reshape(width, group + 128)
    w_in = cols[:, :group]
    vectors = cols[:, group : group + 8 + n_up].T.astype(f32)
    gain_a, shift_a, bias_q, bias_v, bias_out, gain_b, shift_b, bias_down = (vectors[i] for i in range(8))
    bias_up = vectors[8:].reshape(n_up, n_all, w_rows).transpose(1, 0, 2)

    rows_all = jnp.zeros((n_head, tok_rows, width), bf16)
    for k in range(n_head):
        rows_all = put(rows_all, sent[k], (me_head - k) % n_head)
    rows_all = rows_all.reshape(block_rows, width)

    rows_all, down_weight, up_cols, out_rows = lax.optimization_barrier((rows_all, down_weight, up_cols, out_rows))
    rows_all = rows_all.astype(f32)
    joint = jnp.concatenate([up_cols, out_rows], axis=1)
    joint = lax.all_gather(joint, ("head", "u", "v"), axis=0, tiled=True)
    w_up = joint[:, : 2 * f_half]
    w_out = joint[:, 2 * f_half :]
    w_down = gather_axis(down_weight, "head")

    normed, unit_all, inverse_all = norm_forward(rows_all, gain_a, shift_a)
    normed_low = normed.astype(bf16)
    group_bias = jnp.stack([bias_q, jnp.zeros_like(bias_q), bias_v]).reshape(3, n_head, hb, HEAD_DIM)
    group_bias = lax.dynamic_index_in_dim(group_bias, me_head, 1, keepdims=False).transpose(1, 0, 2).reshape(group, 1)
    projected = lax.dot_general(w_in, normed_low, (((0,), (1,)), ((), ())), preferred_element_type=f32)
    projected = (projected + group_bias).astype(bf16)
    qkv = lax.all_to_all(
        projected.reshape(hb, 3 * HEAD_DIM, block_rows), ("u", "v"), split_axis=0, concat_axis=0, tiled=True
    )
    qkv, w_down = lax.optimization_barrier((qkv, w_down))
    far = [shifted(qkv, "rest", k) for k in range(1, n_rest)]
    far = jnp.stack(far) if n_rest > 2 else far[0][None]

    far, w_down = lax.optimization_barrier((far, w_down))
    w_down = [gather_axis(w_down[:, :f_rows], "u"), gather_axis(w_down[:, f_rows:], "v")]

    doc_start = jnp.zeros_like(segment)
    for doc in range(1, DOCS):
        first = jnp.sum((segment < doc).astype(jnp.int32))
        doc_start = jnp.where(segment == doc, first, doc_start)
    starts = lax.dynamic_index_in_dim(doc_start.reshape(hb, n_rest, block_rows), me_rest, 1, keepdims=False)
    starts_q = starts.reshape(-1, BLOCK_Q)
    lo = starts_q[:, 0] // BLOCK_K
    mid = (starts_q[:, -1] + BLOCK_K - 1) // BLOCK_K
    q_first = (jnp.arange(hb, dtype=jnp.int32)[:, None] * n_rest + me_rest) * block_rows
    q_first = (q_first + jnp.arange(block_rows // BLOCK_Q, dtype=jnp.int32)[None] * BLOCK_Q).reshape(-1)
    bounds = (lo, mid, q_first, me_rest.astype(jnp.int32).reshape(1))
    starts = starts.reshape(hb, 1, block_rows)

    attended, wide, lse = attention_forward(bounds, qkv, far, starts, n_head, tok_rows)
    attended, w_down = lax.optimization_barrier((attended, w_down))
    w_down = [gather_axis(w_down[0], "v"), gather_axis(w_down[1], "u")]
    w_down = [w.reshape(f_half, width) for w in w_down]
    back = lax.all_to_all(
        attended.reshape(HEADS, HEAD_DIM, tok_rows), ("head", "u", "v"), split_axis=0, concat_axis=0, tiled=True
    ).reshape(width, tok_rows)

    rows = tokens.astype(f32)
    branch = lax.dot_general(back, w_out, (((0,), (0,)), ((), ())), preferred_element_type=f32) + bias_out
    middle = rows + branch
    hidden_in, unit_mid, inverse_mid = norm_forward(middle, gain_b, shift_b)
    hidden_low = hidden_in.astype(bf16)
    hidden_all = gather_axis(hidden_low, "rest").reshape(n_rest * tok_rows, width)
    cot_all = gather_axis(cotangent, "rest").reshape(n_rest * tok_rows, width)
    bias_units = bias_up.reshape(n_head, n_u, n_v, n_rest, 2, f_rows)
    bias_units = lax.dynamic_index_in_dim(bias_units, me_rest, 3, keepdims=False)
    bias_units = jnp.concatenate(
        [bias_units[..., 0, :].transpose(2, 1, 0, 3).reshape(-1), bias_units[..., 1, :].transpose(1, 2, 0, 3).reshape(-1)]
    )
    pre = jnp.dot(hidden_all, w_up, preferred_element_type=f32) + bias_units
    act, slope = gelu_parts(pre)
    act_low = act.astype(bf16)
    acts = act_low[:, :f_half], act_low[:, f_half:]
    down = jnp.dot(acts[0], w_down[0], preferred_element_type=f32)
    down = down + jnp.dot(acts[1], w_down[1], preferred_element_type=f32)
    down = reduce_axis(down.reshape(n_rest, tok_rows, width), "rest")
    output = (middle + down + bias_down).astype(bf16)
    grad_out = cotangent.astype(f32)
    grad_act = jnp.concatenate(
        [jnp.einsum("td,fd->tf", cot_all, w, preferred_element_type=f32) for w in w_down], axis=1
    )
    grad_pre = (grad_act * slope).astype(bf16)
    grad_hidden = jnp.einsum("tf,df->td", grad_pre, w_up, preferred_element_type=f32)
    grad_hidden = reduce_axis(grad_hidden.reshape(n_rest, tok_rows, width), "rest")
    grad_middle = grad_out + norm_inner(grad_hidden, unit_mid, inverse_mid, gain_b)
    grad_branch = grad_middle.astype(bf16)
    grad_back = lax.dot_general(w_out, grad_branch, (((1,), (1,)), ((), ())), preferred_element_type=f32).astype(bf16)
    grad_heads = lax.all_to_all(
        grad_back.reshape(HEADS, HEAD_DIM, tok_rows), ("head", "u", "v"), split_axis=0, concat_axis=0, tiled=True
    ).reshape(n_head, hb, HEAD_DIM, tok_rows)

    down_grads = [jnp.einsum("tf,td->fd", a, cot_all, preferred_element_type=f32).astype(bf16) for a in acts]
    up_grad = jnp.einsum("td,tf->df", hidden_all, grad_pre, preferred_element_type=f32).astype(bf16)
    out_grad = jnp.einsum("dt,te->de", back, grad_branch, preferred_element_type=f32).astype(bf16)
    out_grad = out_grad.reshape(chips, n_rest, w_rows, width).transpose(1, 0, 2, 3)
    out_grad = reduce_axis(out_grad, "rest").astype(bf16)
    up_grad = up_grad.reshape(n_head, n_u, n_v, -1, 2 * f_half)
    out_grad = out_grad.reshape(n_head, n_u, n_v, -1, width)
    down_a = down_grads[0].reshape(n_v, n_u, n_head, f_rows, width)
    down_b = down_grads[1].reshape(n_u, n_v, n_head, f_rows, width)
    sums = [
        jnp.sum(grad_branch.astype(f32), axis=0),
        jnp.sum(grad_hidden * unit_mid, axis=0),
        jnp.sum(grad_hidden, axis=0),
        jnp.sum(grad_out, axis=0),
    ]
    unit_sum = jnp.sum(grad_pre.astype(f32), axis=0)
    unit_sum = jnp.stack(
        [
            unit_sum[:f_half].reshape(n_v, n_u, n_head, f_rows).transpose(2, 1, 0, 3),
            unit_sum[f_half:].reshape(n_u, n_v, n_head, f_rows).transpose(2, 0, 1, 3),
        ],
        axis=3,
    ).reshape(chips, 1, 2 * f_rows)
    unit_sum = jnp.where((jnp.arange(n_rest) == me_rest)[:, None], unit_sum, 0.0).reshape(n_head, n_blk, n_up, w_rows)

    grad_heads, up_grad, down_a, out_grad, down_b = lax.optimization_barrier(
        (grad_heads, up_grad, down_a, out_grad, down_b)
    )
    begun = [reduce_begin(up_grad, "u", 1), reduce_begin(down_a, "v"), reduce_begin(out_grad, "v", 2)]
    begun.append(reduce_begin(down_b, "head", 2))

    dq, dkv = attention_backward(bounds, qkv, far, starts, grad_heads, wide, lse)
    dq, dkv, begun = lax.optimization_barrier((dq, dkv, begun))
    up_grad, down_a, out_grad, down_b = (reduce_end(x).astype(bf16) for x in begun)
    up_begun = reduce_begin(up_grad, "head")
    down_a = jnp.concatenate([down_a, out_grad.transpose(1, 0, 2, 3)], axis=2)
    dkv = reduce_axis(dkv, "rest").astype(bf16)
    grad_proj = lax.all_to_all(
        jnp.concatenate([dq, dkv], axis=1), ("u", "v"), split_axis=0, concat_axis=0, tiled=True
    ).reshape(group, block_rows)

    grad_normed = lax.dot_general(grad_proj, w_in, (((0,), (1,)), ((), ())), preferred_element_type=f32)
    tokens_low = grad_normed.astype(bf16).reshape(n_head, tok_rows, width)
    tokens_low, grad_proj, up_begun = lax.optimization_barrier((tokens_low, grad_proj, up_begun))
    begun = reduce_begin(tokens_low, "head")
    up_grad = reduce_end(up_begun).astype(bf16)

    in_grad = lax.dot_general(normed_low, grad_proj, (((0,), (1,)), ((), ())), preferred_element_type=f32)
    rowed = lambda x: x.reshape(n_head, n_blk, w_rows)
    gain_grad = rowed(jnp.sum(grad_normed * unit_all, axis=0))
    shift_grad = rowed(jnp.sum(grad_normed, axis=0))
    col_sum = jnp.sum(grad_proj.astype(f32), axis=1).reshape(hb, 3, HEAD_DIM)
    mine = (jnp.arange(n_head) == me_head)[:, None, None]
    query_sum = jnp.where(mine, col_sum[:, 0].reshape(1, n_blk, w_rows), 0.0)
    value_sum = jnp.where(mine, col_sum[:, 2].reshape(1, n_blk, w_rows), 0.0)
    extra = jnp.stack([gain_grad, shift_grad, query_sum, value_sum, *(rowed(x) for x in sums)], axis=2)
    extra = jnp.concatenate([extra, unit_sum], axis=2)
    n_extra = extra.shape[2]
    extra = jnp.pad(extra.transpose(0, 1, 3, 2), ((0, 0), (0, 0), (0, 0), (0, width - group - n_extra)))
    joined = jnp.concatenate([in_grad.reshape(n_head, n_blk, w_rows, group), extra], axis=-1).astype(bf16)
    joined = joined.reshape(n_head, n_u, n_v, n_rest, w_rows, width)
    joined = reduce_axis(joined, "rest", 3).astype(bf16)
    joined, up_grad, down_a, down_b = lax.optimization_barrier((joined, up_grad, down_a, down_b))
    joined = reduce_axis(joined, "u", 1).astype(bf16)
    joined = reduce_axis(joined, "v", 1).astype(bf16)

    up_grad = reduce_axis(up_grad, "v").astype(bf16).reshape(n_rest, w_rows, 2 * f_half)
    down_a = reduce_axis(down_a, "u").astype(bf16)
    down_b = reduce_axis(down_b, "u").astype(bf16)

    begun, joined, up_grad, down_a, down_b = lax.optimization_barrier((begun, joined, up_grad, down_a, down_b))
    split = down_a.shape[1]
    last = reduce_begin(jnp.concatenate([down_a, joined], axis=1), "head")
    down_b = reduce_axis(down_b, "v")
    up_grad = exchange_axis(up_grad, "rest").astype(f32)
    down_a = reduce_end([x[:split] for x in last])
    out_weight_grad = down_a[f_rows:]
    down_weight_grad = jnp.concatenate([down_a[:f_rows], down_b], axis=0)
    joined = jnp.zeros((n_head, w_rows, width), bf16)
    for k in range(n_head):
        joined = put(joined, last[k][split:], (me_head - k) % n_head)
    joined = joined.astype(f32)
    up_weight_grad = jnp.stack(
        [
            up_grad[..., :f_half].reshape(n_rest, w_rows, n_v, n_u, n_head, f_rows).transpose(1, 4, 3, 2, 0, 5),
            up_grad[..., f_half:].reshape(n_rest, w_rows, n_u, n_v, n_head, f_rows).transpose(1, 4, 2, 3, 0, 5),
        ],
        axis=5,
    ).reshape(w_rows, -1)
    in_weight_grad = joined[:, :, :group].reshape(n_head, w_rows, hb, 3, HEAD_DIM).transpose(1, 3, 0, 2, 4)
    in_weight_grad = in_weight_grad.reshape(w_rows, 3 * width)
    extra = jnp.sum(joined[:, :, group : group + n_extra], axis=0).T
    norm_gain_grad, norm_shift_grad, query_bias_grad, value_bias_grad = (extra[i] for i in range(4))
    out_bias_grad, post_gain_grad, post_shift_grad, down_bias_grad = (extra[i] for i in range(4, 8))
    up_bias_grad = extra[8:].reshape(-1)

    grad_tokens = reduce_end(begun)
    unit_in = lax.dynamic_index_in_dim(unit_all.reshape(n_head, tok_rows, width), me_head, 0, keepdims=False)
    inverse_in = lax.dynamic_index_in_dim(inverse_all.reshape(n_head, tok_rows, 1), me_head, 0, keepdims=False)
    tokens_grad = (grad_middle + norm_inner(grad_tokens, unit_in, inverse_in, gain_a)).astype(bf16)
    return (
        output,
        tokens_grad,
        norm_gain_grad,
        norm_shift_grad,
        in_weight_grad,
        query_bias_grad,
        value_bias_grad,
        out_weight_grad,
        out_bias_grad,
        post_gain_grad,
        post_shift_grad,
        up_weight_grad,
        up_bias_grad,
        down_weight_grad,
        down_bias_grad,
    )


def solution(mesh):
    n_head, n_blk = mesh.shape["head"], mesh.shape["blk"]
    hb = HEADS // n_head
    n_u = 2 if hb % 2 == 0 else 1
    fine = Mesh(mesh.devices.reshape(n_head, n_u, hb // n_u, n_blk // hb), ALL)
    tok = P(("u", "v", "rest", "head"), None)
    vec = P(ALL)
    mat = P(ALL, None)
    return jax.shard_map(
        on_device,
        mesh=fine,
        in_specs=(tok, tok, P(), vec, vec, mat, vec, vec, mat, vec, vec, vec, mat, vec, mat, vec),
        out_specs=(tok, tok, vec, vec, mat, vec, vec, mat, vec, vec, vec, mat, vec, mat, vec),
        check_vma=False,
    )
```

```python
import functools

import jax
import jax.numpy as jnp
from jax import lax
from jax.experimental import pallas as pl
from jax.experimental.pallas import tpu as pltpu
from jax.sharding import Mesh
from jax.sharding import PartitionSpec as P

HEADS = 16
HEAD_DIM = 64
DOCS = 4
BLOCK_Q = 512
BLOCK_K = 512
VMEM_BYTES = 56 * 1024 * 1024

EPS = 1e-05
NEGATIVE = -1e30
GELU_C = 0.7978845608028654
SCALE = HEAD_DIM ** (-0.5)
ALL = ("head", "u", "v", "rest")
f32 = jnp.float32
bf16 = jnp.bfloat16


def norm_forward(rows, gain, shift):
    center = rows - jnp.mean(rows, axis=-1, keepdims=True)
    var = jnp.mean(center * center, axis=-1, keepdims=True)
    inverse = lax.rsqrt(var + EPS)
    unit = center * inverse
    return (unit * gain + shift, unit, inverse)


def norm_inner(grad, unit, inverse, gain):
    scaled = grad * gain
    inner = (
        scaled
        - jnp.mean(scaled, axis=-1, keepdims=True)
        - unit * jnp.mean(scaled * unit, axis=-1, keepdims=True)
    )
    return inverse * inner


def gelu_parts(pre):
    cubic = pre * pre * pre
    tangent = jnp.tanh(GELU_C * (pre + 0.044715 * cubic))
    value = 0.5 * pre * (1.0 + tangent)
    slope = 0.5 * (1.0 + tangent) + 0.5 * pre * (1.0 - tangent * tangent) * GELU_C * (
        1.0 + 3.0 * 0.044715 * pre * pre
    )
    return (value, slope)


def shifted(x, axis, k):
    n = lax.axis_size(axis)
    return lax.ppermute(x, axis, [(i, (i + k) % n) for i in range(n)])


def put(buffer, x, index):
    return lax.dynamic_update_index_in_dim(buffer, x, index, 0)


def gather_axis(x, axis):
    n = lax.axis_size(axis)
    if n == 1:
        return x[None]
    me = lax.axis_index(axis)
    out = put(jnp.zeros((n,) + x.shape, x.dtype), x, me)
    for k in range(1, n):
        out = put(out, shifted(x, axis, k), (me - k) % n)
    return out


def reduce_begin(x, axis, dim=0):
    n = lax.axis_size(axis)
    if n == 1:
        return [lax.index_in_dim(x, 0, dim, keepdims=False)]
    me = lax.axis_index(axis)
    pieces = [lax.dynamic_index_in_dim(x, (me + k) % n, dim, keepdims=False) for k in range(n)]
    return pieces[:1] + [shifted(pieces[k], axis, k) for k in range(1, n)]


def reduce_end(pieces):
    total = pieces[0].astype(f32)
    for piece in pieces[1:]:
        total = total + piece.astype(f32)
    return total


def reduce_axis(x, axis, dim=0):
    return reduce_end(reduce_begin(x, axis, dim))


def exchange_axis(x, axis):
    n = lax.axis_size(axis)
    if n == 1:
        return x
    me = lax.axis_index(axis)
    mine = lax.dynamic_index_in_dim(x, me, 0, keepdims=False)
    out = put(jnp.zeros_like(x), mine, me)
    for k in range(1, n):
        piece = lax.dynamic_index_in_dim(x, (me + k) % n, 0, keepdims=False)
        out = put(out, shifted(piece, axis, k), (me - k) % n)
    return out


def allowed_keys(kb, starts, pos):
    t = kb * BLOCK_K + lax.broadcasted_iota(jnp.int32, (BLOCK_K, BLOCK_Q), 0)
    return (t >= starts) & (t <= pos)


def lay_rows(me, own_ref, far_ref, rows_ref, cols_ref, first):
    hb, _, block_rows = own_ref.shape
    n_rest = far_ref.shape[0] + 1
    subs = block_rows // BLOCK_K

    def lay(read, b, rest):
        for sub in range(subs):
            kb = (b * n_rest + rest) * subs + sub
            block = read(b)[:, sub * BLOCK_K : (sub + 1) * BLOCK_K]
            rows_ref[pl.ds(pl.multiple_of(kb * BLOCK_K, BLOCK_K), BLOCK_K), :] = block[HEAD_DIM:].T
            cols_ref[kb] = block[first : first + HEAD_DIM]

    def each(b, _):
        lay(lambda b: own_ref[b], b, me)
        for k in range(1, n_rest):
            lay(lambda b: far_ref[k - 1, b], b, (me - k) % n_rest)
        return 0

    lax.fori_loop(0, hb, each, 0)


def forward_kernel(
    lo_ref, mid_ref, q0_ref, me_ref, q_ref, own_ref, far_ref, start_ref, o_ref, wide_ref, lse_ref, rows_ref, cols_ref
):
    step = pl.program_id(0)

    @pl.when(step == 0)
    def _():
        lay_rows(me_ref[0], own_ref, far_ref, rows_ref, cols_ref, 2 * HEAD_DIM)

    first = q0_ref[step]
    q = q_ref[0] * jnp.asarray(SCALE, bf16)
    q_pad = jnp.concatenate([q, jnp.zeros_like(q)], axis=0)
    starts = start_ref[0]
    pos = first + lax.broadcasted_iota(jnp.int32, (1, BLOCK_Q), 1)

    def body(masked, kb, carry):
        top, total, acc = carry
        rows = rows_ref[pl.ds(pl.multiple_of(kb * BLOCK_K, BLOCK_K), BLOCK_K), :]
        s = jnp.dot(rows, q_pad, preferred_element_type=f32)
        if masked:
            s = jnp.where(allowed_keys(kb, starts, pos), s, NEGATIVE)
        new_top = jnp.maximum(top, jnp.max(s, axis=0, keepdims=True))
        p = jnp.exp(s - new_top)
        factor = jnp.exp(top - new_top)
        values = cols_ref[kb]
        acc = acc * factor + jnp.dot(values, p.astype(bf16), preferred_element_type=f32)
        return (new_top, total * factor + jnp.sum(p, axis=0, keepdims=True), acc)

    diagonal = first // BLOCK_K
    mid = jnp.minimum(mid_ref[step], diagonal)
    carry = (
        jnp.full((1, BLOCK_Q), NEGATIVE, f32),
        jnp.zeros((1, BLOCK_Q), f32),
        jnp.zeros((HEAD_DIM, BLOCK_Q), f32),
    )
    carry = lax.fori_loop(lo_ref[step], mid, functools.partial(body, True), carry)
    carry = lax.fori_loop(mid, diagonal, functools.partial(body, False), carry)
    last = (first + BLOCK_Q + BLOCK_K - 1) // BLOCK_K
    top, total, acc = lax.fori_loop(diagonal, last, functools.partial(body, True), carry)
    out = acc / total
    wide_ref[0] = out
    lse_ref[0] = top + jnp.log(total)
    low = out.astype(bf16)
    piece = o_ref.shape[3]
    for i in range(o_ref.shape[0]):
        o_ref[i, 0] = low[:, i * piece : (i + 1) * piece]


def backward_kernel(
    n_steps,
    lo_ref,
    mid_ref,
    q0_ref,
    me_ref,
    q_ref,
    own_ref,
    far_ref,
    start_ref,
    do_ref,
    wide_ref,
    lse_ref,
    dq_ref,
    dkv_ref,
    rows_ref,
    cols_ref,
    acc_ref,
):
    step = pl.program_id(0)

    @pl.when(step == 0)
    def _():
        lay_rows(me_ref[0], own_ref, far_ref, rows_ref, cols_ref, HEAD_DIM)
        acc_ref[...] = jnp.zeros_like(acc_ref)

    @pl.when(step < n_steps)
    def _():
        first = q0_ref[step]
        q = q_ref[0] * jnp.asarray(SCALE, bf16)
        do = jnp.concatenate([do_ref[i, 0] for i in range(do_ref.shape[0])], axis=1)
        zero = jnp.zeros_like(q)
        q_pad = jnp.concatenate([q, zero], axis=0)
        do_pad = jnp.concatenate([zero, do], axis=0)
        q_rows = q_pad.T
        do_rows = do_pad.T
        starts = start_ref[0]
        lse = lse_ref[0]
        delta = jnp.sum(do.astype(f32) * wide_ref[0], axis=0, keepdims=True)
        pos = first + lax.broadcasted_iota(jnp.int32, (1, BLOCK_Q), 1)

        def body(masked, kb, dq):
            at = pl.ds(pl.multiple_of(kb * BLOCK_K, BLOCK_K), BLOCK_K)
            rows = rows_ref[at, :]
            s = jnp.dot(rows, q_pad, preferred_element_type=f32)
            p = jnp.exp(s - lse)
            if masked:
                p = jnp.where(allowed_keys(kb, starts, pos), p, 0.0)
            dp = jnp.dot(rows, do_pad, preferred_element_type=f32)
            ds = (p * (dp - delta)).astype(bf16)
            acc_ref[at, :] += jnp.dot(p.astype(bf16), do_rows, preferred_element_type=f32) + jnp.dot(
                ds, q_rows, preferred_element_type=f32
            )
            return dq + jnp.dot(cols_ref[kb], ds, preferred_element_type=f32)

        diagonal = first // BLOCK_K
        mid = jnp.minimum(mid_ref[step], diagonal)
        dq = jnp.zeros((HEAD_DIM, BLOCK_Q), f32)
        dq = lax.fori_loop(lo_ref[step], mid, functools.partial(body, True), dq)
        dq = lax.fori_loop(mid, diagonal, functools.partial(body, False), dq)
        last = (first + BLOCK_Q + BLOCK_K - 1) // BLOCK_K
        dq = lax.fori_loop(diagonal, last, functools.partial(body, True), dq)
        dq_ref[0] = (dq * SCALE).astype(bf16)

    @pl.when(step >= n_steps)
    def _():
        kb = jnp.maximum(step - n_steps, 0)
        at = pl.ds(pl.multiple_of(kb * BLOCK_K, BLOCK_K), BLOCK_K)
        dkv_ref[0, 0] = acc_ref[at, :].astype(bf16).T


def attention_specs(qkv, far, tok_rows):
    hb, depth, block_rows = qkv.shape
    subs = block_rows // BLOCK_Q
    pieces = BLOCK_Q // tok_rows

    def wrap(index):
        return lambda i, *_: index(i)

    q_spec = lambda cap: pl.BlockSpec((1, HEAD_DIM, BLOCK_Q), wrap(lambda i: (cap(i) // subs, 0, cap(i) % subs)))
    row_spec = lambda cap: pl.BlockSpec((1, 1, BLOCK_Q), wrap(lambda i: (cap(i) // subs, 0, cap(i) % subs)))
    piece_spec = lambda cap: pl.BlockSpec(
        (pieces, 1, HEAD_DIM, tok_rows), wrap(lambda i: (cap(i) % subs, cap(i) // subs, 0, 0))
    )
    own_spec = pl.BlockSpec((hb, depth, block_rows), wrap(lambda i: (0, 0, 0)), pipeline_mode=pl.Buffered(1))
    far_spec = pl.BlockSpec(far.shape, wrap(lambda i: (0, 0, 0, 0)), pipeline_mode=pl.Buffered(1))
    return q_spec, row_spec, piece_spec, own_spec, far_spec


def padded_cost(products, queries, keys):
    pairs = queries * keys // 2
    return pl.CostEstimate(flops=products * 2 * 256 * pairs, transcendentals=pairs, bytes_accessed=8 * keys * HEAD_DIM)


def attention_forward(bounds, qkv, far, starts, n_head, tok_rows):
    hb, _, block_rows = qkv.shape
    queries = hb * block_rows
    keys = queries * (far.shape[0] + 1)
    q_spec, row_spec, piece_spec, own_spec, far_spec = attention_specs(qkv, far, tok_rows)
    same = lambda i: i
    return pl.pallas_call(
        forward_kernel,
        grid_spec=pltpu.PrefetchScalarGridSpec(
            num_scalar_prefetch=4,
            grid=(queries // BLOCK_Q,),
            in_specs=[q_spec(same), own_spec, far_spec, row_spec(same)],
            out_specs=[piece_spec(same), q_spec(same), row_spec(same)],
            scratch_shapes=[
                pltpu.VMEM((keys, 2 * HEAD_DIM), bf16),
                pltpu.VMEM((keys // BLOCK_K, HEAD_DIM, BLOCK_K), bf16),
            ],
        ),
        out_shape=[
            jax.ShapeDtypeStruct((n_head, hb, HEAD_DIM, tok_rows), bf16),
            jax.ShapeDtypeStruct((hb, HEAD_DIM, block_rows), f32),
            jax.ShapeDtypeStruct((hb, 1, block_rows), f32),
        ],
        compiler_params=pltpu.CompilerParams(vmem_limit_bytes=VMEM_BYTES),
        cost_estimate=padded_cost(2, queries, keys),
        name="attention_forward",
    )(*bounds, qkv, qkv, far, starts)


def attention_backward(bounds, qkv, far, starts, do, wide, lse):
    hb, _, block_rows = qkv.shape
    n_rest = far.shape[0] + 1
    queries = hb * block_rows
    keys = queries * n_rest
    n_kb = keys // BLOCK_K
    subs = block_rows // BLOCK_K
    n_steps = queries // BLOCK_Q
    q_spec, row_spec, piece_spec, own_spec, far_spec = attention_specs(qkv, far, do.shape[3])
    cap = lambda i: jnp.minimum(i, n_steps - 1)

    def place(i, *_):
        kb = jnp.maximum(i - n_steps, 0)
        return (kb // subs % n_rest, kb // subs // n_rest, 0, kb % subs)

    return pl.pallas_call(
        functools.partial(backward_kernel, n_steps),
        grid_spec=pltpu.PrefetchScalarGridSpec(
            num_scalar_prefetch=4,
            grid=(n_steps + n_kb,),
            in_specs=[q_spec(cap), own_spec, far_spec, row_spec(cap), piece_spec(cap), q_spec(cap), row_spec(cap)],
            out_specs=[q_spec(cap), pl.BlockSpec((1, 1, 2 * HEAD_DIM, BLOCK_K), place)],
            scratch_shapes=[
                pltpu.VMEM((keys, 2 * HEAD_DIM), bf16),
                pltpu.VMEM((n_kb, HEAD_DIM, BLOCK_K), bf16),
                pltpu.VMEM((keys, 2 * HEAD_DIM), f32),
            ],
        ),
        out_shape=[
            jax.ShapeDtypeStruct((hb, HEAD_DIM, block_rows), bf16),
            jax.ShapeDtypeStruct((n_rest, hb, 2 * HEAD_DIM, block_rows), bf16),
        ],
        compiler_params=pltpu.CompilerParams(vmem_limit_bytes=VMEM_BYTES),
        cost_estimate=padded_cost(5, queries, keys),
        name="attention_backward",
    )(*bounds, qkv, qkv, far, starts, do, wide, lse)


def on_device(
    tokens,
    cotangent,
    segment,
    norm_gain,
    norm_shift,
    in_weight,
    query_bias,
    value_bias,
    out_weight,
    out_bias,
    post_gain,
    post_shift,
    up_weight,
    up_bias,
    down_weight,
    down_bias,
):
    n_head, n_u, n_v, n_rest = (lax.axis_size(a) for a in ALL)
    hb = n_u * n_v
    n_blk = hb * n_rest
    n_all = n_head * n_blk
    me_head, me_u, me_v, me_rest = (lax.axis_index(a) for a in ALL)
    me_blk = (me_u * n_v + me_v) * n_rest + me_rest
    tok_rows, width = tokens.shape
    block_rows = tok_rows * n_head
    length = segment.shape[0]
    w_rows = in_weight.shape[0]
    group = 3 * hb * HEAD_DIM

    chips = n_head * hb
    f_rows = down_weight.shape[0] // 2

    n_up = up_bias.shape[0] // w_rows
    vectors = [norm_gain, norm_shift, query_bias, value_bias, out_bias, post_gain, post_shift, down_bias]
    vectors = jnp.concatenate([jnp.stack(vectors), up_bias.reshape(n_up, w_rows)]).T
    vectors = jnp.pad(vectors, ((0, 0), (0, 128 - vectors.shape[1])))
    cols = in_weight.reshape(w_rows, 3, n_head, hb, HEAD_DIM).transpose(2, 0, 3, 1, 4).reshape(n_head, w_rows, group)
    cols = jnp.concatenate([cols, jnp.broadcast_to(vectors, (n_head, w_rows, 128))], axis=2)
    cols = exchange_axis(cols, "head")
    cols, tokens, up_weight, down_weight, out_weight = lax.optimization_barrier(
        (cols, tokens, up_weight, down_weight, out_weight)
    )

    units = up_weight.reshape(w_rows, chips, n_rest, 2, f_rows).transpose(2, 0, 3, 1, 4)
    f_half = chips * f_rows
    up_cols = exchange_axis(units.reshape(n_rest, w_rows, 2 * f_half), "rest").reshape(n_rest * w_rows, 2 * f_half)
    out_rows = gather_axis(out_weight, "rest").reshape(n_rest * w_rows, width)
    down_rows = down_weight.reshape(2, f_rows, width)
    if f_rows == n_rest * w_rows:
        joint = jnp.concatenate([up_cols, down_rows[0], down_rows[1], out_rows], axis=1)
        joint = lax.all_gather(joint, ("head", "u", "v"), axis=0, tiled=True)
        w_up = joint[:, : 2 * f_half]
        w_down = [joint[:, 2 * f_half + i * width : 2 * f_half + (i + 1) * width] for i in range(2)]
        w_out = joint[:, 2 * f_half + 2 * width :]
    else:
        w_up, w_down_a, w_down_b, w_out = (
            lax.all_gather(w, ("head", "u", "v"), axis=0, tiled=True)
            for w in (up_cols, down_rows[0], down_rows[1], out_rows)
        )
        w_down = [w_down_a, w_down_b]

    cols = gather_axis(gather_axis(cols, "v"), "u")
    sent = [tokens] + [shifted(tokens, "head", k) for k in range(1, n_head)]
    sent, cols = lax.optimization_barrier((sent, cols))
    cols = gather_axis(cols, "rest")
    cols = cols.transpose(3, 1, 2, 0, 4, 5).reshape(width, group + 128)
    w_in = cols[:, :group]
    vectors = cols[:, group : group + 8 + n_up].T.astype(f32)
    gain_a, shift_a, bias_q, bias_v, bias_out, gain_b, shift_b, bias_down = (vectors[i] for i in range(8))
    bias_up = vectors[8:].reshape(n_up, n_all, w_rows).transpose(1, 0, 2)

    rows_all = jnp.zeros((n_head, tok_rows, width), bf16)
    for k in range(n_head):
        rows_all = put(rows_all, sent[k], (me_head - k) % n_head)
    rows_all = rows_all.reshape(block_rows, width)

    rows_all = rows_all.astype(f32)
    normed, unit_all, inverse_all = norm_forward(rows_all, gain_a, shift_a)
    normed_low = normed.astype(bf16)
    group_bias = jnp.stack([bias_q, jnp.zeros_like(bias_q), bias_v]).reshape(3, n_head, hb, HEAD_DIM)
    group_bias = lax.dynamic_index_in_dim(group_bias, me_head, 1, keepdims=False).transpose(1, 0, 2).reshape(group, 1)
    projected = lax.dot_general(w_in, normed_low, (((0,), (1,)), ((), ())), preferred_element_type=f32)
    projected = (projected + group_bias).astype(bf16)
    qkv = lax.all_to_all(
        projected.reshape(hb, 3 * HEAD_DIM, block_rows), ("u", "v"), split_axis=0, concat_axis=0, tiled=True
    )
    far = [shifted(qkv, "rest", k) for k in range(1, n_rest)]
    far = jnp.stack(far) if n_rest > 2 else far[0][None]

    doc_start = jnp.zeros_like(segment)
    for doc in range(1, DOCS):
        first = jnp.sum((segment < doc).astype(jnp.int32))
        doc_start = jnp.where(segment == doc, first, doc_start)
    starts = lax.dynamic_index_in_dim(doc_start.reshape(hb, n_rest, block_rows), me_rest, 1, keepdims=False)
    starts_q = starts.reshape(-1, BLOCK_Q)
    lo = starts_q[:, 0] // BLOCK_K
    mid = (starts_q[:, -1] + BLOCK_K - 1) // BLOCK_K
    q_first = (jnp.arange(hb, dtype=jnp.int32)[:, None] * n_rest + me_rest) * block_rows
    q_first = (q_first + jnp.arange(block_rows // BLOCK_Q, dtype=jnp.int32)[None] * BLOCK_Q).reshape(-1)
    bounds = (lo, mid, q_first, me_rest.astype(jnp.int32).reshape(1))
    starts = starts.reshape(hb, 1, block_rows)

    attended, wide, lse = attention_forward(bounds, qkv, far, starts, n_head, tok_rows)
    back = lax.all_to_all(
        attended.reshape(HEADS, HEAD_DIM, tok_rows), ("head", "u", "v"), split_axis=0, concat_axis=0, tiled=True
    ).reshape(width, tok_rows)

    rows = tokens.astype(f32)
    branch = lax.dot_general(back, w_out, (((0,), (0,)), ((), ())), preferred_element_type=f32) + bias_out
    middle = rows + branch
    hidden_in, unit_mid, inverse_mid = norm_forward(middle, gain_b, shift_b)
    hidden_low = hidden_in.astype(bf16)
    hidden_all = gather_axis(hidden_low, "rest").reshape(n_rest * tok_rows, width)
    cot_all = gather_axis(cotangent, "rest").reshape(n_rest * tok_rows, width)
    bias_units = lax.dynamic_index_in_dim(bias_up.reshape(chips, n_rest, 2, f_rows), me_rest, 1, keepdims=False)
    bias_units = bias_units.transpose(1, 0, 2).reshape(-1)
    pre = jnp.dot(hidden_all, w_up, preferred_element_type=f32) + bias_units
    act, slope = gelu_parts(pre)
    act_low = act.astype(bf16)
    acts = act_low[:, :f_half], act_low[:, f_half:]
    down = jnp.dot(acts[0], w_down[0], preferred_element_type=f32)
    down = down + jnp.dot(acts[1], w_down[1], preferred_element_type=f32)
    down = reduce_axis(down.reshape(n_rest, tok_rows, width), "rest")
    output = (middle + down + bias_down).astype(bf16)
    grad_out = cotangent.astype(f32)
    grad_act = jnp.concatenate(
        [jnp.einsum("td,fd->tf", cot_all, w, preferred_element_type=f32) for w in w_down], axis=1
    )
    grad_pre = (grad_act * slope).astype(bf16)
    grad_hidden = jnp.einsum("tf,df->td", grad_pre, w_up, preferred_element_type=f32)
    grad_hidden = reduce_axis(grad_hidden.reshape(n_rest, tok_rows, width), "rest")
    grad_middle = grad_out + norm_inner(grad_hidden, unit_mid, inverse_mid, gain_b)
    grad_branch = grad_middle.astype(bf16)
    grad_back = lax.dot_general(w_out, grad_branch, (((1,), (1,)), ((), ())), preferred_element_type=f32).astype(bf16)
    grad_heads = lax.all_to_all(
        grad_back.reshape(HEADS, HEAD_DIM, tok_rows), ("head", "u", "v"), split_axis=0, concat_axis=0, tiled=True
    ).reshape(n_head, hb, HEAD_DIM, tok_rows)

    down_grads = [jnp.einsum("tf,td->fd", a, cot_all, preferred_element_type=f32).astype(bf16) for a in acts]
    up_grad = jnp.einsum("td,tf->df", hidden_all, grad_pre, preferred_element_type=f32).astype(bf16)
    out_grad = jnp.einsum("dt,te->de", back, grad_branch, preferred_element_type=f32).astype(bf16)
    out_grad = out_grad.reshape(chips, n_rest, w_rows, width).transpose(1, 0, 2, 3)
    out_grad = reduce_axis(out_grad, "rest").astype(bf16)
    up_grad = up_grad.reshape(n_head, n_u, n_v, -1, 2 * f_half)
    out_grad = out_grad.reshape(n_head, n_u, n_v, -1, width)
    down_a, down_b = (x.reshape(n_head, n_u, n_v, f_rows, width) for x in down_grads)
    sums = [
        jnp.sum(grad_branch.astype(f32), axis=0),
        jnp.sum(grad_hidden * unit_mid, axis=0),
        jnp.sum(grad_hidden, axis=0),
        jnp.sum(grad_out, axis=0),
    ]
    unit_sum = jnp.sum(grad_pre.astype(f32), axis=0)
    unit_sum = unit_sum.reshape(2, chips, f_rows).transpose(1, 0, 2).reshape(chips, 1, 2 * f_rows)
    unit_sum = jnp.where((jnp.arange(n_rest) == me_rest)[:, None], unit_sum, 0.0).reshape(n_head, n_blk, n_up, w_rows)

    grad_heads, up_grad, down_a, out_grad, down_b = lax.optimization_barrier(
        (grad_heads, up_grad, down_a, out_grad, down_b)
    )
    begun = [reduce_begin(up_grad, "u", 1), reduce_begin(down_a, "v", 2), reduce_begin(out_grad, "v", 2)]
    begun.append(reduce_begin(down_b, "head"))

    dq, dkv = attention_backward(bounds, qkv, far, starts, grad_heads, wide, lse)
    dq, dkv, begun = lax.optimization_barrier((dq, dkv, begun))
    up_grad, down_a, out_grad, down_b = (reduce_end(x).astype(bf16) for x in begun)
    down_a = jnp.concatenate([down_a, out_grad], axis=2)
    dkv = reduce_axis(dkv, "rest").astype(bf16)
    grad_proj = lax.all_to_all(
        jnp.concatenate([dq, dkv], axis=1), ("u", "v"), split_axis=0, concat_axis=0, tiled=True
    ).reshape(group, block_rows)

    grad_normed = lax.dot_general(grad_proj, w_in, (((0,), (1,)), ((), ())), preferred_element_type=f32)
    tokens_low = grad_normed.astype(bf16).reshape(n_head, tok_rows, width)
    tokens_low, grad_proj = lax.optimization_barrier((tokens_low, grad_proj))
    begun = reduce_begin(tokens_low, "head")

    in_grad = lax.dot_general(normed_low, grad_proj, (((0,), (1,)), ((), ())), preferred_element_type=f32)
    rowed = lambda x: x.reshape(n_head, n_blk, w_rows)
    gain_grad = rowed(jnp.sum(grad_normed * unit_all, axis=0))
    shift_grad = rowed(jnp.sum(grad_normed, axis=0))
    col_sum = jnp.sum(grad_proj.astype(f32), axis=1).reshape(hb, 3, HEAD_DIM)
    mine = (jnp.arange(n_head) == me_head)[:, None, None]
    query_sum = jnp.where(mine, col_sum[:, 0].reshape(1, n_blk, w_rows), 0.0)
    value_sum = jnp.where(mine, col_sum[:, 2].reshape(1, n_blk, w_rows), 0.0)
    extra = jnp.stack([gain_grad, shift_grad, query_sum, value_sum, *(rowed(x) for x in sums)], axis=2)
    extra = jnp.concatenate([extra, unit_sum], axis=2)
    n_extra = extra.shape[2]
    extra = jnp.pad(extra.transpose(0, 1, 3, 2), ((0, 0), (0, 0), (0, 0), (0, width - group - n_extra)))
    joined = jnp.concatenate([in_grad.reshape(n_head, n_blk, w_rows, group), extra], axis=-1).astype(bf16)
    joined = joined.reshape(n_head, n_u, n_v, n_rest, w_rows, width)
    early, begun = begun[:2], begun[2:]
    early, joined, up_grad, down_a, down_b = lax.optimization_barrier((early, joined, up_grad, down_a, down_b))
    joined = reduce_axis(joined, "rest", 3).astype(bf16)
    joined = reduce_axis(joined, "u", 1).astype(bf16)
    joined = reduce_axis(joined, "v", 1).astype(bf16)

    up_grad = reduce_axis(up_grad, "v", 1).astype(bf16)
    n_rows = n_head * down_a.shape[2]
    down_a = down_a.transpose(1, 0, 2, 3).reshape(n_u, n_rows, width)
    down_a = reduce_axis(jnp.concatenate([down_a, down_b.reshape(n_u, -1, width)], axis=1), "u").astype(bf16)
    down_b = down_a[n_rows:].reshape(n_v, f_rows, width)
    down_a = down_a[:n_rows].reshape(n_head, -1, width)

    begun, joined, up_grad, down_a, down_b = lax.optimization_barrier((begun, joined, up_grad, down_a, down_b))
    split = down_a.shape[1]
    last = reduce_begin(jnp.concatenate([down_a, joined], axis=1), "head")
    down_b = reduce_axis(down_b, "v")
    up_grad = reduce_axis(up_grad, "head").astype(bf16).reshape(n_rest, w_rows, 2 * f_half)
    up_grad = exchange_axis(up_grad, "rest").astype(f32)
    down_a = reduce_end([x[:split] for x in last])
    out_weight_grad = down_a[f_rows:]
    down_weight_grad = jnp.concatenate([down_a[:f_rows], down_b], axis=0)
    joined = jnp.zeros((n_head, w_rows, width), bf16)
    for k in range(n_head):
        joined = put(joined, last[k][split:], (me_head - k) % n_head)
    joined = joined.astype(f32)
    up_weight_grad = up_grad.reshape(n_rest, w_rows, 2, chips, f_rows).transpose(1, 3, 0, 2, 4).reshape(w_rows, -1)
    in_weight_grad = joined[:, :, :group].reshape(n_head, w_rows, hb, 3, HEAD_DIM).transpose(1, 3, 0, 2, 4)
    in_weight_grad = in_weight_grad.reshape(w_rows, 3 * width)
    extra = jnp.sum(joined[:, :, group : group + n_extra], axis=0).T
    norm_gain_grad, norm_shift_grad, query_bias_grad, value_bias_grad = (extra[i] for i in range(4))
    out_bias_grad, post_gain_grad, post_shift_grad, down_bias_grad = (extra[i] for i in range(4, 8))
    up_bias_grad = extra[8:].reshape(-1)

    grad_tokens = reduce_end(early + begun)
    unit_in = lax.dynamic_index_in_dim(unit_all.reshape(n_head, tok_rows, width), me_head, 0, keepdims=False)
    inverse_in = lax.dynamic_index_in_dim(inverse_all.reshape(n_head, tok_rows, 1), me_head, 0, keepdims=False)
    tokens_grad = (grad_middle + norm_inner(grad_tokens, unit_in, inverse_in, gain_a)).astype(bf16)
    return (
        output,
        tokens_grad,
        norm_gain_grad,
        norm_shift_grad,
        in_weight_grad,
        query_bias_grad,
        value_bias_grad,
        out_weight_grad,
        out_bias_grad,
        post_gain_grad,
        post_shift_grad,
        up_weight_grad,
        up_bias_grad,
        down_weight_grad,
        down_bias_grad,
    )


def solution(mesh):
    n_head, n_blk = mesh.shape["head"], mesh.shape["blk"]
    hb = HEADS // n_head
    n_u = 2 if hb % 2 == 0 else 1
    fine = Mesh(mesh.devices.reshape(n_head, n_u, hb // n_u, n_blk // hb), ALL)
    tok = P(("u", "v", "rest", "head"), None)
    vec = P(ALL)
    mat = P(ALL, None)
    return jax.shard_map(
        on_device,
        mesh=fine,
        in_specs=(tok, tok, P(), vec, vec, mat, vec, vec, mat, vec, vec, vec, mat, vec, mat, vec),
        out_specs=(tok, tok, vec, vec, mat, vec, vec, mat, vec, vec, vec, mat, vec, mat, vec),
        check_vma=False,
    )
```

```python
import functools

import jax
import jax.numpy as jnp
from jax import lax
from jax.experimental import pallas as pl
from jax.experimental.pallas import tpu as pltpu
from jax.sharding import Mesh
from jax.sharding import PartitionSpec as P

HEADS = 16
HEAD_DIM = 64
DOCS = 4
FORWARD_Q = 1024
BLOCK_Q = 512
BLOCK_K = 512
VMEM_BYTES = 56 * 1024 * 1024

EPS = 1e-05
NEGATIVE = -1e30
GELU_C = 0.7978845608028654
SCALE = HEAD_DIM ** (-0.5)
ALL = ("head", "u", "v", "rest")
f32 = jnp.float32
bf16 = jnp.bfloat16


def norm_forward(rows, gain, shift):
    center = rows - jnp.mean(rows, axis=-1, keepdims=True)
    var = jnp.mean(center * center, axis=-1, keepdims=True)
    inverse = lax.rsqrt(var + EPS)
    unit = center * inverse
    return (unit * gain + shift, unit, inverse)


def norm_inner(grad, unit, inverse, gain):
    scaled = grad * gain
    inner = (
        scaled
        - jnp.mean(scaled, axis=-1, keepdims=True)
        - unit * jnp.mean(scaled * unit, axis=-1, keepdims=True)
    )
    return inverse * inner


def gelu_parts(pre):
    cubic = pre * pre * pre
    tangent = jnp.tanh(GELU_C * (pre + 0.044715 * cubic))
    value = 0.5 * pre * (1.0 + tangent)
    slope = 0.5 * (1.0 + tangent) + 0.5 * pre * (1.0 - tangent * tangent) * GELU_C * (
        1.0 + 3.0 * 0.044715 * pre * pre
    )
    return (value, slope)


def shifted(x, axis, k):
    n = lax.axis_size(axis)
    return lax.ppermute(x, axis, [(i, (i + k) % n) for i in range(n)])


def put(buffer, x, index):
    return lax.dynamic_update_index_in_dim(buffer, x, index, 0)


def gather_axis(x, axis):
    n = lax.axis_size(axis)
    if n == 1:
        return x[None]
    me = lax.axis_index(axis)
    out = put(jnp.zeros((n,) + x.shape, x.dtype), x, me)
    for k in range(1, n):
        out = put(out, shifted(x, axis, k), (me - k) % n)
    return out


def reduce_begin(x, axis, dim=0):
    n = lax.axis_size(axis)
    if n == 1:
        return [lax.index_in_dim(x, 0, dim, keepdims=False)]
    me = lax.axis_index(axis)
    pieces = [lax.dynamic_index_in_dim(x, (me + k) % n, dim, keepdims=False) for k in range(n)]
    return pieces[:1] + [shifted(pieces[k], axis, k) for k in range(1, n)]


def reduce_end(pieces):
    total = pieces[0].astype(f32)
    for piece in pieces[1:]:
        total = total + piece.astype(f32)
    return total


def reduce_axis(x, axis, dim=0):
    return reduce_end(reduce_begin(x, axis, dim))


def exchange_axis(x, axis):
    n = lax.axis_size(axis)
    if n == 1:
        return x
    me = lax.axis_index(axis)
    mine = lax.dynamic_index_in_dim(x, me, 0, keepdims=False)
    out = put(jnp.zeros_like(x), mine, me)
    for k in range(1, n):
        piece = lax.dynamic_index_in_dim(x, (me + k) % n, 0, keepdims=False)
        out = put(out, shifted(piece, axis, k), (me - k) % n)
    return out


def allowed_keys(kb, starts, pos):
    t = kb * BLOCK_K + lax.broadcasted_iota(jnp.int32, (BLOCK_K, pos.shape[1]), 0)
    return (t >= starts) & (t <= pos)


def lay_rows(me, own_ref, far_ref, rows_ref, cols_ref, first):
    hb, _, block_rows = own_ref.shape
    n_rest = far_ref.shape[0] + 1
    subs = block_rows // BLOCK_K

    def lay(read, b, rest):
        for sub in range(subs):
            kb = (b * n_rest + rest) * subs + sub
            block = read(b)[:, sub * BLOCK_K : (sub + 1) * BLOCK_K]
            rows_ref[pl.ds(pl.multiple_of(kb * BLOCK_K, BLOCK_K), BLOCK_K), :] = block[HEAD_DIM:].T
            cols_ref[kb] = block[first : first + HEAD_DIM]

    def each(b, _):
        lay(lambda b: own_ref[b], b, me)
        for k in range(1, n_rest):
            lay(lambda b: far_ref[k - 1, b], b, (me - k) % n_rest)
        return 0

    lax.fori_loop(0, hb, each, 0)


def forward_kernel(
    lo_ref, mid_ref, q0_ref, me_ref, q_ref, own_ref, far_ref, start_ref, o_ref, wide_ref, lse_ref, rows_ref, cols_ref
):
    step = pl.program_id(0)

    @pl.when(step == 0)
    def _():
        lay_rows(me_ref[0], own_ref, far_ref, rows_ref, cols_ref, 2 * HEAD_DIM)

    first = q0_ref[step]
    q = q_ref[0] * jnp.asarray(SCALE, bf16)
    q_pad = jnp.concatenate([q, jnp.zeros_like(q)], axis=0)
    starts = start_ref[0]
    pos = first + lax.broadcasted_iota(jnp.int32, (1, FORWARD_Q), 1)

    def body(masked, kb, carry):
        top, total, acc = carry
        rows = rows_ref[pl.ds(pl.multiple_of(kb * BLOCK_K, BLOCK_K), BLOCK_K), :]
        s = jnp.dot(rows, q_pad, preferred_element_type=f32)
        if masked:
            s = jnp.where(allowed_keys(kb, starts, pos), s, NEGATIVE)
        new_top = jnp.maximum(top, jnp.max(s, axis=0, keepdims=True))
        p = jnp.exp(s - new_top)
        factor = jnp.exp(top - new_top)
        values = cols_ref[kb]
        acc = acc * factor + jnp.dot(values, p.astype(bf16), preferred_element_type=f32)
        return (new_top, total * factor + jnp.sum(p, axis=0, keepdims=True), acc)

    diagonal = first // BLOCK_K
    mid = jnp.minimum(mid_ref[step], diagonal)
    carry = (
        jnp.full((1, FORWARD_Q), NEGATIVE, f32),
        jnp.zeros((1, FORWARD_Q), f32),
        jnp.zeros((HEAD_DIM, FORWARD_Q), f32),
    )
    carry = lax.fori_loop(lo_ref[step], mid, functools.partial(body, True), carry)
    carry = lax.fori_loop(mid, diagonal, functools.partial(body, False), carry)
    last = (first + FORWARD_Q + BLOCK_K - 1) // BLOCK_K
    top, total, acc = lax.fori_loop(diagonal, last, functools.partial(body, True), carry)
    out = acc / total
    wide_ref[0] = out
    lse_ref[0] = top + jnp.log(total)
    low = out.astype(bf16)
    piece = o_ref.shape[3]
    for i in range(o_ref.shape[0]):
        o_ref[i, 0] = low[:, i * piece : (i + 1) * piece]


def backward_kernel(
    n_steps,
    lo_ref,
    mid_ref,
    q0_ref,
    me_ref,
    q_ref,
    own_ref,
    far_ref,
    start_ref,
    do_ref,
    wide_ref,
    lse_ref,
    dq_ref,
    dkv_ref,
    rows_ref,
    cols_ref,
    acc_ref,
):
    step = pl.program_id(0)

    @pl.when(step == 0)
    def _():
        lay_rows(me_ref[0], own_ref, far_ref, rows_ref, cols_ref, HEAD_DIM)
        acc_ref[...] = jnp.zeros_like(acc_ref)

    @pl.when(step < n_steps)
    def _():
        first = q0_ref[step]
        q = q_ref[0] * jnp.asarray(SCALE, bf16)
        do = jnp.concatenate([do_ref[i, 0] for i in range(do_ref.shape[0])], axis=1)
        zero = jnp.zeros_like(q)
        q_pad = jnp.concatenate([q, zero], axis=0)
        do_pad = jnp.concatenate([zero, do], axis=0)
        q_rows = q_pad.T
        do_rows = do_pad.T
        starts = start_ref[0]
        lse = lse_ref[0]
        delta = jnp.sum(do.astype(f32) * wide_ref[0], axis=0, keepdims=True)
        pos = first + lax.broadcasted_iota(jnp.int32, (1, BLOCK_Q), 1)

        def body(masked, kb, dq):
            at = pl.ds(pl.multiple_of(kb * BLOCK_K, BLOCK_K), BLOCK_K)
            rows = rows_ref[at, :]
            s = jnp.dot(rows, q_pad, preferred_element_type=f32)
            p = jnp.exp(s - lse)
            if masked:
                p = jnp.where(allowed_keys(kb, starts, pos), p, 0.0)
            dp = jnp.dot(rows, do_pad, preferred_element_type=f32)
            ds = (p * (dp - delta)).astype(bf16)
            acc_ref[at, :] += jnp.dot(p.astype(bf16), do_rows, preferred_element_type=f32) + jnp.dot(
                ds, q_rows, preferred_element_type=f32
            )
            return dq + jnp.dot(cols_ref[kb], ds, preferred_element_type=f32)

        diagonal = first // BLOCK_K
        mid = jnp.minimum(mid_ref[step], diagonal)
        dq = jnp.zeros((HEAD_DIM, BLOCK_Q), f32)
        dq = lax.fori_loop(lo_ref[step], mid, functools.partial(body, True), dq)
        dq = lax.fori_loop(mid, diagonal, functools.partial(body, False), dq)
        last = (first + BLOCK_Q + BLOCK_K - 1) // BLOCK_K
        dq = lax.fori_loop(diagonal, last, functools.partial(body, True), dq)
        dq_ref[0] = (dq * SCALE).astype(bf16)

    @pl.when(step >= n_steps)
    def _():
        kb = jnp.maximum(step - n_steps, 0)
        at = pl.ds(pl.multiple_of(kb * BLOCK_K, BLOCK_K), BLOCK_K)
        dkv_ref[0, 0] = acc_ref[at, :].astype(bf16).T


def attention_specs(qkv, far, tok_rows, block_q):
    hb, depth, block_rows = qkv.shape
    subs = block_rows // block_q
    pieces = block_q // tok_rows

    def wrap(index):
        return lambda i, *_: index(i)

    q_spec = lambda cap: pl.BlockSpec((1, HEAD_DIM, block_q), wrap(lambda i: (cap(i) // subs, 0, cap(i) % subs)))
    row_spec = lambda cap: pl.BlockSpec((1, 1, block_q), wrap(lambda i: (cap(i) // subs, 0, cap(i) % subs)))
    piece_spec = lambda cap: pl.BlockSpec(
        (pieces, 1, HEAD_DIM, tok_rows), wrap(lambda i: (cap(i) % subs, cap(i) // subs, 0, 0))
    )
    own_spec = pl.BlockSpec((hb, depth, block_rows), wrap(lambda i: (0, 0, 0)), pipeline_mode=pl.Buffered(1))
    far_spec = pl.BlockSpec(far.shape, wrap(lambda i: (0, 0, 0, 0)), pipeline_mode=pl.Buffered(1))
    return q_spec, row_spec, piece_spec, own_spec, far_spec


def padded_cost(products, queries, keys):
    pairs = queries * keys // 2
    return pl.CostEstimate(flops=products * 2 * 256 * pairs, transcendentals=pairs, bytes_accessed=8 * keys * HEAD_DIM)


def attention_forward(bounds, qkv, far, starts, n_head, tok_rows):
    hb, _, block_rows = qkv.shape
    queries = hb * block_rows
    keys = queries * (far.shape[0] + 1)
    q_spec, row_spec, piece_spec, own_spec, far_spec = attention_specs(qkv, far, tok_rows, FORWARD_Q)
    same = lambda i: i
    return pl.pallas_call(
        forward_kernel,
        grid_spec=pltpu.PrefetchScalarGridSpec(
            num_scalar_prefetch=4,
            grid=(queries // FORWARD_Q,),
            in_specs=[q_spec(same), own_spec, far_spec, row_spec(same)],
            out_specs=[piece_spec(same), q_spec(same), row_spec(same)],
            scratch_shapes=[
                pltpu.VMEM((keys, 2 * HEAD_DIM), bf16),
                pltpu.VMEM((keys // BLOCK_K, HEAD_DIM, BLOCK_K), bf16),
            ],
        ),
        out_shape=[
            jax.ShapeDtypeStruct((n_head, hb, HEAD_DIM, tok_rows), bf16),
            jax.ShapeDtypeStruct((hb, HEAD_DIM, block_rows), f32),
            jax.ShapeDtypeStruct((hb, 1, block_rows), f32),
        ],
        compiler_params=pltpu.CompilerParams(vmem_limit_bytes=VMEM_BYTES),
        cost_estimate=padded_cost(2, queries, keys),
        name="attention_forward",
    )(*bounds, qkv, qkv, far, starts)


def attention_backward(bounds, qkv, far, starts, do, wide, lse):
    hb, _, block_rows = qkv.shape
    n_rest = far.shape[0] + 1
    queries = hb * block_rows
    keys = queries * n_rest
    n_kb = keys // BLOCK_K
    subs = block_rows // BLOCK_K
    n_steps = queries // BLOCK_Q
    q_spec, row_spec, piece_spec, own_spec, far_spec = attention_specs(qkv, far, do.shape[3], BLOCK_Q)
    cap = lambda i: jnp.minimum(i, n_steps - 1)

    def place(i, *_):
        kb = jnp.maximum(i - n_steps, 0)
        return (kb // subs % n_rest, kb // subs // n_rest, 0, kb % subs)

    return pl.pallas_call(
        functools.partial(backward_kernel, n_steps),
        grid_spec=pltpu.PrefetchScalarGridSpec(
            num_scalar_prefetch=4,
            grid=(n_steps + n_kb,),
            in_specs=[q_spec(cap), own_spec, far_spec, row_spec(cap), piece_spec(cap), q_spec(cap), row_spec(cap)],
            out_specs=[q_spec(cap), pl.BlockSpec((1, 1, 2 * HEAD_DIM, BLOCK_K), place)],
            scratch_shapes=[
                pltpu.VMEM((keys, 2 * HEAD_DIM), bf16),
                pltpu.VMEM((n_kb, HEAD_DIM, BLOCK_K), bf16),
                pltpu.VMEM((keys, 2 * HEAD_DIM), f32),
            ],
        ),
        out_shape=[
            jax.ShapeDtypeStruct((hb, HEAD_DIM, block_rows), bf16),
            jax.ShapeDtypeStruct((n_rest, hb, 2 * HEAD_DIM, block_rows), bf16),
        ],
        compiler_params=pltpu.CompilerParams(vmem_limit_bytes=VMEM_BYTES),
        cost_estimate=padded_cost(5, queries, keys),
        name="attention_backward",
    )(*bounds, qkv, qkv, far, starts, do, wide, lse)


def on_device(
    tokens,
    cotangent,
    segment,
    norm_gain,
    norm_shift,
    in_weight,
    query_bias,
    value_bias,
    out_weight,
    out_bias,
    post_gain,
    post_shift,
    up_weight,
    up_bias,
    down_weight,
    down_bias,
):
    n_head, n_u, n_v, n_rest = (lax.axis_size(a) for a in ALL)
    hb = n_u * n_v
    n_blk = hb * n_rest
    n_all = n_head * n_blk
    me_head, me_u, me_v, me_rest = (lax.axis_index(a) for a in ALL)
    me_blk = (me_u * n_v + me_v) * n_rest + me_rest
    tok_rows, width = tokens.shape
    block_rows = tok_rows * n_head
    length = segment.shape[0]
    w_rows = in_weight.shape[0]
    group = 3 * hb * HEAD_DIM

    chips = n_head * hb
    f_rows = down_weight.shape[0] // 2

    n_up = up_bias.shape[0] // w_rows
    vectors = [norm_gain, norm_shift, query_bias, value_bias, out_bias, post_gain, post_shift, down_bias]
    vectors = jnp.concatenate([jnp.stack(vectors), up_bias.reshape(n_up, w_rows)]).T
    vectors = jnp.pad(vectors, ((0, 0), (0, 128 - vectors.shape[1])))
    cols = in_weight.reshape(w_rows, 3, n_head, hb, HEAD_DIM).transpose(2, 0, 3, 1, 4).reshape(n_head, w_rows, group)
    cols = jnp.concatenate([cols, jnp.broadcast_to(vectors, (n_head, w_rows, 128))], axis=2)
    cols = exchange_axis(cols, "head")
    cols, tokens = lax.optimization_barrier((cols, tokens))

    units = up_weight.reshape(w_rows, chips, n_rest, 2, f_rows).transpose(2, 0, 3, 1, 4)
    f_half = chips * f_rows
    up_cols = exchange_axis(units.reshape(n_rest, w_rows, 2 * f_half), "rest").reshape(n_rest * w_rows, 2 * f_half)
    out_rows = gather_axis(out_weight, "rest").reshape(n_rest * w_rows, width)
    down_rows = down_weight.reshape(2, f_rows, width)
    if f_rows == n_rest * w_rows:
        joint = jnp.concatenate([up_cols, down_rows[0], down_rows[1], out_rows], axis=1)
        joint = lax.all_gather(joint, ("head", "u", "v"), axis=0, tiled=True)
        w_up = joint[:, : 2 * f_half]
        w_down = [joint[:, 2 * f_half + i * width : 2 * f_half + (i + 1) * width] for i in range(2)]
        w_out = joint[:, 2 * f_half + 2 * width :]
    else:
        w_up, w_down_a, w_down_b, w_out = (
            lax.all_gather(w, ("head", "u", "v"), axis=0, tiled=True)
            for w in (up_cols, down_rows[0], down_rows[1], out_rows)
        )
        w_down = [w_down_a, w_down_b]

    cols = gather_axis(gather_axis(cols, "v"), "u")
    sent = [tokens] + [shifted(tokens, "head", k) for k in range(1, n_head)]
    sent, cols = lax.optimization_barrier((sent, cols))
    cols = gather_axis(cols, "rest")
    cols = cols.transpose(3, 1, 2, 0, 4, 5).reshape(width, group + 128)
    w_in = cols[:, :group]
    vectors = cols[:, group : group + 8 + n_up].T.astype(f32)
    gain_a, shift_a, bias_q, bias_v, bias_out, gain_b, shift_b, bias_down = (vectors[i] for i in range(8))
    bias_up = vectors[8:].reshape(n_up, n_all, w_rows).transpose(1, 0, 2)

    rows_all = jnp.zeros((n_head, tok_rows, width), bf16)
    for k in range(n_head):
        rows_all = put(rows_all, sent[k], (me_head - k) % n_head)
    rows_all = rows_all.reshape(block_rows, width)

    rows_all = rows_all.astype(f32)
    normed, unit_all, inverse_all = norm_forward(rows_all, gain_a, shift_a)
    normed_low = normed.astype(bf16)
    group_bias = jnp.stack([bias_q, jnp.zeros_like(bias_q), bias_v]).reshape(3, n_head, hb, HEAD_DIM)
    group_bias = lax.dynamic_index_in_dim(group_bias, me_head, 1, keepdims=False).transpose(1, 0, 2).reshape(group, 1)
    projected = lax.dot_general(w_in, normed_low, (((0,), (1,)), ((), ())), preferred_element_type=f32)
    projected = (projected + group_bias).astype(bf16)
    qkv = lax.all_to_all(
        projected.reshape(hb, 3 * HEAD_DIM, block_rows), ("u", "v"), split_axis=0, concat_axis=0, tiled=True
    )
    far = [shifted(qkv, "rest", k) for k in range(1, n_rest)]
    far = jnp.stack(far) if n_rest > 2 else far[0][None]

    doc_start = jnp.zeros_like(segment)
    for doc in range(1, DOCS):
        first = jnp.sum((segment < doc).astype(jnp.int32))
        doc_start = jnp.where(segment == doc, first, doc_start)
    starts = lax.dynamic_index_in_dim(doc_start.reshape(hb, n_rest, block_rows), me_rest, 1, keepdims=False)

    def bounds(block_q):
        of_block = starts.reshape(-1, block_q)
        lo = of_block[:, 0] // BLOCK_K
        mid = (of_block[:, -1] + BLOCK_K - 1) // BLOCK_K
        q_first = (jnp.arange(hb, dtype=jnp.int32)[:, None] * n_rest + me_rest) * block_rows
        q_first = (q_first + jnp.arange(block_rows // block_q, dtype=jnp.int32)[None] * block_q).reshape(-1)
        return (lo, mid, q_first, me_rest.astype(jnp.int32).reshape(1))

    forward_bounds, backward_bounds = bounds(FORWARD_Q), bounds(BLOCK_Q)
    starts = starts.reshape(hb, 1, block_rows)

    attended, wide, lse = attention_forward(forward_bounds, qkv, far, starts, n_head, tok_rows)
    back = lax.all_to_all(
        attended.reshape(HEADS, HEAD_DIM, tok_rows), ("head", "u", "v"), split_axis=0, concat_axis=0, tiled=True
    ).reshape(width, tok_rows)

    rows = tokens.astype(f32)
    branch = lax.dot_general(back, w_out, (((0,), (0,)), ((), ())), preferred_element_type=f32) + bias_out
    middle = rows + branch
    hidden_in, unit_mid, inverse_mid = norm_forward(middle, gain_b, shift_b)
    hidden_low = hidden_in.astype(bf16)
    hidden_all = gather_axis(hidden_low, "rest").reshape(n_rest * tok_rows, width)
    cot_all = gather_axis(cotangent, "rest").reshape(n_rest * tok_rows, width)
    bias_units = lax.dynamic_index_in_dim(bias_up.reshape(chips, n_rest, 2, f_rows), me_rest, 1, keepdims=False)
    bias_units = bias_units.transpose(1, 0, 2).reshape(-1)
    pre = jnp.dot(hidden_all, w_up, preferred_element_type=f32) + bias_units
    act, slope = gelu_parts(pre)
    act_low = act.astype(bf16)
    acts = act_low[:, :f_half], act_low[:, f_half:]
    down = jnp.dot(acts[0], w_down[0], preferred_element_type=f32)
    down = down + jnp.dot(acts[1], w_down[1], preferred_element_type=f32)
    down = reduce_axis(down.reshape(n_rest, tok_rows, width), "rest")
    output = (middle + down + bias_down).astype(bf16)
    grad_out = cotangent.astype(f32)
    grad_act = jnp.concatenate(
        [jnp.einsum("td,fd->tf", cot_all, w, preferred_element_type=f32) for w in w_down], axis=1
    )
    grad_pre = (grad_act * slope).astype(bf16)
    grad_hidden = jnp.einsum("tf,df->td", grad_pre, w_up, preferred_element_type=f32)
    grad_hidden = reduce_axis(grad_hidden.reshape(n_rest, tok_rows, width), "rest")
    grad_middle = grad_out + norm_inner(grad_hidden, unit_mid, inverse_mid, gain_b)
    grad_branch = grad_middle.astype(bf16)
    grad_back = lax.dot_general(w_out, grad_branch, (((1,), (1,)), ((), ())), preferred_element_type=f32).astype(bf16)
    grad_heads = lax.all_to_all(
        grad_back.reshape(HEADS, HEAD_DIM, tok_rows), ("head", "u", "v"), split_axis=0, concat_axis=0, tiled=True
    ).reshape(n_head, hb, HEAD_DIM, tok_rows)

    down_grads = [jnp.einsum("tf,td->fd", a, cot_all, preferred_element_type=f32).astype(bf16) for a in acts]
    up_grad = jnp.einsum("td,tf->df", hidden_all, grad_pre, preferred_element_type=f32).astype(bf16)
    out_grad = jnp.einsum("dt,te->de", back, grad_branch, preferred_element_type=f32).astype(bf16)
    out_grad = out_grad.reshape(chips, n_rest, w_rows, width).transpose(1, 0, 2, 3)
    out_grad = reduce_axis(out_grad, "rest").astype(bf16)
    up_grad = up_grad.reshape(n_head, n_u, n_v, -1, 2 * f_half)
    out_grad = out_grad.reshape(n_head, n_u, n_v, -1, width)
    down_a, down_b = (x.reshape(n_head, n_u, n_v, f_rows, width) for x in down_grads)
    sums = [
        jnp.sum(grad_branch.astype(f32), axis=0),
        jnp.sum(grad_hidden * unit_mid, axis=0),
        jnp.sum(grad_hidden, axis=0),
        jnp.sum(grad_out, axis=0),
    ]
    unit_sum = jnp.sum(grad_pre.astype(f32), axis=0)
    unit_sum = unit_sum.reshape(2, chips, f_rows).transpose(1, 0, 2).reshape(chips, 1, 2 * f_rows)
    unit_sum = jnp.where((jnp.arange(n_rest) == me_rest)[:, None], unit_sum, 0.0).reshape(n_head, n_blk, n_up, w_rows)

    down_a = jnp.concatenate([down_a, out_grad], axis=3)
    grad_heads, up_grad, down_a, down_b = lax.optimization_barrier((grad_heads, up_grad, down_a, down_b))
    begun = [reduce_begin(up_grad, "u", 1), reduce_begin(down_a, "v", 2), reduce_begin(down_b, "head")]

    dq, dkv = attention_backward(backward_bounds, qkv, far, starts, grad_heads, wide, lse)
    dq, dkv, begun = lax.optimization_barrier((dq, dkv, begun))
    up_grad, down_a, down_b = (reduce_end(x).astype(bf16) for x in begun)
    dkv = reduce_axis(dkv, "rest").astype(bf16)
    grad_proj = lax.all_to_all(
        jnp.concatenate([dq, dkv], axis=1), ("u", "v"), split_axis=0, concat_axis=0, tiled=True
    ).reshape(group, block_rows)

    grad_normed = lax.dot_general(grad_proj, w_in, (((0,), (1,)), ((), ())), preferred_element_type=f32)
    tokens_low = grad_normed.astype(bf16).reshape(n_head, tok_rows, width)
    tokens_low, grad_proj = lax.optimization_barrier((tokens_low, grad_proj))
    begun = reduce_begin(tokens_low, "head")

    in_grad = lax.dot_general(normed_low, grad_proj, (((0,), (1,)), ((), ())), preferred_element_type=f32)
    rowed = lambda x: x.reshape(n_head, n_blk, w_rows)
    gain_grad = rowed(jnp.sum(grad_normed * unit_all, axis=0))
    shift_grad = rowed(jnp.sum(grad_normed, axis=0))
    col_sum = jnp.sum(grad_proj.astype(f32), axis=1).reshape(hb, 3, HEAD_DIM)
    mine = (jnp.arange(n_head) == me_head)[:, None, None]
    query_sum = jnp.where(mine, col_sum[:, 0].reshape(1, n_blk, w_rows), 0.0)
    value_sum = jnp.where(mine, col_sum[:, 2].reshape(1, n_blk, w_rows), 0.0)
    extra = jnp.stack([gain_grad, shift_grad, query_sum, value_sum, *(rowed(x) for x in sums)], axis=2)
    extra = jnp.concatenate([extra, unit_sum], axis=2)
    n_extra = extra.shape[2]
    extra = jnp.pad(extra.transpose(0, 1, 3, 2), ((0, 0), (0, 0), (0, 0), (0, width - group - n_extra)))
    joined = jnp.concatenate([in_grad.reshape(n_head, n_blk, w_rows, group), extra], axis=-1).astype(bf16)
    joined = joined.reshape(n_head, n_u, n_v, n_rest, w_rows, width)
    early, begun = begun[:2], begun[2:]
    early, joined, up_grad, down_a, down_b = lax.optimization_barrier((early, joined, up_grad, down_a, down_b))
    joined = reduce_axis(joined, "rest", 3).astype(bf16)
    joined = reduce_axis(joined, "u", 1).astype(bf16)
    joined = reduce_axis(joined, "v", 1).astype(bf16)

    up_grad = reduce_axis(up_grad, "v", 1).astype(bf16)
    n_rows = n_head * down_a.shape[2]
    down_a = down_a.transpose(1, 0, 2, 3).reshape(n_u, n_rows, width)
    down_a = reduce_axis(jnp.concatenate([down_a, down_b.reshape(n_u, -1, width)], axis=1), "u").astype(bf16)
    down_b = down_a[n_rows:].reshape(n_v, f_rows, width)
    down_a = down_a[:n_rows].reshape(n_head, -1, width)

    begun, joined, up_grad, down_a, down_b = lax.optimization_barrier((begun, joined, up_grad, down_a, down_b))
    split = down_a.shape[1]
    last = reduce_begin(jnp.concatenate([down_a, joined], axis=1), "head")
    down_b = reduce_axis(down_b, "v")
    up_grad = reduce_axis(up_grad, "head").astype(bf16).reshape(n_rest, w_rows, 2 * f_half)
    up_grad = exchange_axis(up_grad, "rest").astype(f32)
    down_a = reduce_end([x[:split] for x in last])
    out_weight_grad = down_a[f_rows:]
    down_weight_grad = jnp.concatenate([down_a[:f_rows], down_b], axis=0)
    joined = jnp.zeros((n_head, w_rows, width), bf16)
    for k in range(n_head):
        joined = put(joined, last[k][split:], (me_head - k) % n_head)
    joined = joined.astype(f32)
    up_weight_grad = up_grad.reshape(n_rest, w_rows, 2, chips, f_rows).transpose(1, 3, 0, 2, 4).reshape(w_rows, -1)
    in_weight_grad = joined[:, :, :group].reshape(n_head, w_rows, hb, 3, HEAD_DIM).transpose(1, 3, 0, 2, 4)
    in_weight_grad = in_weight_grad.reshape(w_rows, 3 * width)
    extra = jnp.sum(joined[:, :, group : group + n_extra], axis=0).T
    norm_gain_grad, norm_shift_grad, query_bias_grad, value_bias_grad = (extra[i] for i in range(4))
    out_bias_grad, post_gain_grad, post_shift_grad, down_bias_grad = (extra[i] for i in range(4, 8))
    up_bias_grad = extra[8:].reshape(-1)

    grad_tokens = reduce_end(early + begun)
    unit_in = lax.dynamic_index_in_dim(unit_all.reshape(n_head, tok_rows, width), me_head, 0, keepdims=False)
    inverse_in = lax.dynamic_index_in_dim(inverse_all.reshape(n_head, tok_rows, 1), me_head, 0, keepdims=False)
    tokens_grad = (grad_middle + norm_inner(grad_tokens, unit_in, inverse_in, gain_a)).astype(bf16)
    return (
        output,
        tokens_grad,
        norm_gain_grad,
        norm_shift_grad,
        in_weight_grad,
        query_bias_grad,
        value_bias_grad,
        out_weight_grad,
        out_bias_grad,
        post_gain_grad,
        post_shift_grad,
        up_weight_grad,
        up_bias_grad,
        down_weight_grad,
        down_bias_grad,
    )


def solution(mesh):
    n_head, n_blk = mesh.shape["head"], mesh.shape["blk"]
    hb = HEADS // n_head
    n_u = 2 if hb % 2 == 0 else 1
    fine = Mesh(mesh.devices.reshape(n_head, n_u, hb // n_u, n_blk // hb), ALL)
    tok = P(("u", "v", "rest", "head"), None)
    vec = P(ALL)
    mat = P(ALL, None)
    return jax.shard_map(
        on_device,
        mesh=fine,
        in_specs=(tok, tok, P(), vec, vec, mat, vec, vec, mat, vec, vec, vec, mat, vec, mat, vec),
        out_specs=(tok, tok, vec, vec, mat, vec, vec, mat, vec, vec, vec, mat, vec, mat, vec),
        check_vma=False,
    )
```

```python
import functools

import jax
import jax.numpy as jnp
from jax import lax
from jax.experimental import pallas as pl
from jax.experimental.pallas import tpu as pltpu
from jax.sharding import Mesh
from jax.sharding import PartitionSpec as P

HEADS = 16
HEAD_DIM = 64
DOCS = 4
FORWARD_Q = 1024
BLOCK_Q = 512
BLOCK_K = 512
VMEM_BYTES = 56 * 1024 * 1024

EPS = 1e-05
NEGATIVE = -1e30
GELU_C = 0.7978845608028654
SCALE = HEAD_DIM ** (-0.5)
ALL = ("head", "u", "v", "rest")
f32 = jnp.float32
bf16 = jnp.bfloat16


def norm_forward(rows, gain, shift):
    center = rows - jnp.mean(rows, axis=-1, keepdims=True)
    var = jnp.mean(center * center, axis=-1, keepdims=True)
    inverse = lax.rsqrt(var + EPS)
    unit = center * inverse
    return (unit * gain + shift, unit, inverse)


def norm_inner(grad, unit, inverse, gain):
    scaled = grad * gain
    inner = (
        scaled
        - jnp.mean(scaled, axis=-1, keepdims=True)
        - unit * jnp.mean(scaled * unit, axis=-1, keepdims=True)
    )
    return inverse * inner


def gelu_parts(pre):
    cubic = pre * pre * pre
    tangent = jnp.tanh(GELU_C * (pre + 0.044715 * cubic))
    value = 0.5 * pre * (1.0 + tangent)
    slope = 0.5 * (1.0 + tangent) + 0.5 * pre * (1.0 - tangent * tangent) * GELU_C * (
        1.0 + 3.0 * 0.044715 * pre * pre
    )
    return (value, slope)


def shifted(x, axis, k):
    n = lax.axis_size(axis)
    return lax.ppermute(x, axis, [(i, (i + k) % n) for i in range(n)])


def put(buffer, x, index):
    return lax.dynamic_update_index_in_dim(buffer, x, index, 0)


def gather_axis(x, axis):
    n = lax.axis_size(axis)
    if n == 1:
        return x[None]
    me = lax.axis_index(axis)
    out = put(jnp.zeros((n,) + x.shape, x.dtype), x, me)
    for k in range(1, n):
        out = put(out, shifted(x, axis, k), (me - k) % n)
    return out


def reduce_begin(x, axis, dim=0):
    n = lax.axis_size(axis)
    if n == 1:
        return [lax.index_in_dim(x, 0, dim, keepdims=False)]
    me = lax.axis_index(axis)
    pieces = [lax.dynamic_index_in_dim(x, (me + k) % n, dim, keepdims=False) for k in range(n)]
    return pieces[:1] + [shifted(pieces[k], axis, k) for k in range(1, n)]


def reduce_end(pieces):
    total = pieces[0].astype(f32)
    for piece in pieces[1:]:
        total = total + piece.astype(f32)
    return total


def reduce_axis(x, axis, dim=0):
    return reduce_end(reduce_begin(x, axis, dim))


def exchange_axis(x, axis):
    n = lax.axis_size(axis)
    if n == 1:
        return x
    me = lax.axis_index(axis)
    mine = lax.dynamic_index_in_dim(x, me, 0, keepdims=False)
    out = put(jnp.zeros_like(x), mine, me)
    for k in range(1, n):
        piece = lax.dynamic_index_in_dim(x, (me + k) % n, 0, keepdims=False)
        out = put(out, shifted(piece, axis, k), (me - k) % n)
    return out


def allowed_keys(kb, starts, pos):
    t = kb * BLOCK_K + lax.broadcasted_iota(jnp.int32, (BLOCK_K, pos.shape[1]), 0)
    return (t >= starts) & (t <= pos)


def lay_rows(me, own_ref, far_ref, rows_ref, cols_ref, first):
    hb, _, block_rows = own_ref.shape
    n_rest = far_ref.shape[0] + 1
    subs = block_rows // BLOCK_K

    def lay(read, b, rest):
        for sub in range(subs):
            kb = (b * n_rest + rest) * subs + sub
            block = read(b)[:, sub * BLOCK_K : (sub + 1) * BLOCK_K]
            rows_ref[pl.ds(pl.multiple_of(kb * BLOCK_K, BLOCK_K), BLOCK_K), :] = block[HEAD_DIM:].T
            cols_ref[kb] = block[first : first + HEAD_DIM]

    def each(b, _):
        lay(lambda b: own_ref[b], b, me)
        for k in range(1, n_rest):
            lay(lambda b: far_ref[k - 1, b], b, (me - k) % n_rest)
        return 0

    lax.fori_loop(0, hb, each, 0)


def forward_kernel(
    lo_ref, mid_ref, q0_ref, me_ref, q_ref, own_ref, far_ref, start_ref, o_ref, wide_ref, lse_ref, rows_ref, cols_ref
):
    step = pl.program_id(0)

    @pl.when(step == 0)
    def _():
        lay_rows(me_ref[0], own_ref, far_ref, rows_ref, cols_ref, 2 * HEAD_DIM)

    first = q0_ref[step]
    q = q_ref[0] * jnp.asarray(SCALE, bf16)
    q_pad = jnp.concatenate([q, jnp.zeros_like(q)], axis=0)
    starts = start_ref[0]
    pos = first + lax.broadcasted_iota(jnp.int32, (1, FORWARD_Q), 1)

    def body(masked, kb, carry):
        top, total, acc = carry
        rows = rows_ref[pl.ds(pl.multiple_of(kb * BLOCK_K, BLOCK_K), BLOCK_K), :]
        s = jnp.dot(rows, q_pad, preferred_element_type=f32)
        if masked:
            s = jnp.where(allowed_keys(kb, starts, pos), s, NEGATIVE)
        new_top = jnp.maximum(top, jnp.max(s, axis=0, keepdims=True))
        p = jnp.exp(s - new_top)
        factor = jnp.exp(top - new_top)
        values = cols_ref[kb]
        acc = acc * factor + jnp.dot(values, p.astype(bf16), preferred_element_type=f32)
        return (new_top, total * factor + jnp.sum(p, axis=0, keepdims=True), acc)

    diagonal = first // BLOCK_K
    mid = jnp.minimum(mid_ref[step], diagonal)
    carry = (
        jnp.full((1, FORWARD_Q), NEGATIVE, f32),
        jnp.zeros((1, FORWARD_Q), f32),
        jnp.zeros((HEAD_DIM, FORWARD_Q), f32),
    )
    carry = lax.fori_loop(lo_ref[step], mid, functools.partial(body, True), carry)
    carry = lax.fori_loop(mid, diagonal, functools.partial(body, False), carry)
    last = (first + FORWARD_Q + BLOCK_K - 1) // BLOCK_K
    top, total, acc = lax.fori_loop(diagonal, last, functools.partial(body, True), carry)
    out = acc / total
    wide_ref[0] = out
    lse_ref[0] = top + jnp.log(total)
    low = out.astype(bf16)
    piece = o_ref.shape[3]
    for i in range(o_ref.shape[0]):
        o_ref[i, 0] = low[:, i * piece : (i + 1) * piece]


def backward_kernel(
    n_steps,
    lo_ref,
    mid_ref,
    q0_ref,
    me_ref,
    q_ref,
    own_ref,
    far_ref,
    start_ref,
    do_ref,
    wide_ref,
    lse_ref,
    dq_ref,
    dkv_ref,
    rows_ref,
    cols_ref,
    acc_ref,
):
    step = pl.program_id(0)

    @pl.when(step == 0)
    def _():
        lay_rows(me_ref[0], own_ref, far_ref, rows_ref, cols_ref, HEAD_DIM)
        acc_ref[...] = jnp.zeros_like(acc_ref)

    @pl.when(step < n_steps)
    def _():
        first = q0_ref[step]
        q = q_ref[0] * jnp.asarray(SCALE, bf16)
        do = jnp.concatenate([do_ref[i, 0] for i in range(do_ref.shape[0])], axis=1)
        zero = jnp.zeros_like(q)
        q_pad = jnp.concatenate([q, zero], axis=0)
        do_pad = jnp.concatenate([zero, do], axis=0)
        q_rows = q_pad.T
        do_rows = do_pad.T
        starts = start_ref[0]
        lse = lse_ref[0]
        delta = jnp.sum(do.astype(f32) * wide_ref[0], axis=0, keepdims=True)
        pos = first + lax.broadcasted_iota(jnp.int32, (1, BLOCK_Q), 1)

        def body(masked, kb, dq):
            at = pl.ds(pl.multiple_of(kb * BLOCK_K, BLOCK_K), BLOCK_K)
            rows = rows_ref[at, :]
            s = jnp.dot(rows, q_pad, preferred_element_type=f32)
            p = jnp.exp(s - lse)
            if masked:
                p = jnp.where(allowed_keys(kb, starts, pos), p, 0.0)
            dp = jnp.dot(rows, do_pad, preferred_element_type=f32)
            ds = (p * (dp - delta)).astype(bf16)
            acc_ref[at, :] += jnp.dot(p.astype(bf16), do_rows, preferred_element_type=f32) + jnp.dot(
                ds, q_rows, preferred_element_type=f32
            )
            return dq + jnp.dot(cols_ref[kb], ds, preferred_element_type=f32)

        diagonal = first // BLOCK_K
        mid = jnp.minimum(mid_ref[step], diagonal)
        dq = jnp.zeros((HEAD_DIM, BLOCK_Q), f32)
        dq = lax.fori_loop(lo_ref[step], mid, functools.partial(body, True), dq)
        dq = lax.fori_loop(mid, diagonal, functools.partial(body, False), dq)
        last = (first + BLOCK_Q + BLOCK_K - 1) // BLOCK_K
        dq = lax.fori_loop(diagonal, last, functools.partial(body, True), dq)
        dq_ref[0] = (dq * SCALE).astype(bf16)

    @pl.when(step >= n_steps)
    def _():
        kb = jnp.maximum(step - n_steps, 0)
        at = pl.ds(pl.multiple_of(kb * BLOCK_K, BLOCK_K), BLOCK_K)
        dkv_ref[0, 0] = acc_ref[at, :].astype(bf16).T


def attention_specs(qkv, far, tok_rows, block_q):
    hb, depth, block_rows = qkv.shape
    subs = block_rows // block_q
    pieces = block_q // tok_rows

    def wrap(index):
        return lambda i, *_: index(i)

    q_spec = lambda cap: pl.BlockSpec((1, HEAD_DIM, block_q), wrap(lambda i: (cap(i) // subs, 0, cap(i) % subs)))
    row_spec = lambda cap: pl.BlockSpec((1, 1, block_q), wrap(lambda i: (cap(i) // subs, 0, cap(i) % subs)))
    piece_spec = lambda cap: pl.BlockSpec(
        (pieces, 1, HEAD_DIM, tok_rows), wrap(lambda i: (cap(i) % subs, cap(i) // subs, 0, 0))
    )
    own_spec = pl.BlockSpec((hb, depth, block_rows), wrap(lambda i: (0, 0, 0)), pipeline_mode=pl.Buffered(1))
    far_spec = pl.BlockSpec(far.shape, wrap(lambda i: (0, 0, 0, 0)), pipeline_mode=pl.Buffered(1))
    return q_spec, row_spec, piece_spec, own_spec, far_spec


def padded_cost(products, queries, keys):
    pairs = queries * keys // 2
    return pl.CostEstimate(flops=products * 2 * 256 * pairs, transcendentals=pairs, bytes_accessed=8 * keys * HEAD_DIM)


def attention_forward(bounds, qkv, far, starts, n_head, tok_rows):
    hb, _, block_rows = qkv.shape
    queries = hb * block_rows
    keys = queries * (far.shape[0] + 1)
    q_spec, row_spec, piece_spec, own_spec, far_spec = attention_specs(qkv, far, tok_rows, FORWARD_Q)
    same = lambda i: i
    return pl.pallas_call(
        forward_kernel,
        grid_spec=pltpu.PrefetchScalarGridSpec(
            num_scalar_prefetch=4,
            grid=(queries // FORWARD_Q,),
            in_specs=[q_spec(same), own_spec, far_spec, row_spec(same)],
            out_specs=[piece_spec(same), q_spec(same), row_spec(same)],
            scratch_shapes=[
                pltpu.VMEM((keys, 2 * HEAD_DIM), bf16),
                pltpu.VMEM((keys // BLOCK_K, HEAD_DIM, BLOCK_K), bf16),
            ],
        ),
        out_shape=[
            jax.ShapeDtypeStruct((n_head, hb, HEAD_DIM, tok_rows), bf16),
            jax.ShapeDtypeStruct((hb, HEAD_DIM, block_rows), f32),
            jax.ShapeDtypeStruct((hb, 1, block_rows), f32),
        ],
        compiler_params=pltpu.CompilerParams(vmem_limit_bytes=VMEM_BYTES),
        cost_estimate=padded_cost(2, queries, keys),
        name="attention_forward",
    )(*bounds, qkv, qkv, far, starts)


def attention_backward(bounds, qkv, far, starts, do, wide, lse):
    hb, _, block_rows = qkv.shape
    n_rest = far.shape[0] + 1
    queries = hb * block_rows
    keys = queries * n_rest
    n_kb = keys // BLOCK_K
    subs = block_rows // BLOCK_K
    n_steps = queries // BLOCK_Q
    q_spec, row_spec, piece_spec, own_spec, far_spec = attention_specs(qkv, far, do.shape[3], BLOCK_Q)
    cap = lambda i: jnp.minimum(i, n_steps - 1)

    def place(i, *_):
        kb = jnp.maximum(i - n_steps, 0)
        return (kb // subs % n_rest, kb // subs // n_rest, 0, kb % subs)

    return pl.pallas_call(
        functools.partial(backward_kernel, n_steps),
        grid_spec=pltpu.PrefetchScalarGridSpec(
            num_scalar_prefetch=4,
            grid=(n_steps + n_kb,),
            in_specs=[q_spec(cap), own_spec, far_spec, row_spec(cap), piece_spec(cap), q_spec(cap), row_spec(cap)],
            out_specs=[q_spec(cap), pl.BlockSpec((1, 1, 2 * HEAD_DIM, BLOCK_K), place)],
            scratch_shapes=[
                pltpu.VMEM((keys, 2 * HEAD_DIM), bf16),
                pltpu.VMEM((n_kb, HEAD_DIM, BLOCK_K), bf16),
                pltpu.VMEM((keys, 2 * HEAD_DIM), f32),
            ],
        ),
        out_shape=[
            jax.ShapeDtypeStruct((hb, HEAD_DIM, block_rows), bf16),
            jax.ShapeDtypeStruct((n_rest, hb, 2 * HEAD_DIM, block_rows), bf16),
        ],
        compiler_params=pltpu.CompilerParams(vmem_limit_bytes=VMEM_BYTES),
        cost_estimate=padded_cost(5, queries, keys),
        name="attention_backward",
    )(*bounds, qkv, qkv, far, starts, do, wide, lse)


def on_device(
    tokens,
    cotangent,
    segment,
    norm_gain,
    norm_shift,
    in_weight,
    query_bias,
    value_bias,
    out_weight,
    out_bias,
    post_gain,
    post_shift,
    up_weight,
    up_bias,
    down_weight,
    down_bias,
):
    n_head, n_u, n_v, n_rest = (lax.axis_size(a) for a in ALL)
    hb = n_u * n_v
    n_blk = hb * n_rest
    n_all = n_head * n_blk
    me_head, me_u, me_v, me_rest = (lax.axis_index(a) for a in ALL)
    me_blk = (me_u * n_v + me_v) * n_rest + me_rest
    tok_rows, width = tokens.shape
    block_rows = tok_rows * n_head
    length = segment.shape[0]
    w_rows = in_weight.shape[0]
    group = 3 * hb * HEAD_DIM

    chips = n_head * hb
    f_rows = down_weight.shape[0] // 2

    n_up = up_bias.shape[0] // w_rows
    vectors = [norm_gain, norm_shift, query_bias, value_bias, out_bias, post_gain, post_shift, down_bias]
    vectors = jnp.concatenate([jnp.stack(vectors), up_bias.reshape(n_up, w_rows)]).T
    vectors = jnp.pad(vectors, ((0, 0), (0, 128 - vectors.shape[1])))
    cols = in_weight.reshape(w_rows, 3, n_head, hb, HEAD_DIM).transpose(2, 0, 3, 1, 4).reshape(n_head, w_rows, group)
    cols = jnp.concatenate([cols, jnp.broadcast_to(vectors, (n_head, w_rows, 128))], axis=2)
    cols = exchange_axis(cols, "head")
    cols, tokens = lax.optimization_barrier((cols, tokens))

    units = up_weight.reshape(w_rows, chips, n_rest, 2, f_rows).transpose(2, 0, 3, 1, 4)
    f_half = chips * f_rows
    up_cols = exchange_axis(units.reshape(n_rest, w_rows, 2 * f_half), "rest").reshape(n_rest * w_rows, 2 * f_half)
    out_rows = gather_axis(out_weight, "rest").reshape(n_rest * w_rows, width)
    down_rows = down_weight.reshape(2, f_rows, width)
    if f_rows == n_rest * w_rows:
        joint = jnp.concatenate([up_cols, down_rows[0], down_rows[1], out_rows], axis=1)
        joint = lax.all_gather(joint, ("head", "u", "v"), axis=0, tiled=True)
        w_up = joint[:, : 2 * f_half]
        w_down = [joint[:, 2 * f_half + i * width : 2 * f_half + (i + 1) * width] for i in range(2)]
        w_out = joint[:, 2 * f_half + 2 * width :]
    else:
        w_up, w_down_a, w_down_b, w_out = (
            lax.all_gather(w, ("head", "u", "v"), axis=0, tiled=True)
            for w in (up_cols, down_rows[0], down_rows[1], out_rows)
        )
        w_down = [w_down_a, w_down_b]

    sent = [tokens] + [shifted(tokens, "head", k) for k in range(1, n_head)]
    nearest, cols = lax.optimization_barrier((sent[1], cols))
    sent = [tokens, nearest] + sent[2:]
    cols = gather_axis(gather_axis(cols, "v"), "u")
    sent, cols = lax.optimization_barrier((sent, cols))
    cols = gather_axis(cols, "rest")
    cols = cols.transpose(3, 1, 2, 0, 4, 5).reshape(width, group + 128)
    w_in = cols[:, :group]
    vectors = cols[:, group : group + 8 + n_up].T.astype(f32)
    gain_a, shift_a, bias_q, bias_v, bias_out, gain_b, shift_b, bias_down = (vectors[i] for i in range(8))
    bias_up = vectors[8:].reshape(n_up, n_all, w_rows).transpose(1, 0, 2)

    rows_all = jnp.zeros((n_head, tok_rows, width), bf16)
    for k in range(n_head):
        rows_all = put(rows_all, sent[k], (me_head - k) % n_head)
    rows_all = rows_all.reshape(block_rows, width)

    rows_all = rows_all.astype(f32)
    normed, unit_all, inverse_all = norm_forward(rows_all, gain_a, shift_a)
    normed_low = normed.astype(bf16)
    group_bias = jnp.stack([bias_q, jnp.zeros_like(bias_q), bias_v]).reshape(3, n_head, hb, HEAD_DIM)
    group_bias = lax.dynamic_index_in_dim(group_bias, me_head, 1, keepdims=False).transpose(1, 0, 2).reshape(group, 1)
    projected = lax.dot_general(w_in, normed_low, (((0,), (1,)), ((), ())), preferred_element_type=f32)
    projected = (projected + group_bias).astype(bf16)
    qkv = lax.all_to_all(
        projected.reshape(hb, 3 * HEAD_DIM, block_rows), ("u", "v"), split_axis=0, concat_axis=0, tiled=True
    )
    far = [shifted(qkv, "rest", k) for k in range(1, n_rest)]
    far = jnp.stack(far) if n_rest > 2 else far[0][None]

    doc_start = jnp.zeros_like(segment)
    for doc in range(1, DOCS):
        first = jnp.sum((segment < doc).astype(jnp.int32))
        doc_start = jnp.where(segment == doc, first, doc_start)
    starts = lax.dynamic_index_in_dim(doc_start.reshape(hb, n_rest, block_rows), me_rest, 1, keepdims=False)

    def bounds(block_q):
        of_block = starts.reshape(-1, block_q)
        lo = of_block[:, 0] // BLOCK_K
        mid = (of_block[:, -1] + BLOCK_K - 1) // BLOCK_K
        q_first = (jnp.arange(hb, dtype=jnp.int32)[:, None] * n_rest + me_rest) * block_rows
        q_first = (q_first + jnp.arange(block_rows // block_q, dtype=jnp.int32)[None] * block_q).reshape(-1)
        return (lo, mid, q_first, me_rest.astype(jnp.int32).reshape(1))

    forward_bounds, backward_bounds = bounds(FORWARD_Q), bounds(BLOCK_Q)
    starts = starts.reshape(hb, 1, block_rows)

    attended, wide, lse = attention_forward(forward_bounds, qkv, far, starts, n_head, tok_rows)
    back = lax.all_to_all(
        attended.reshape(HEADS, HEAD_DIM, tok_rows), ("head", "u", "v"), split_axis=0, concat_axis=0, tiled=True
    ).reshape(width, tok_rows)

    rows = tokens.astype(f32)
    branch = lax.dot_general(back, w_out, (((0,), (0,)), ((), ())), preferred_element_type=f32) + bias_out
    middle = rows + branch
    hidden_in, unit_mid, inverse_mid = norm_forward(middle, gain_b, shift_b)
    hidden_low = hidden_in.astype(bf16)
    hidden_all = gather_axis(hidden_low, "rest").reshape(n_rest * tok_rows, width)
    cot_all = gather_axis(cotangent, "rest").reshape(n_rest * tok_rows, width)
    bias_units = lax.dynamic_index_in_dim(bias_up.reshape(chips, n_rest, 2, f_rows), me_rest, 1, keepdims=False)
    bias_units = bias_units.transpose(1, 0, 2).reshape(-1)
    pre = jnp.dot(hidden_all, w_up, preferred_element_type=f32) + bias_units
    act, slope = gelu_parts(pre)
    act_low = act.astype(bf16)
    acts = act_low[:, :f_half], act_low[:, f_half:]
    down = jnp.dot(acts[0], w_down[0], preferred_element_type=f32)
    down = down + jnp.dot(acts[1], w_down[1], preferred_element_type=f32)
    down = reduce_axis(down.reshape(n_rest, tok_rows, width), "rest")
    output = (middle + down + bias_down).astype(bf16)
    grad_out = cotangent.astype(f32)
    grad_act = jnp.concatenate(
        [jnp.einsum("td,fd->tf", cot_all, w, preferred_element_type=f32) for w in w_down], axis=1
    )
    grad_pre = (grad_act * slope).astype(bf16)
    grad_hidden = jnp.einsum("tf,df->td", grad_pre, w_up, preferred_element_type=f32)
    grad_hidden = reduce_axis(grad_hidden.reshape(n_rest, tok_rows, width), "rest")
    grad_middle = grad_out + norm_inner(grad_hidden, unit_mid, inverse_mid, gain_b)
    grad_branch = grad_middle.astype(bf16)
    grad_back = lax.dot_general(w_out, grad_branch, (((1,), (1,)), ((), ())), preferred_element_type=f32).astype(bf16)
    grad_heads = lax.all_to_all(
        grad_back.reshape(HEADS, HEAD_DIM, tok_rows), ("head", "u", "v"), split_axis=0, concat_axis=0, tiled=True
    ).reshape(n_head, hb, HEAD_DIM, tok_rows)

    down_grads = [jnp.einsum("tf,td->fd", a, cot_all, preferred_element_type=f32).astype(bf16) for a in acts]
    up_grad = jnp.einsum("td,tf->df", hidden_all, grad_pre, preferred_element_type=f32).astype(bf16)
    out_grad = jnp.einsum("dt,te->de", back, grad_branch, preferred_element_type=f32).astype(bf16)
    out_grad = out_grad.reshape(chips, n_rest, w_rows, width).transpose(1, 0, 2, 3)
    out_grad = reduce_axis(out_grad, "rest").astype(bf16)
    up_grad = up_grad.reshape(n_head, n_u, n_v, -1, 2 * f_half)
    out_grad = out_grad.reshape(n_head, n_u, n_v, -1, width)
    down_a, down_b = (x.reshape(n_head, n_u, n_v, f_rows, width) for x in down_grads)
    sums = [
        jnp.sum(grad_branch.astype(f32), axis=0),
        jnp.sum(grad_hidden * unit_mid, axis=0),
        jnp.sum(grad_hidden, axis=0),
        jnp.sum(grad_out, axis=0),
    ]
    unit_sum = jnp.sum(grad_pre.astype(f32), axis=0)
    unit_sum = unit_sum.reshape(2, chips, f_rows).transpose(1, 0, 2).reshape(chips, 1, 2 * f_rows)
    unit_sum = jnp.where((jnp.arange(n_rest) == me_rest)[:, None], unit_sum, 0.0).reshape(n_head, n_blk, n_up, w_rows)

    down_a = jnp.concatenate([down_a, out_grad], axis=3)
    grad_heads, up_grad, down_a, down_b = lax.optimization_barrier((grad_heads, up_grad, down_a, down_b))
    begun = [reduce_begin(up_grad, "u", 1), reduce_begin(down_a, "v", 2), reduce_begin(down_b, "head")]

    dq, dkv = attention_backward(backward_bounds, qkv, far, starts, grad_heads, wide, lse)
    dq, dkv, begun = lax.optimization_barrier((dq, dkv, begun))
    up_grad, down_a, down_b = (reduce_end(x).astype(bf16) for x in begun)
    down_begun = reduce_begin(down_a, "head")
    dkv = reduce_axis(dkv, "rest").astype(bf16)
    grad_proj = lax.all_to_all(
        jnp.concatenate([dq, dkv], axis=1), ("u", "v"), split_axis=0, concat_axis=0, tiled=True
    ).reshape(group, block_rows)

    grad_normed = lax.dot_general(grad_proj, w_in, (((0,), (1,)), ((), ())), preferred_element_type=f32)
    tokens_low = grad_normed.astype(bf16).reshape(n_head, tok_rows, width)
    tokens_low, grad_proj = lax.optimization_barrier((tokens_low, grad_proj))
    begun = reduce_begin(tokens_low, "head")

    in_grad = lax.dot_general(normed_low, grad_proj, (((0,), (1,)), ((), ())), preferred_element_type=f32)
    rowed = lambda x: x.reshape(n_head, n_blk, w_rows)
    gain_grad = rowed(jnp.sum(grad_normed * unit_all, axis=0))
    shift_grad = rowed(jnp.sum(grad_normed, axis=0))
    col_sum = jnp.sum(grad_proj.astype(f32), axis=1).reshape(hb, 3, HEAD_DIM)
    mine = (jnp.arange(n_head) == me_head)[:, None, None]
    query_sum = jnp.where(mine, col_sum[:, 0].reshape(1, n_blk, w_rows), 0.0)
    value_sum = jnp.where(mine, col_sum[:, 2].reshape(1, n_blk, w_rows), 0.0)
    extra = jnp.stack([gain_grad, shift_grad, query_sum, value_sum, *(rowed(x) for x in sums)], axis=2)
    extra = jnp.concatenate([extra, unit_sum], axis=2)
    n_extra = extra.shape[2]
    extra = jnp.pad(extra.transpose(0, 1, 3, 2), ((0, 0), (0, 0), (0, 0), (0, width - group - n_extra)))
    joined = jnp.concatenate([in_grad.reshape(n_head, n_blk, w_rows, group), extra], axis=-1).astype(bf16)
    joined = joined.reshape(n_head, n_u, n_v, n_rest, w_rows, width)
    early, begun = begun[:2], begun[2:]
    early, joined, up_grad, down_begun, down_b = lax.optimization_barrier(
        (early, joined, up_grad, down_begun, down_b)
    )
    joined = reduce_axis(joined, "rest", 3).astype(bf16)
    joined = reduce_axis(joined, "u", 1).astype(bf16)
    joined = reduce_axis(joined, "v", 1).astype(bf16)

    up_grad = reduce_axis(up_grad, "v", 1).astype(bf16)
    down_a = reduce_end(down_begun).astype(bf16)
    n_rows = down_a.shape[1]
    down_a = reduce_axis(jnp.concatenate([down_a, down_b.reshape(n_u, -1, width)], axis=1), "u")
    down_b = down_a[n_rows:].astype(bf16).reshape(n_v, f_rows, width)
    down_a = down_a[:n_rows]

    begun, joined, up_grad, down_b = lax.optimization_barrier((begun, joined, up_grad, down_b))
    down_b = reduce_axis(down_b, "v")
    up_grad = reduce_axis(up_grad, "head").astype(bf16).reshape(n_rest, w_rows, 2 * f_half)
    up_grad = exchange_axis(up_grad, "rest").astype(f32)
    out_weight_grad = down_a[f_rows:]
    down_weight_grad = jnp.concatenate([down_a[:f_rows], down_b], axis=0)
    joined = exchange_axis(joined, "head").astype(f32)
    up_weight_grad = up_grad.reshape(n_rest, w_rows, 2, chips, f_rows).transpose(1, 3, 0, 2, 4).reshape(w_rows, -1)
    in_weight_grad = joined[:, :, :group].reshape(n_head, w_rows, hb, 3, HEAD_DIM).transpose(1, 3, 0, 2, 4)
    in_weight_grad = in_weight_grad.reshape(w_rows, 3 * width)
    extra = jnp.sum(joined[:, :, group : group + n_extra], axis=0).T
    norm_gain_grad, norm_shift_grad, query_bias_grad, value_bias_grad = (extra[i] for i in range(4))
    out_bias_grad, post_gain_grad, post_shift_grad, down_bias_grad = (extra[i] for i in range(4, 8))
    up_bias_grad = extra[8:].reshape(-1)

    grad_tokens = reduce_end(early + begun)
    unit_in = lax.dynamic_index_in_dim(unit_all.reshape(n_head, tok_rows, width), me_head, 0, keepdims=False)
    inverse_in = lax.dynamic_index_in_dim(inverse_all.reshape(n_head, tok_rows, 1), me_head, 0, keepdims=False)
    tokens_grad = (grad_middle + norm_inner(grad_tokens, unit_in, inverse_in, gain_a)).astype(bf16)
    return (
        output,
        tokens_grad,
        norm_gain_grad,
        norm_shift_grad,
        in_weight_grad,
        query_bias_grad,
        value_bias_grad,
        out_weight_grad,
        out_bias_grad,
        post_gain_grad,
        post_shift_grad,
        up_weight_grad,
        up_bias_grad,
        down_weight_grad,
        down_bias_grad,
    )


def solution(mesh):
    n_head, n_blk = mesh.shape["head"], mesh.shape["blk"]
    hb = HEADS // n_head
    n_u = 2 if hb % 2 == 0 else 1
    fine = Mesh(mesh.devices.reshape(n_head, n_u, hb // n_u, n_blk // hb), ALL)
    tok = P(("u", "v", "rest", "head"), None)
    vec = P(ALL)
    mat = P(ALL, None)
    return jax.shard_map(
        on_device,
        mesh=fine,
        in_specs=(tok, tok, P(), vec, vec, mat, vec, vec, mat, vec, vec, vec, mat, vec, mat, vec),
        out_specs=(tok, tok, vec, vec, mat, vec, vec, mat, vec, vec, vec, mat, vec, mat, vec),
        check_vma=False,
    )
```
